512 devices in a mesh: index: 64 (over z, y), query: 8 (over x, core).
Axes of the slice: x: 4, y: 4, z: 16, core: 2. Of those that a mesh axis runs over, the one named last changes fastest.
Arguments:
- queries: bfloat16 [256, 32, 128], P('query'), may hold values from -6 to 6
- passages: bfloat16 [32768, 128, 128], P(('index', 'query')), may hold values from -0.5 to 0.5
- lengths: int32 [32768], P(('index', 'query')), may hold values from 1 to 128
- candidates: int32 [256, 1024], P('query', 'index'), may hold values from 0 to 32767, as said below
Outputs:
- scores: float32 [256, 1024], P('query', 'index')
The draws below stay inside these ranges and needn't reach their ends.
Inputs may be any that keep to these rules, and one draw needn't show every extreme that they name: Block b is stored on the device of flat position b // 64 along index+query. The 32 x 16 candidates held by one device name blocks of any one storing device at most 2 times, and exactly 2 times for some storing device.
All inputs are finite; a program needn't handle non-finite values.
Results may differ from the reference program's by a relative error of at most 0.0003.
Values may be sent and summed in bfloat16 or wider, within the bound.
No kernel may reach another device: no remote copies, remote signals or barrier semaphores. Data moves between devices by JAX's collectives and lax.ppermute only.
A program may use at most 64 MiB of HBM per device.

```python
import jax
import jax.numpy as jnp
from jax import lax

DIM = 128
QT = 32
PTOK = 128
BLK_DEV = 64
Q_DEV = 32
CAND_DEV = 16
CAP = 2
NQ = 256
CAND = 1024
BLOCKS = 32768


def draw_candidates(key, part):
    groups_q = NQ // Q_DEV
    groups_i = CAND // CAND_DEV
    owners = BLOCKS // BLK_DEV
    total_slots = owners * CAP
    request_count = Q_DEV * CAND_DEV

    def single(dev_key):
        key_first, key_order, key_mix, key_local = jax.random.split(dev_key, 4)
        first_owner = jax.random.randint(key_first, (), 0, owners)
        ranking = jax.random.permutation(key_order, total_slots).astype(jnp.int32)
        slot_owner = jnp.arange(total_slots, dtype=jnp.int32) // CAP
        ranking = ranking + total_slots * (slot_owner != first_owner).astype(jnp.int32)
        picked = jnp.argsort(ranking)[:request_count].astype(jnp.int32)
        picked = jax.random.permutation(key_mix, picked)
        local_block = jax.random.randint(key_local, (request_count,), 0, BLK_DEV)
        return picked // CAP * BLK_DEV + local_block
    dev_keys = jax.random.split(key, groups_q * groups_i)
    blocks_all = jax.vmap(single)(dev_keys).reshape(groups_q, groups_i, Q_DEV, CAND_DEV)
    return blocks_all.transpose(0, 2, 1, 3).reshape(NQ, CAND).astype(jnp.int32)


def with_ends(entries, own_key, smallest, top_value):
    index_at = [jax.random.randint(jax.random.fold_in(own_key, axis), (), 0, length) for axis, length in enumerate(entries.shape)]
    main_axis = entries.shape.index(max(entries.shape))
    next_to = index_at[:main_axis] + [(index_at[main_axis] + 1) % entries.shape[main_axis]] + index_at[main_axis + 1:]
    return entries.at[tuple(index_at)].set(smallest).at[tuple(next_to)].set(top_value)


def shard_levels(key, dims, pieces, smallest, top_value):
    level = 1.0
    for axis_at, parts in pieces:
        draws = jax.random.uniform(jax.random.fold_in(jax.random.fold_in(key, 6), axis_at), (parts,), jnp.float32, smallest / len(pieces), top_value / len(pieces))
        level = level * jnp.repeat(jnp.exp(draws), dims[axis_at] // parts).reshape((-1,) + (1,) * (len(dims) - 1 - axis_at))
    return level


def gaussian(key, extent, deviation, bound, cuts=(), held_as=jnp.bfloat16):
    level = shard_levels(key, extent, cuts, -0.22, 0.18) if cuts else 1.0
    drawn = jax.random.normal(key, extent, jnp.float32) * deviation * level
    return jnp.minimum(jnp.maximum(drawn, -bound), bound).astype(held_as)


def setup_inputs(seed: int = 0) -> dict:
    streams_of = jax.random.split(jax.random.key(seed), 5)
    queries = gaussian(streams_of[0], (NQ, QT, DIM), 1.0, 6.0, ((0, 8),))
    passages = gaussian(streams_of[1], (BLOCKS, PTOK, DIM), DIM ** -0.5, 0.5, ((0, 512),))
    lengths = with_ends(jax.random.randint(streams_of[2], (BLOCKS,), 1, PTOK + 1), jax.random.fold_in(streams_of[2], 1), 1, PTOK).astype(jnp.int32)
    candidates = draw_candidates(jax.random.fold_in(streams_of[4], 71), 0)
    return {"queries": queries, "passages": passages, "lengths": lengths, "candidates": candidates}


def reference(queries, passages, lengths, candidates):
    token_pos = jnp.arange(passages.shape[1]).astype(jnp.int32)

    def per_query(packed):
        query_rows, chosen = packed
        block_rows = passages[chosen].astype(jnp.float32)
        similar = jnp.einsum("td,cpd->ctp", query_rows.astype(jnp.float32), block_rows)
        live = token_pos[None, None, :] < lengths[chosen][:, None, None]
        best = jnp.max(jnp.where(live, similar, -jnp.inf), axis=2)
        return jnp.mean(best, axis=1)

    return lax.map(per_query, (queries, candidates))
```

```python
import jax
import jax.numpy as jnp
from jax import lax
from jax.experimental import pallas as pl
from jax.experimental.pallas import tpu as pltpu
from jax.sharding import PartitionSpec as P

Z, Y, Q = 16, 4, 8
YQ = Y * Q
OWNERS = Z * YQ
BLK = 64
QL, CL = 32, 16
NQ = Q * QL
T, D, PT = 32, 128, 128
GROUP = 8
GMAX = 192
UNROLL = 8
BIG = 1 << 30

Z_GROUPS = [[r + YQ * z for z in range(Z)] for r in range(YQ)]
YQ_GROUPS = [[YQ * z + r for r in range(YQ)] for z in range(Z)]


def iota(shape, axis):
    return lax.broadcasted_iota(jnp.int32, shape, axis)


def exchange(x, groups):
    return lax.all_to_all(
        x, ("index", "query"), split_axis=0, concat_axis=0, tiled=True,
        axis_index_groups=groups,
    )


def request_kernel(cand_ref, table_ref, first_ref):
    cand = cand_ref[...]
    lane_owner = iota((CL, OWNERS), 1)
    sub = iota((CL, 1), 0)
    low = jnp.full((CL, OWNERS), BIG, jnp.int32)
    high = jnp.full((CL, OWNERS), -1, jnp.int32)
    for q in range(QL):
        col = cand[:, q : q + 1]
        key = (q << 10) + (sub << 6) + (col & 63)
        match = (col >> 6) == lane_owner
        low = jnp.minimum(low, jnp.where(match, key, BIG))
        high = jnp.maximum(high, jnp.where(match, key, -1))
    first = jnp.min(low, axis=0, keepdims=True)
    last = jnp.max(high, axis=0, keepdims=True)
    first_ref[...] = first

    def code(key):
        return ((key >> 10) << 6) + (key & 63)

    slot0 = jnp.where(last >= 0, code(first), -1)
    slot1 = jnp.where((last >= 0) & (last != first), code(last), -1)
    row = iota((Z, 128), 0)
    lane = iota((Z, 128), 1)
    out = jnp.full((Z, 128), -1, jnp.int32)
    for k, slot in enumerate((slot0, slot1)):
        for j in range(4):
            shift = (32 * k - 32 * j) % 128
            for t in range(4):
                seg = jnp.broadcast_to(slot[:, 128 * t : 128 * (t + 1)], (Z, 128))
                seg = pltpu.roll(seg, shift, 1) if shift else seg
                out = jnp.where((row == 4 * t + j) & (lane >> 5 == k), seg, out)
    table_ref[...] = out


def turn_kernel(x_ref, o_ref):
    x = jnp.concatenate([x_ref[...], jnp.zeros((112, 128), jnp.int32)], axis=0)
    xt = jnp.transpose(x)
    lane = iota((YQ, 128), 1)
    o_ref[...] = jnp.where(lane < Z, xt[:YQ], pltpu.roll(xt[YQ : 2 * YQ], Z, 1))


def back_kernel(x_ref, o_ref):
    x = jnp.concatenate([x_ref[...], jnp.zeros((96, 128), jnp.float32)], axis=0)
    xt = jnp.transpose(x)
    lane = iota((Z, 128), 1)
    o_ref[...] = jnp.where(lane < YQ, xt[:Z], pltpu.roll(xt[Z : 2 * Z], YQ, 1))


def split3(x):
    hi = x.astype(jnp.bfloat16)
    rest = x - hi.astype(jnp.float32)
    mid = rest.astype(jnp.bfloat16)
    low = (rest - mid.astype(jnp.float32)).astype(jnp.bfloat16)
    return hi, mid, low


def dot(a, b, dims):
    return lax.dot_general(a, b, (dims, ((), ())), preferred_element_type=jnp.float32)


def score_kernel(len_ref, code_ref, q_ref, p_ref, o_ref, plan, plan_s, onehot, best, sem):
    code = jnp.full((Q, 128), -1, jnp.int32)
    lane8 = iota((Q, 128), 1)
    for y in range(Y):
        part = code_ref[Q * y : Q * (y + 1), :]
        part = pltpu.roll(part, 32 * y, 1) if y else part
        code = jnp.where(lane8 >> 5 == y, part, code)
    valid = code >= 0
    block = jnp.where(valid, code & 63, BLK)
    query = jnp.where(valid, (code >> 6) + QL * iota((Q, 128), 0), 0)

    b_iota = iota((BLK, 128), 0)
    hits = [block[q : q + 1, :] == b_iota for q in range(Q)]
    hit = jnp.concatenate([h.astype(jnp.float32) for h in hits], axis=0).astype(jnp.bfloat16)
    r_i, c_i = iota((128, 128), 0), iota((128, 128), 1)
    earlier = jnp.concatenate(
        [(r_i < c_i).astype(jnp.float32), jnp.ones((128, 128), jnp.float32)], axis=1
    ).astype(jnp.bfloat16)
    sums = dot(hit, earlier, ((1,), (0,)))
    base = jnp.zeros((BLK, 128), jnp.float32)
    bases = []
    for q in range(Q):
        bases.append(base + sums[BLK * q : BLK * (q + 1), :128])
        base = base + sums[BLK * q : BLK * (q + 1), 128:]
    groups = ((base.astype(jnp.int32) + (GROUP - 1)) >> 3).astype(jnp.float32)
    l_i, m_i = iota((BLK, BLK), 0), iota((BLK, BLK), 1)
    before = dot(
        (m_i < l_i).astype(jnp.float32).astype(jnp.bfloat16),
        groups.astype(jnp.bfloat16),
        ((1,), (0,)),
    )
    ends = (before + groups).astype(jnp.int32)
    dest = jnp.concatenate(
        [
            jnp.sum(jnp.where(hits[q], GROUP * before + bases[q], 0.0), axis=0, keepdims=True)
            for q in range(Q)
        ],
        axis=0,
    ).astype(jnp.int32)

    g_iota = iota((GMAX, 128), 0)
    c_iota = iota((GROUP, 128), 0)
    named = []
    for q in range(Q):
        d = dest[q : q + 1, :]
        onehot[:, 128 * q : 128 * (q + 1)] = (
            ((d >> 3) == g_iota).astype(jnp.float32).astype(jnp.bfloat16)
        )
        here = ((d & 7) == c_iota) & valid[q : q + 1, :]
        named.append(jnp.where(here, query[q : q + 1, :], 0).astype(jnp.float32))
    lists = dot(
        jnp.concatenate(named, axis=1).astype(jnp.bfloat16), onehot[...], ((1,), (1,))
    )
    plan[0:GROUP, 0:GMAX] = lists.astype(jnp.int32)
    g_lane = iota((BLK, 256), 1)
    ends2 = jnp.concatenate([ends, ends], axis=1)
    owner_block = jnp.minimum(
        jnp.sum((ends2 <= g_lane).astype(jnp.int32), axis=0, keepdims=True), BLK - 1
    )
    total = jnp.broadcast_to(ends2[BLK - 1 : BLK, :], (1, 256))
    plan[GROUP : 2 * GROUP, :] = jnp.where(
        iota((GROUP, 256), 0) == 0,
        jnp.broadcast_to(owner_block, (GROUP, 256)),
        jnp.broadcast_to(total, (GROUP, 256)),
    )
    copy = pltpu.make_async_copy(plan, plan_s, sem)
    copy.start()
    best[...] = jnp.zeros((GMAX, GROUP * T), jnp.float32)
    copy.wait()

    token = iota((PT, GROUP * T), 0)

    def step(it, carry):
        rows = []
        for u in range(UNROLL):
            g = it * UNROLL + u
            b = plan_s[GROUP, g]
            rows_q = jnp.concatenate([q_ref[plan_s[c, g]] for c in range(GROUP)], axis=0)
            similar = dot(p_ref[b], rows_q, ((1,), (1,)))
            similar = jnp.where(token < len_ref[b], similar, -jnp.inf)
            rows.append(jnp.max(similar, axis=0, keepdims=True))
        best[pl.ds(pl.multiple_of(it * UNROLL, UNROLL), UNROLL), :] = jnp.concatenate(rows, axis=0)
        return carry

    lax.fori_loop(0, (plan_s[GROUP + 1, 0] + (UNROLL - 1)) // UNROLL, step, 0)

    w = (iota((GROUP, GROUP * T), 0) == (iota((GROUP, GROUP * T), 1) >> 5)).astype(jnp.float32)
    w = w.astype(jnp.bfloat16)
    means = sum(dot(w, part, ((1,), (1,))) for part in split3(best[...])) * (1.0 / T)
    picked = dot(jnp.concatenate(split3(means), axis=0), onehot[...], ((1,), (0,)))
    picked = picked[0:GROUP] + picked[GROUP : 2 * GROUP] + picked[2 * GROUP : 3 * GROUP]
    out = []
    for q in range(Q):
        here = (dest[q : q + 1, :] & 7) == c_iota
        out.append(
            jnp.sum(jnp.where(here, picked[:, 128 * q : 128 * (q + 1)], 0.0), axis=0, keepdims=True)
        )
    out = jnp.concatenate(out, axis=0)
    for y in range(Y):
        shift = (128 - 32 * y) % 128
        o_ref[Q * y : Q * (y + 1), :] = pltpu.roll(out, shift, 1) if shift else out


def place_kernel(cand_ref, first_ref, x_ref, o_ref):
    cand = cand_ref[...]
    x = x_ref[...]
    lane = iota((1, 128), 1)
    values = []
    for k in range(2):
        segs = []
        for t in range(4):
            seg = jnp.zeros((1, 128), jnp.float32)
            for j in range(4):
                row = x[4 * t + j : 4 * t + j + 1, :]
                shift = (32 * j - 32 * k) % 128
                row = pltpu.roll(row, shift, 1) if shift else row
                seg = jnp.where(lane >> 5 == j, row, seg)
            segs.append(seg)
        values.append(jnp.concatenate(segs, axis=1))
    lane_owner = iota((CL, OWNERS), 1)
    sub = iota((CL, 1), 0)
    first = jnp.broadcast_to(first_ref[...], (CL, OWNERS))
    value0 = jnp.broadcast_to(values[0], (CL, OWNERS))
    value1 = jnp.broadcast_to(values[1], (CL, OWNERS))
    out_lane = iota((CL, QL), 1)
    out = jnp.zeros((CL, QL), jnp.float32)
    for q in range(QL):
        col = cand[:, q : q + 1]
        key = (q << 10) + (sub << 6) + (col & 63)
        value = jnp.where(first == key, value0, value1)
        hit = jnp.where((col >> 6) == lane_owner, value, 0.0)
        out = jnp.where(out_lane == q, jnp.sum(hit, axis=1, keepdims=True), out)
    o_ref[...] = out


def small_call(kernel, out_shape, *args):
    return pl.pallas_call(kernel, out_shape=out_shape)(*args)


def shards(queries, passages, lengths, candidates):
    every = lax.all_to_all(
        jnp.broadcast_to(queries[None], (Q,) + queries.shape),
        "query", split_axis=0, concat_axis=0, tiled=True,
    ).reshape(NQ, T, D)
    cand = candidates.T
    table, first = small_call(
        request_kernel,
        (
            jax.ShapeDtypeStruct((Z, 128), jnp.int32),
            jax.ShapeDtypeStruct((1, OWNERS), jnp.int32),
        ),
        cand,
    )
    got = exchange(table, Z_GROUPS)
    got = small_call(turn_kernel, jax.ShapeDtypeStruct((YQ, 128), jnp.int32), got)
    codes = exchange(got, YQ_GROUPS)
    vmem = pl.BlockSpec(memory_space=pltpu.VMEM)
    scores = pl.pallas_call(
        score_kernel,
        out_shape=jax.ShapeDtypeStruct((YQ, 128), jnp.float32),
        in_specs=[pl.BlockSpec(memory_space=pltpu.SMEM), vmem, vmem, vmem],
        out_specs=vmem,
        scratch_shapes=[
            pltpu.VMEM((2 * GROUP, 256), jnp.int32),
            pltpu.SMEM((2 * GROUP, 256), jnp.int32),
            pltpu.VMEM((GMAX, Q * 128), jnp.bfloat16),
            pltpu.VMEM((GMAX, GROUP * T), jnp.float32),
            pltpu.SemaphoreType.DMA,
        ],
        compiler_params=pltpu.CompilerParams(vmem_limit_bytes=32 << 20),
    )(lengths, codes, every, passages)
    back = exchange(scores, YQ_GROUPS)
    back = small_call(back_kernel, jax.ShapeDtypeStruct((Z, 128), jnp.float32), back)
    back = exchange(back, Z_GROUPS)
    out = small_call(
        place_kernel, jax.ShapeDtypeStruct((CL, QL), jnp.float32), cand, first, back
    )
    return out.T


def solution(mesh):
    in_specs = (
        P("query", None, None),
        P(("index", "query"), None, None),
        P(("index", "query")),
        P("query", "index"),
    )
    return jax.shard_map(
        shards, mesh=mesh, in_specs=in_specs, out_specs=P("query", "index"), check_vma=False
    )
```

```python
import jax
import jax.numpy as jnp
from jax import lax
from jax.experimental import pallas as pl
from jax.experimental.pallas import tpu as pltpu
from jax.sharding import PartitionSpec as P

Z, Y, Q = 16, 4, 8
YQ = Y * Q
OWNERS = Z * YQ
BLK = 64
QL, CL = 32, 16
NQ = Q * QL
T, D, PT = 32, 128, 128
GROUP = 8
GMAX = 192
UNROLL = 8
BIG = 1 << 30

Z_GROUPS = [[r + YQ * z for z in range(Z)] for r in range(YQ)]
YQ_GROUPS = [[YQ * z + r for r in range(YQ)] for z in range(Z)]


def iota(shape, axis):
    return lax.broadcasted_iota(jnp.int32, shape, axis)


def exchange(x, groups):
    return lax.all_to_all(
        x, ("index", "query"), split_axis=0, concat_axis=0, tiled=True,
        axis_index_groups=groups,
    )


def request_kernel(cand_ref, table_ref, first_ref):
    cand = cand_ref[...]
    lane_owner = iota((CL, OWNERS), 1)
    sub = iota((CL, 1), 0)
    low = jnp.full((CL, OWNERS), BIG, jnp.int32)
    high = jnp.full((CL, OWNERS), -1, jnp.int32)
    for q in range(QL):
        col = cand[:, q : q + 1]
        key = (q << 10) + (sub << 6) + (col & 63)
        match = (col >> 6) == lane_owner
        low = jnp.minimum(low, jnp.where(match, key, BIG))
        high = jnp.maximum(high, jnp.where(match, key, -1))
    first = jnp.min(low, axis=0, keepdims=True)
    last = jnp.max(high, axis=0, keepdims=True)
    first_ref[...] = first

    def code(key):
        return ((key >> 10) << 6) + (key & 63)

    slot0 = jnp.where(last >= 0, code(first), -1)
    slot1 = jnp.where((last >= 0) & (last != first), code(last), -1)
    row = iota((Z, 128), 0)
    lane = iota((Z, 128), 1)
    out = jnp.full((Z, 128), -1, jnp.int32)
    for k, slot in enumerate((slot0, slot1)):
        for j in range(4):
            shift = (32 * k - 32 * j) % 128
            for t in range(4):
                seg = jnp.broadcast_to(slot[:, 128 * t : 128 * (t + 1)], (Z, 128))
                seg = pltpu.roll(seg, shift, 1) if shift else seg
                out = jnp.where((row == 4 * t + j) & (lane >> 5 == k), seg, out)
    table_ref[...] = out


def turn_kernel(x_ref, o_ref):
    x = jnp.concatenate([x_ref[...], jnp.zeros((112, 128), jnp.int32)], axis=0)
    xt = jnp.transpose(x)
    lane = iota((YQ, 128), 1)
    o_ref[...] = jnp.where(lane < Z, xt[:YQ], pltpu.roll(xt[YQ : 2 * YQ], Z, 1))


def back_kernel(x_ref, o_ref):
    x = jnp.concatenate([x_ref[...], jnp.zeros((96, 128), jnp.float32)], axis=0)
    xt = jnp.transpose(x)
    lane = iota((Z, 128), 1)
    o_ref[...] = jnp.where(lane < YQ, xt[:Z], pltpu.roll(xt[Z : 2 * Z], YQ, 1))


def split3(x):
    hi = x.astype(jnp.bfloat16)
    rest = x - hi.astype(jnp.float32)
    mid = rest.astype(jnp.bfloat16)
    low = (rest - mid.astype(jnp.float32)).astype(jnp.bfloat16)
    return hi, mid, low


def dot(a, b, dims):
    return lax.dot_general(a, b, (dims, ((), ())), preferred_element_type=jnp.float32)


def score_kernel(len_ref, code_ref, q_ref, p_ref, o_ref, plan, plan_s, onehot, best, sem):
    code = jnp.full((Q, 128), -1, jnp.int32)
    lane8 = iota((Q, 128), 1)
    for y in range(Y):
        part = code_ref[Q * y : Q * (y + 1), :]
        part = pltpu.roll(part, 32 * y, 1) if y else part
        code = jnp.where(lane8 >> 5 == y, part, code)
    valid = code >= 0
    block = jnp.where(valid, code & 63, BLK)
    query = jnp.where(valid, (code >> 6) + QL * iota((Q, 128), 0), 0)

    b_iota = iota((BLK, 128), 0)
    hits = [block[q : q + 1, :] == b_iota for q in range(Q)]
    hit = jnp.concatenate([h.astype(jnp.float32) for h in hits], axis=0).astype(jnp.bfloat16)
    r_i, c_i = iota((128, 128), 0), iota((128, 128), 1)
    earlier = jnp.concatenate(
        [(r_i < c_i).astype(jnp.float32), jnp.ones((128, 128), jnp.float32)], axis=1
    ).astype(jnp.bfloat16)
    sums = dot(hit, earlier, ((1,), (0,)))
    base = jnp.zeros((BLK, 128), jnp.float32)
    bases = []
    for q in range(Q):
        bases.append(base + sums[BLK * q : BLK * (q + 1), :128])
        base = base + sums[BLK * q : BLK * (q + 1), 128:]
    groups = ((base.astype(jnp.int32) + (GROUP - 1)) >> 3).astype(jnp.float32)
    l_i, m_i = iota((BLK, BLK), 0), iota((BLK, BLK), 1)
    before = dot(
        (m_i < l_i).astype(jnp.float32).astype(jnp.bfloat16),
        groups.astype(jnp.bfloat16),
        ((1,), (0,)),
    )
    ends = (before + groups).astype(jnp.int32)
    dest = jnp.concatenate(
        [
            jnp.sum(jnp.where(hits[q], GROUP * before + bases[q], 0.0), axis=0, keepdims=True)
            for q in range(Q)
        ],
        axis=0,
    ).astype(jnp.int32)

    g_iota = iota((GMAX, 128), 0)
    c_iota = iota((GROUP, 128), 0)
    named = []
    for q in range(Q):
        d = dest[q : q + 1, :]
        onehot[:, 128 * q : 128 * (q + 1)] = (
            ((d >> 3) == g_iota).astype(jnp.float32).astype(jnp.bfloat16)
        )
        here = ((d & 7) == c_iota) & valid[q : q + 1, :]
        named.append(jnp.where(here, query[q : q + 1, :], 0).astype(jnp.float32))
    lists = dot(
        jnp.concatenate(named, axis=1).astype(jnp.bfloat16), onehot[...], ((1,), (1,))
    )
    plan[0:GROUP, 0:GMAX] = lists.astype(jnp.int32)
    g_lane = iota((BLK, 256), 1)
    ends2 = jnp.concatenate([ends, ends], axis=1)
    owner_block = jnp.minimum(
        jnp.sum((ends2 <= g_lane).astype(jnp.int32), axis=0, keepdims=True), BLK - 1
    )
    total = jnp.broadcast_to(ends2[BLK - 1 : BLK, :], (1, 256))
    plan[GROUP : 2 * GROUP, :] = jnp.where(
        iota((GROUP, 256), 0) == 0,
        jnp.broadcast_to(owner_block, (GROUP, 256)),
        jnp.broadcast_to(total, (GROUP, 256)),
    )
    copy = pltpu.make_async_copy(plan, plan_s, sem)
    copy.start()
    best[...] = jnp.zeros((GMAX, GROUP * T), jnp.float32)
    copy.wait()

    token = iota((PT, GROUP * T), 0)

    def step(it, carry):
        rows = []
        for u in range(UNROLL):
            g = it * UNROLL + u
            b = plan_s[GROUP, g]
            rows_q = jnp.concatenate([q_ref[plan_s[c, g]] for c in range(GROUP)], axis=0)
            similar = dot(p_ref[b], rows_q, ((1,), (1,)))
            similar = jnp.where(token < len_ref[b], similar, -jnp.inf)
            rows.append(jnp.max(similar, axis=0, keepdims=True))
        best[pl.ds(pl.multiple_of(it * UNROLL, UNROLL), UNROLL), :] = jnp.concatenate(rows, axis=0)
        return carry

    lax.fori_loop(0, (plan_s[GROUP + 1, 0] + (UNROLL - 1)) // UNROLL, step, 0)

    w = (iota((GROUP, GROUP * T), 0) == (iota((GROUP, GROUP * T), 1) >> 5)).astype(jnp.float32)
    w = w.astype(jnp.bfloat16)
    means = sum(dot(w, part, ((1,), (1,))) for part in split3(best[...])) * (1.0 / T)
    picked = dot(jnp.concatenate(split3(means), axis=0), onehot[...], ((1,), (0,)))
    picked = picked[0:GROUP] + picked[GROUP : 2 * GROUP] + picked[2 * GROUP : 3 * GROUP]
    out = []
    for q in range(Q):
        here = (dest[q : q + 1, :] & 7) == c_iota
        out.append(
            jnp.sum(jnp.where(here, picked[:, 128 * q : 128 * (q + 1)], 0.0), axis=0, keepdims=True)
        )
    out = jnp.concatenate(out, axis=0)
    for y in range(Y):
        shift = (128 - 32 * y) % 128
        o_ref[Q * y : Q * (y + 1), :] = pltpu.roll(out, shift, 1) if shift else out


def place_kernel(cand_ref, first_ref, x_ref, o_ref):
    cand = cand_ref[...]
    x = x_ref[...]
    lane = iota((1, 128), 1)
    values = []
    for k in range(2):
        segs = []
        for t in range(4):
            seg = jnp.zeros((1, 128), jnp.float32)
            for j in range(4):
                row = x[4 * t + j : 4 * t + j + 1, :]
                shift = (32 * j - 32 * k) % 128
                row = pltpu.roll(row, shift, 1) if shift else row
                seg = jnp.where(lane >> 5 == j, row, seg)
            segs.append(seg)
        values.append(jnp.concatenate(segs, axis=1))
    lane_owner = iota((CL, OWNERS), 1)
    sub = iota((CL, 1), 0)
    first = jnp.broadcast_to(first_ref[...], (CL, OWNERS))
    value0 = jnp.broadcast_to(values[0], (CL, OWNERS))
    value1 = jnp.broadcast_to(values[1], (CL, OWNERS))
    out_lane = iota((CL, QL), 1)
    out = jnp.zeros((CL, QL), jnp.float32)
    for q in range(QL):
        col = cand[:, q : q + 1]
        key = (q << 10) + (sub << 6) + (col & 63)
        value = jnp.where(first == key, value0, value1)
        hit = jnp.where((col >> 6) == lane_owner, value, 0.0)
        out = jnp.where(out_lane == q, jnp.sum(hit, axis=1, keepdims=True), out)
    o_ref[...] = out


def small_call(kernel, out_shape, *args):
    return pl.pallas_call(kernel, out_shape=out_shape)(*args)


def shards(queries, passages, lengths, candidates):
    every = lax.all_gather(queries, "query", axis=0, tiled=True)
    cand = candidates.T
    table, first = small_call(
        request_kernel,
        (
            jax.ShapeDtypeStruct((Z, 128), jnp.int32),
            jax.ShapeDtypeStruct((1, OWNERS), jnp.int32),
        ),
        cand,
    )
    got = exchange(table, Z_GROUPS)
    got = small_call(turn_kernel, jax.ShapeDtypeStruct((YQ, 128), jnp.int32), got)
    codes = exchange(got, YQ_GROUPS)
    vmem = pl.BlockSpec(memory_space=pltpu.VMEM)
    scores = pl.pallas_call(
        score_kernel,
        out_shape=jax.ShapeDtypeStruct((YQ, 128), jnp.float32),
        in_specs=[pl.BlockSpec(memory_space=pltpu.SMEM), vmem, vmem, vmem],
        out_specs=vmem,
        scratch_shapes=[
            pltpu.VMEM((2 * GROUP, 256), jnp.int32),
            pltpu.SMEM((2 * GROUP, 256), jnp.int32),
            pltpu.VMEM((GMAX, Q * 128), jnp.bfloat16),
            pltpu.VMEM((GMAX, GROUP * T), jnp.float32),
            pltpu.SemaphoreType.DMA,
        ],
        compiler_params=pltpu.CompilerParams(vmem_limit_bytes=32 << 20),
    )(lengths, codes, every, passages)
    back = exchange(scores, YQ_GROUPS)
    back = small_call(back_kernel, jax.ShapeDtypeStruct((Z, 128), jnp.float32), back)
    back = exchange(back, Z_GROUPS)
    out = small_call(
        place_kernel, jax.ShapeDtypeStruct((CL, QL), jnp.float32), cand, first, back
    )
    return out.T


def solution(mesh):
    in_specs = (
        P("query", None, None),
        P(("index", "query"), None, None),
        P(("index", "query")),
        P("query", "index"),
    )
    return jax.shard_map(
        shards, mesh=mesh, in_specs=in_specs, out_specs=P("query", "index"), check_vma=False
    )
```

```python
import jax
import jax.numpy as jnp
from jax import lax
from jax.experimental import pallas as pl
from jax.experimental.pallas import tpu as pltpu
from jax.sharding import PartitionSpec as P

Z, Y, Q = 16, 4, 8
YQ = Y * Q
OWNERS = Z * YQ
BLK = 64
QL, CL = 32, 16
NQ = Q * QL
T, D, PT = 32, 128, 128
GROUP = 8
GMAX = 192
UNROLL = 8
BIG = 1 << 30

Z_GROUPS = [[r + YQ * z for z in range(Z)] for r in range(YQ)]
YQ_GROUPS = [[YQ * z + r for r in range(YQ)] for z in range(Z)]


def iota(shape, axis):
    return lax.broadcasted_iota(jnp.int32, shape, axis)


def exchange(x, groups):
    return lax.all_to_all(
        x, ("index", "query"), split_axis=0, concat_axis=0, tiled=True,
        axis_index_groups=groups,
    )


def spread(rows, row, lane):
    out = jnp.zeros((Z, 128), jnp.int32)
    for k, slot in enumerate(rows):
        for j in range(4):
            shift = (32 * k - 32 * j) % 128
            for t in range(4):
                seg = jnp.broadcast_to(slot[:, 128 * t : 128 * (t + 1)], (Z, 128))
                seg = pltpu.roll(seg, shift, 1) if shift else seg
                out = jnp.where((row == 4 * t + j) & (lane >> 5 == k), seg, out)
    return out


def request_kernel(cand_ref, code_ref, key_ref):
    cand = cand_ref[...]
    lane_owner = iota((CL, OWNERS), 1)
    sub = iota((CL, 1), 0)
    low = jnp.full((CL, OWNERS), BIG, jnp.int32)
    high = jnp.full((CL, OWNERS), -1, jnp.int32)
    for q in range(QL):
        col = cand[:, q : q + 1]
        key = (q << 10) + (sub << 6) + (col & 63)
        match = (col >> 6) == lane_owner
        low = jnp.minimum(low, jnp.where(match, key, BIG))
        high = jnp.maximum(high, jnp.where(match, key, -1))
    last = jnp.max(high, axis=0, keepdims=True)
    first = jnp.where(last >= 0, jnp.min(low, axis=0, keepdims=True), -1)
    last = jnp.where(last != first, last, -1)
    row = iota((Z, 128), 0)
    lane = iota((Z, 128), 1)
    key = spread((first, last), row, lane)
    key_ref[...] = key
    code_ref[...] = jnp.where(
        (key >= 0) & (lane < 2 * YQ), ((key >> 10) << 6) + (key & 63), -1
    )


def turn_kernel(x_ref, o_ref):
    x = jnp.concatenate([x_ref[...], jnp.zeros((112, 128), jnp.int32)], axis=0)
    xt = jnp.transpose(x)
    lane = iota((YQ, 128), 1)
    o_ref[...] = jnp.where(lane < Z, xt[:YQ], pltpu.roll(xt[YQ : 2 * YQ], Z, 1))


def back_kernel(x_ref, o_ref):
    x = jnp.concatenate([x_ref[...], jnp.zeros((96, 128), jnp.float32)], axis=0)
    xt = jnp.transpose(x)
    lane = iota((Z, 128), 1)
    o_ref[...] = jnp.where(lane < YQ, xt[:Z], pltpu.roll(xt[Z : 2 * Z], YQ, 1))


def split3(x):
    hi = x.astype(jnp.bfloat16)
    rest = x - hi.astype(jnp.float32)
    mid = rest.astype(jnp.bfloat16)
    low = (rest - mid.astype(jnp.float32)).astype(jnp.bfloat16)
    return hi, mid, low


def dot(a, b, dims):
    return lax.dot_general(a, b, (dims, ((), ())), preferred_element_type=jnp.float32)


def score_kernel(
    len_hbm, code_ref, q_hbm, p_hbm, o_ref,
    len_ref, q_ref, p_ref, plan, plan_s, onehot, best, sem, len_sem, q_sem, p_sem,
):
    len_copy = pltpu.make_async_copy(len_hbm, len_ref, len_sem)
    len_copy.start()
    p_copy = pltpu.make_async_copy(p_hbm, p_ref, p_sem)
    p_copy.start()
    q_copy = pltpu.make_async_copy(q_hbm, q_ref, q_sem)
    q_copy.start()
    code = jnp.full((Q, 128), -1, jnp.int32)
    lane8 = iota((Q, 128), 1)
    for y in range(Y):
        part = code_ref[Q * y : Q * (y + 1), :]
        part = pltpu.roll(part, 32 * y, 1) if y else part
        code = jnp.where(lane8 >> 5 == y, part, code)
    valid = code >= 0
    block = jnp.where(valid, code & 63, BLK)
    query = jnp.where(valid, (code >> 6) + QL * iota((Q, 128), 0), 0)

    b_iota = iota((BLK, 128), 0)
    hits = [block[q : q + 1, :] == b_iota for q in range(Q)]
    hit = jnp.concatenate([h.astype(jnp.float32) for h in hits], axis=0).astype(jnp.bfloat16)
    r_i, c_i = iota((128, 128), 0), iota((128, 128), 1)
    earlier = jnp.concatenate(
        [(r_i < c_i).astype(jnp.float32), jnp.ones((128, 128), jnp.float32)], axis=1
    ).astype(jnp.bfloat16)
    sums = dot(hit, earlier, ((1,), (0,)))
    base = jnp.zeros((BLK, 128), jnp.float32)
    bases = []
    for q in range(Q):
        bases.append(base + sums[BLK * q : BLK * (q + 1), :128])
        base = base + sums[BLK * q : BLK * (q + 1), 128:]
    groups = ((base.astype(jnp.int32) + (GROUP - 1)) >> 3).astype(jnp.float32)
    l_i, m_i = iota((BLK, BLK), 0), iota((BLK, BLK), 1)
    before = dot(
        (m_i < l_i).astype(jnp.float32).astype(jnp.bfloat16),
        groups.astype(jnp.bfloat16),
        ((1,), (0,)),
    )
    ends = (before + groups).astype(jnp.int32)
    dest = jnp.concatenate(
        [
            jnp.sum(jnp.where(hits[q], GROUP * before + bases[q], 0.0), axis=0, keepdims=True)
            for q in range(Q)
        ],
        axis=0,
    ).astype(jnp.int32)

    g_iota = iota((GMAX, 128), 0)
    c_iota = iota((GROUP, 128), 0)
    named = []
    for q in range(Q):
        d = dest[q : q + 1, :]
        onehot[:, 128 * q : 128 * (q + 1)] = (
            ((d >> 3) == g_iota).astype(jnp.float32).astype(jnp.bfloat16)
        )
        here = ((d & 7) == c_iota) & valid[q : q + 1, :]
        named.append(jnp.where(here, query[q : q + 1, :], 0).astype(jnp.float32))
    lists = dot(
        jnp.concatenate(named, axis=1).astype(jnp.bfloat16), onehot[...], ((1,), (1,))
    )
    plan[0:GROUP, 0:GMAX] = lists.astype(jnp.int32)
    g_lane = iota((BLK, 256), 1)
    ends2 = jnp.concatenate([ends, ends], axis=1)
    owner_block = jnp.minimum(
        jnp.sum((ends2 <= g_lane).astype(jnp.int32), axis=0, keepdims=True), BLK - 1
    )
    total = jnp.broadcast_to(ends2[BLK - 1 : BLK, :], (1, 256))
    plan[GROUP : 2 * GROUP, :] = jnp.where(
        iota((GROUP, 256), 0) == 0,
        jnp.broadcast_to(owner_block, (GROUP, 256)),
        jnp.broadcast_to(total, (GROUP, 256)),
    )
    copy = pltpu.make_async_copy(plan, plan_s, sem)
    copy.start()
    best[...] = jnp.zeros((GMAX, GROUP * T), jnp.float32)
    copy.wait()
    len_copy.wait()
    p_copy.wait()
    q_copy.wait()

    token = iota((PT, GROUP * T), 0)

    def step(it, carry):
        rows = []
        for u in range(UNROLL):
            g = it * UNROLL + u
            b = plan_s[GROUP, g]
            rows_q = jnp.concatenate([q_ref[plan_s[c, g]] for c in range(GROUP)], axis=0)
            similar = dot(p_ref[b], rows_q, ((1,), (1,)))
            similar = jnp.where(token < len_ref[b], similar, -jnp.inf)
            rows.append(jnp.max(similar, axis=0, keepdims=True))
        best[pl.ds(pl.multiple_of(it * UNROLL, UNROLL), UNROLL), :] = jnp.concatenate(rows, axis=0)
        return carry

    lax.fori_loop(0, (plan_s[GROUP + 1, 0] + (UNROLL - 1)) // UNROLL, step, 0)

    w = (iota((GROUP, GROUP * T), 0) == (iota((GROUP, GROUP * T), 1) >> 5)).astype(jnp.float32)
    w = w.astype(jnp.bfloat16)
    means = sum(dot(w, part, ((1,), (1,))) for part in split3(best[...])) * (1.0 / T)
    picked = dot(jnp.concatenate(split3(means), axis=0), onehot[...], ((1,), (0,)))
    picked = picked[0:GROUP] + picked[GROUP : 2 * GROUP] + picked[2 * GROUP : 3 * GROUP]
    out = []
    for q in range(Q):
        here = (dest[q : q + 1, :] & 7) == c_iota
        out.append(
            jnp.sum(jnp.where(here, picked[:, 128 * q : 128 * (q + 1)], 0.0), axis=0, keepdims=True)
        )
    out = jnp.concatenate(out, axis=0)
    for y in range(Y):
        shift = (128 - 32 * y) % 128
        o_ref[Q * y : Q * (y + 1), :] = pltpu.roll(out, shift, 1) if shift else out


def place_kernel(cand_ref, key_ref, x_ref, o_ref):
    cand = jnp.concatenate([cand_ref[...], jnp.zeros((CL, 128 - QL), jnp.int32)], axis=1)
    lane = iota((1, 128), 1)
    turned = [cand] + [pltpu.roll(cand, 32 * i, 1) for i in range(1, 4)]
    segs = []
    for t in range(4):
        seg = turned[0][4 * t : 4 * t + 1, :]
        for i in range(1, 4):
            seg = jnp.where(lane >> 5 == i, turned[i][4 * t + i : 4 * t + i + 1, :], seg)
        segs.append(seg)
    asked = jnp.concatenate(segs, axis=1)
    place = iota((1, QL * CL), 1)
    own_key = ((place & 31) << 10) + ((place >> 5) << 6) + (asked & 63)
    owner = asked >> 6
    lane_z = iota((Z, 128), 1)
    x = jnp.where(lane_z < 2 * YQ, x_ref[...], 0.0)
    key = jnp.where(lane_z < YQ, key_ref[...], 0)
    key_high = pltpu.roll(key >> 8, 2 * YQ, 1).astype(jnp.float32)
    key_low = pltpu.roll(key & 255, 3 * YQ, 1).astype(jnp.float32)
    high, mid, low = split3(x)
    high = jnp.where(
        lane_z < 2 * YQ,
        high.astype(jnp.float32),
        jnp.where(lane_z < 3 * YQ, key_high, key_low),
    ).astype(jnp.bfloat16)
    tables = jnp.concatenate([high, mid, low], axis=1)
    on_z = ((owner >> 5) == iota((Z, QL * CL), 0)).astype(jnp.float32).astype(jnp.bfloat16)
    found = dot(tables, on_z, ((0,), (0,)))
    on_yq = (owner & 31) == iota((YQ, QL * CL), 0)

    def pick(rows):
        return jnp.sum(jnp.where(on_yq, rows, 0.0), axis=0, keepdims=True)

    score = found[0 : 2 * YQ] + found[128 : 128 + 2 * YQ] + found[256 : 256 + 2 * YQ]
    first = pick(found[2 * YQ : 3 * YQ] * 256.0 + found[3 * YQ : 4 * YQ])
    out = jnp.where(
        first.astype(jnp.int32) == own_key, pick(score[0:YQ]), pick(score[YQ : 2 * YQ])
    )
    row = iota((CL, 128), 0)
    res = jnp.zeros((CL, 128), jnp.float32)
    for i in range(4):
        for t in range(4):
            seg = jnp.broadcast_to(out[:, 128 * t : 128 * (t + 1)], (CL, 128))
            seg = pltpu.roll(seg, 128 - 32 * i, 1) if i else seg
            res = jnp.where(row == 4 * t + i, seg, res)
    o_ref[...] = res[:, :QL]


VMEM = pl.BlockSpec(memory_space=pltpu.VMEM)


def small_call(kernel, out_shape, *args):
    return pl.pallas_call(
        kernel,
        out_shape=out_shape,
        in_specs=[VMEM] * len(args),
        out_specs=jax.tree.map(lambda _: VMEM, out_shape),
    )(*[pltpu.with_memory_space_constraint(a, pltpu.VMEM) for a in args])


def shards(queries, passages, lengths, candidates):
    every = lax.all_gather(queries, "query", axis=0, tiled=True)
    cand = candidates.T
    table, keys = small_call(
        request_kernel,
        (
            pltpu.VMEM((Z, 128), jnp.int32),
            pltpu.VMEM((Z, 128), jnp.int32),
        ),
        cand,
    )
    got = exchange(table, Z_GROUPS)
    got = small_call(turn_kernel, pltpu.VMEM((YQ, 128), jnp.int32), got)
    codes = exchange(got, YQ_GROUPS)
    hbm = pl.BlockSpec(memory_space=pltpu.HBM)
    scores = pl.pallas_call(
        score_kernel,
        out_shape=jax.ShapeDtypeStruct((YQ, 128), jnp.float32),
        in_specs=[hbm, VMEM, hbm, hbm],
        out_specs=VMEM,
        scratch_shapes=[
            pltpu.SMEM((BLK,), jnp.int32),
            pltpu.VMEM((NQ, T, D), jnp.bfloat16),
            pltpu.VMEM((BLK, PT, D), jnp.bfloat16),
            pltpu.VMEM((2 * GROUP, 256), jnp.int32),
            pltpu.SMEM((2 * GROUP, 256), jnp.int32),
            pltpu.VMEM((GMAX, Q * 128), jnp.bfloat16),
            pltpu.VMEM((GMAX, GROUP * T), jnp.float32),
            pltpu.SemaphoreType.DMA,
            pltpu.SemaphoreType.DMA,
            pltpu.SemaphoreType.DMA,
            pltpu.SemaphoreType.DMA,
        ],
        compiler_params=pltpu.CompilerParams(vmem_limit_bytes=32 << 20),
    )(
        pltpu.with_memory_space_constraint(lengths, pltpu.HBM),
        pltpu.with_memory_space_constraint(codes, pltpu.VMEM),
        pltpu.with_memory_space_constraint(every, pltpu.HBM),
        pltpu.with_memory_space_constraint(passages, pltpu.HBM),
    )
    back = exchange(scores, YQ_GROUPS)
    back = small_call(back_kernel, pltpu.VMEM((Z, 128), jnp.float32), back)
    back = exchange(back, Z_GROUPS)
    out = small_call(
        place_kernel, jax.ShapeDtypeStruct((CL, QL), jnp.float32), cand, keys, back
    )
    return out.T


def solution(mesh):
    in_specs = (
        P("query", None, None),
        P(("index", "query"), None, None),
        P(("index", "query")),
        P("query", "index"),
    )
    return jax.shard_map(
        shards, mesh=mesh, in_specs=in_specs, out_specs=P("query", "index"), check_vma=False
    )
```

```python
import jax
import jax.numpy as jnp
from jax import lax
from jax.experimental import pallas as pl
from jax.experimental.pallas import tpu as pltpu
from jax.sharding import PartitionSpec as P

Z, Y, Q = 16, 4, 8
YQ = Y * Q
OWNERS = Z * YQ
BLK = 64
QL, CL = 32, 16
NQ = Q * QL
T, D, PT = 32, 128, 128
GROUP = 8
GMAX = 192
UNROLL = 8
BIG = 1 << 30

Z_GROUPS = [[r + YQ * z for z in range(Z)] for r in range(YQ)]
YQ_GROUPS = [[YQ * z + r for r in range(YQ)] for z in range(Z)]


def iota(shape, axis):
    return lax.broadcasted_iota(jnp.int32, shape, axis)


def exchange(x, groups):
    return lax.all_to_all(
        x, ("index", "query"), split_axis=0, concat_axis=0, tiled=True,
        axis_index_groups=groups,
    )


def spread(rows, row, lane):
    out = jnp.zeros((Z, 128), jnp.int32)
    for k, slot in enumerate(rows):
        for j in range(4):
            shift = (32 * k - 32 * j) % 128
            for t in range(4):
                seg = jnp.broadcast_to(slot[:, 128 * t : 128 * (t + 1)], (Z, 128))
                seg = pltpu.roll(seg, shift, 1) if shift else seg
                out = jnp.where((row == 4 * t + j) & (lane >> 5 == k), seg, out)
    return out


def request_kernel(cand_ref, code_ref, key_ref):
    cand = cand_ref[...]
    lane_owner = iota((CL, OWNERS), 1)
    sub = iota((CL, 1), 0)
    low = jnp.full((CL, OWNERS), BIG, jnp.int32)
    high = jnp.full((CL, OWNERS), -1, jnp.int32)
    for q in range(QL):
        col = cand[:, q : q + 1]
        key = (q << 10) + (sub << 6) + (col & 63)
        match = (col >> 6) == lane_owner
        low = jnp.minimum(low, jnp.where(match, key, BIG))
        high = jnp.maximum(high, jnp.where(match, key, -1))
    last = jnp.max(high, axis=0, keepdims=True)
    first = jnp.where(last >= 0, jnp.min(low, axis=0, keepdims=True), -1)
    last = jnp.where(last != first, last, -1)
    row = iota((Z, 128), 0)
    lane = iota((Z, 128), 1)
    key = spread((first, last), row, lane)
    key_ref[...] = key
    code_ref[...] = jnp.where(
        (key >= 0) & (lane < 2 * YQ), ((key >> 10) << 6) + (key & 63), -1
    )


def turn_kernel(x_ref, o_ref):
    x = jnp.concatenate([x_ref[...], jnp.zeros((112, 128), jnp.int32)], axis=0)
    xt = jnp.transpose(x)
    lane = iota((YQ, 128), 1)
    o_ref[...] = jnp.where(lane < Z, xt[:YQ], pltpu.roll(xt[YQ : 2 * YQ], Z, 1))


def back_kernel(x_ref, o_ref):
    x = jnp.concatenate([x_ref[...], jnp.zeros((96, 128), jnp.float32)], axis=0)
    xt = jnp.transpose(x)
    lane = iota((Z, 128), 1)
    o_ref[...] = jnp.where(lane < YQ, xt[:Z], pltpu.roll(xt[Z : 2 * Z], YQ, 1))


def split3(x):
    hi = x.astype(jnp.bfloat16)
    rest = x - hi.astype(jnp.float32)
    mid = rest.astype(jnp.bfloat16)
    low = (rest - mid.astype(jnp.float32)).astype(jnp.bfloat16)
    return hi, mid, low


def dot(a, b, dims):
    return lax.dot_general(a, b, (dims, ((), ())), preferred_element_type=jnp.float32)


def score_kernel(
    len_hbm, code_ref, same_ref, other_ref, p_hbm, o_ref,
    len_ref, q_ref, p_ref, plan, plan_s, onehot, best, sem, len_sem, same_sem, other_sem, p_sem,
):
    len_copy = pltpu.make_async_copy(len_hbm, len_ref, len_sem)
    len_copy.start()
    p_copy = pltpu.make_async_copy(p_hbm, p_ref, p_sem)
    p_copy.start()
    half = NQ // 2
    same_copy = pltpu.make_async_copy(same_ref, q_ref.at[pl.ds(0, half)], same_sem)
    same_copy.start()
    other_copy = pltpu.make_async_copy(other_ref, q_ref.at[pl.ds(half, half)], other_sem)
    other_copy.start()
    code = jnp.full((Q, 128), -1, jnp.int32)
    lane8 = iota((Q, 128), 1)
    for y in range(Y):
        part = code_ref[Q * y : Q * (y + 1), :]
        part = pltpu.roll(part, 32 * y, 1) if y else part
        code = jnp.where(lane8 >> 5 == y, part, code)
    valid = code >= 0
    block = jnp.where(valid, code & 63, BLK)
    me = lax.axis_index("query")
    source = iota((Q, 128), 0)
    piece = (((source ^ me) & 1) << 2) + (((me >> 1) - (source >> 1)) & 3)
    query = jnp.where(valid, (code >> 6) + QL * piece, 0)

    b_iota = iota((BLK, 128), 0)
    hits = [block[q : q + 1, :] == b_iota for q in range(Q)]
    hit = jnp.concatenate([h.astype(jnp.float32) for h in hits], axis=0).astype(jnp.bfloat16)
    r_i, c_i = iota((128, 128), 0), iota((128, 128), 1)
    earlier = jnp.concatenate(
        [(r_i < c_i).astype(jnp.float32), jnp.ones((128, 128), jnp.float32)], axis=1
    ).astype(jnp.bfloat16)
    sums = dot(hit, earlier, ((1,), (0,)))
    base = jnp.zeros((BLK, 128), jnp.float32)
    bases = []
    for q in range(Q):
        bases.append(base + sums[BLK * q : BLK * (q + 1), :128])
        base = base + sums[BLK * q : BLK * (q + 1), 128:]
    groups = ((base.astype(jnp.int32) + (GROUP - 1)) >> 3).astype(jnp.float32)
    l_i, m_i = iota((BLK, BLK), 0), iota((BLK, BLK), 1)
    before = dot(
        (m_i < l_i).astype(jnp.float32).astype(jnp.bfloat16),
        groups.astype(jnp.bfloat16),
        ((1,), (0,)),
    )
    ends = (before + groups).astype(jnp.int32)
    dest = jnp.concatenate(
        [
            jnp.sum(jnp.where(hits[q], GROUP * before + bases[q], 0.0), axis=0, keepdims=True)
            for q in range(Q)
        ],
        axis=0,
    ).astype(jnp.int32)

    g_iota = iota((GMAX, 128), 0)
    c_iota = iota((GROUP, 128), 0)
    named = []
    for q in range(Q):
        d = dest[q : q + 1, :]
        onehot[:, 128 * q : 128 * (q + 1)] = (
            ((d >> 3) == g_iota).astype(jnp.float32).astype(jnp.bfloat16)
        )
        here = ((d & 7) == c_iota) & valid[q : q + 1, :]
        named.append(jnp.where(here, query[q : q + 1, :], 0).astype(jnp.float32))
    lists = dot(
        jnp.concatenate(named, axis=1).astype(jnp.bfloat16), onehot[...], ((1,), (1,))
    )
    plan[0:GROUP, 0:GMAX] = lists.astype(jnp.int32)
    g_lane = iota((BLK, 256), 1)
    ends2 = jnp.concatenate([ends, ends], axis=1)
    owner_block = jnp.minimum(
        jnp.sum((ends2 <= g_lane).astype(jnp.int32), axis=0, keepdims=True), BLK - 1
    )
    total = jnp.broadcast_to(ends2[BLK - 1 : BLK, :], (1, 256))
    plan[GROUP : 2 * GROUP, :] = jnp.where(
        iota((GROUP, 256), 0) == 0,
        jnp.broadcast_to(owner_block, (GROUP, 256)),
        jnp.broadcast_to(total, (GROUP, 256)),
    )
    copy = pltpu.make_async_copy(plan, plan_s, sem)
    copy.start()
    best[...] = jnp.zeros((GMAX, GROUP * T), jnp.float32)
    copy.wait()
    len_copy.wait()
    p_copy.wait()
    same_copy.wait()
    other_copy.wait()

    token = iota((PT, GROUP * T), 0)

    def step(it, carry):
        rows = []
        for u in range(UNROLL):
            g = it * UNROLL + u
            b = plan_s[GROUP, g]
            rows_q = jnp.concatenate([q_ref[plan_s[c, g]] for c in range(GROUP)], axis=0)
            similar = dot(p_ref[b], rows_q, ((1,), (1,)))
            similar = jnp.where(token < len_ref[b], similar, -jnp.inf)
            rows.append(jnp.max(similar, axis=0, keepdims=True))
        best[pl.ds(pl.multiple_of(it * UNROLL, UNROLL), UNROLL), :] = jnp.concatenate(rows, axis=0)
        return carry

    lax.fori_loop(0, (plan_s[GROUP + 1, 0] + (UNROLL - 1)) // UNROLL, step, 0)

    w = (iota((GROUP, GROUP * T), 0) == (iota((GROUP, GROUP * T), 1) >> 5)).astype(jnp.float32)
    w = w.astype(jnp.bfloat16)
    means = sum(dot(w, part, ((1,), (1,))) for part in split3(best[...])) * (1.0 / T)
    picked = dot(jnp.concatenate(split3(means), axis=0), onehot[...], ((1,), (0,)))
    picked = picked[0:GROUP] + picked[GROUP : 2 * GROUP] + picked[2 * GROUP : 3 * GROUP]
    out = []
    for q in range(Q):
        here = (dest[q : q + 1, :] & 7) == c_iota
        out.append(
            jnp.sum(jnp.where(here, picked[:, 128 * q : 128 * (q + 1)], 0.0), axis=0, keepdims=True)
        )
    out = jnp.concatenate(out, axis=0)
    for y in range(Y):
        shift = (128 - 32 * y) % 128
        o_ref[Q * y : Q * (y + 1), :] = pltpu.roll(out, shift, 1) if shift else out


def place_kernel(cand_ref, key_ref, x_ref, o_ref):
    cand = jnp.concatenate([cand_ref[...], jnp.zeros((CL, 128 - QL), jnp.int32)], axis=1)
    lane = iota((1, 128), 1)
    turned = [cand] + [pltpu.roll(cand, 32 * i, 1) for i in range(1, 4)]
    segs = []
    for t in range(4):
        seg = turned[0][4 * t : 4 * t + 1, :]
        for i in range(1, 4):
            seg = jnp.where(lane >> 5 == i, turned[i][4 * t + i : 4 * t + i + 1, :], seg)
        segs.append(seg)
    asked = jnp.concatenate(segs, axis=1)
    place = iota((1, QL * CL), 1)
    own_key = ((place & 31) << 10) + ((place >> 5) << 6) + (asked & 63)
    owner = asked >> 6
    lane_z = iota((Z, 128), 1)
    x = jnp.where(lane_z < 2 * YQ, x_ref[...], 0.0)
    key = jnp.where(lane_z < YQ, key_ref[...], 0)
    key_high = pltpu.roll(key >> 8, 2 * YQ, 1).astype(jnp.float32)
    key_low = pltpu.roll(key & 255, 3 * YQ, 1).astype(jnp.float32)
    high, mid, low = split3(x)
    high = jnp.where(
        lane_z < 2 * YQ,
        high.astype(jnp.float32),
        jnp.where(lane_z < 3 * YQ, key_high, key_low),
    ).astype(jnp.bfloat16)
    tables = jnp.concatenate([high, mid, low], axis=1)
    on_z = ((owner >> 5) == iota((Z, QL * CL), 0)).astype(jnp.float32).astype(jnp.bfloat16)
    found = dot(tables, on_z, ((0,), (0,)))
    on_yq = (owner & 31) == iota((YQ, QL * CL), 0)

    def pick(rows):
        return jnp.sum(jnp.where(on_yq, rows, 0.0), axis=0, keepdims=True)

    score = found[0 : 2 * YQ] + found[128 : 128 + 2 * YQ] + found[256 : 256 + 2 * YQ]
    first = pick(found[2 * YQ : 3 * YQ] * 256.0 + found[3 * YQ : 4 * YQ])
    out = jnp.where(
        first.astype(jnp.int32) == own_key, pick(score[0:YQ]), pick(score[YQ : 2 * YQ])
    )
    row = iota((CL, 128), 0)
    res = jnp.zeros((CL, 128), jnp.float32)
    for i in range(4):
        for t in range(4):
            seg = jnp.broadcast_to(out[:, 128 * t : 128 * (t + 1)], (CL, 128))
            seg = pltpu.roll(seg, 128 - 32 * i, 1) if i else seg
            res = jnp.where(row == 4 * t + i, seg, res)
    o_ref[...] = res[:, :QL]


VMEM = pl.BlockSpec(memory_space=pltpu.VMEM)


def small_call(kernel, out_shape, *args):
    return pl.pallas_call(
        kernel,
        out_shape=out_shape,
        in_specs=[VMEM] * len(args),
        out_specs=jax.tree.map(lambda _: VMEM, out_shape),
    )(*[pltpu.with_memory_space_constraint(a, pltpu.VMEM) for a in args])


def shards(queries, passages, lengths, candidates):
    same = [queries] + [
        lax.ppermute(queries, "query", [(k, (k + 2 * d) % Q) for k in range(Q)])
        for d in range(1, Q // 2)
    ]
    cand = candidates.T
    table, keys = small_call(
        request_kernel,
        (
            pltpu.VMEM((Z, 128), jnp.int32),
            pltpu.VMEM((Z, 128), jnp.int32),
        ),
        cand,
    )
    got = exchange(table, Z_GROUPS)
    same = jnp.concatenate(same, axis=0)
    got, same = lax.optimization_barrier((got, same))
    other = lax.ppermute(same, "query", [(k, k ^ 1) for k in range(Q)])
    got = small_call(turn_kernel, pltpu.VMEM((YQ, 128), jnp.int32), got)
    codes = exchange(got, YQ_GROUPS)
    hbm = pl.BlockSpec(memory_space=pltpu.HBM)
    scores = pl.pallas_call(
        score_kernel,
        out_shape=jax.ShapeDtypeStruct((YQ, 128), jnp.float32),
        in_specs=[hbm, VMEM, VMEM, VMEM, hbm],
        out_specs=VMEM,
        scratch_shapes=[
            pltpu.SMEM((BLK,), jnp.int32),
            pltpu.VMEM((NQ, T, D), jnp.bfloat16),
            pltpu.VMEM((BLK, PT, D), jnp.bfloat16),
            pltpu.VMEM((2 * GROUP, 256), jnp.int32),
            pltpu.SMEM((2 * GROUP, 256), jnp.int32),
            pltpu.VMEM((GMAX, Q * 128), jnp.bfloat16),
            pltpu.VMEM((GMAX, GROUP * T), jnp.float32),
            pltpu.SemaphoreType.DMA,
            pltpu.SemaphoreType.DMA,
            pltpu.SemaphoreType.DMA,
            pltpu.SemaphoreType.DMA,
            pltpu.SemaphoreType.DMA,
        ],
        compiler_params=pltpu.CompilerParams(vmem_limit_bytes=32 << 20),
    )(
        pltpu.with_memory_space_constraint(lengths, pltpu.HBM),
        pltpu.with_memory_space_constraint(codes, pltpu.VMEM),
        pltpu.with_memory_space_constraint(same, pltpu.VMEM),
        pltpu.with_memory_space_constraint(other, pltpu.VMEM),
        pltpu.with_memory_space_constraint(passages, pltpu.HBM),
    )
    back = exchange(scores, YQ_GROUPS)
    back = small_call(back_kernel, pltpu.VMEM((Z, 128), jnp.float32), back)
    back = exchange(back, Z_GROUPS)
    out = small_call(
        place_kernel, jax.ShapeDtypeStruct((CL, QL), jnp.float32), cand, keys, back
    )
    return out.T


def solution(mesh):
    in_specs = (
        P("query", None, None),
        P(("index", "query"), None, None),
        P(("index", "query")),
        P("query", "index"),
    )
    return jax.shard_map(
        shards, mesh=mesh, in_specs=in_specs, out_specs=P("query", "index"), check_vma=False
    )
```

```python
import jax
import jax.numpy as jnp
from jax import lax
from jax.experimental import pallas as pl
from jax.experimental.pallas import tpu as pltpu
from jax.sharding import PartitionSpec as P

Z, Y, X, C = 16, 4, 4, 2
YX = Y * X
PLANE = YX * C
OWNERS = Z * PLANE
BLK = 64
BLOCKS = C * BLK
QL, CL = 32, 16
T, D, PT = 32, 128, 128
GROUP = 8
GMAX = 240
UNROLL = 8
BIG = 1 << 30

Z_GROUPS = [[r + PLANE * z for z in range(Z)] for r in range(PLANE)]
YX_GROUPS = [[PLANE * z + C * r + c for r in range(YX)] for z in range(Z) for c in range(C)]


def iota(shape, axis):
    return lax.broadcasted_iota(jnp.int32, shape, axis)


def exchange(x, groups):
    return lax.all_to_all(
        x, ("index", "query"), split_axis=0, concat_axis=0, tiled=True,
        axis_index_groups=groups,
    )


def place_of(cand):
    owner = cand >> 6
    return (owner & ~(PLANE - 1)) + ((owner & 1) << 4) + ((owner >> 1) & (YX - 1))


def spread(rows, row, lane):
    out = jnp.zeros((Z, 128), jnp.int32)
    for k, slot in enumerate(rows):
        for j in range(4):
            shift = (32 * k - 32 * j) % 128
            for t in range(4):
                seg = jnp.broadcast_to(slot[:, 128 * t : 128 * (t + 1)], (Z, 128))
                seg = pltpu.roll(seg, shift, 1) if shift else seg
                out = jnp.where((row == 4 * t + j) & (lane >> 5 == k), seg, out)
    return out


def request_kernel(cand_ref, code_ref, key_ref):
    cand = cand_ref[...]
    owners = place_of(cand)
    keys = (iota((CL, QL), 1) << 10) + (iota((CL, QL), 0) << 6) + (cand & 63)
    lane_owner = iota((CL, OWNERS), 1)
    low = jnp.full((CL, OWNERS), BIG, jnp.int32)
    high = jnp.full((CL, OWNERS), -1, jnp.int32)
    for q in range(QL):
        key = keys[:, q : q + 1]
        match = owners[:, q : q + 1] == lane_owner
        low = jnp.minimum(low, jnp.where(match, key, BIG))
        high = jnp.maximum(high, jnp.where(match, key, -1))
    last = jnp.max(high, axis=0, keepdims=True)
    first = jnp.where(last >= 0, jnp.min(low, axis=0, keepdims=True), -1)
    last = jnp.where(last != first, last, -1)
    row = iota((Z, 128), 0)
    lane = iota((Z, 128), 1)
    key = spread((first, last), row, lane)
    key_ref[...] = key
    code_ref[...] = jnp.where(
        (key >= 0) & (lane < 2 * PLANE), ((key >> 10) << 6) + (key & 63), -1
    )


def turn_kernel(x_ref, o_ref):
    x = x_ref[...]
    xt = jnp.transpose(jnp.concatenate([x, jnp.zeros((112, 128), x.dtype)], axis=0))
    lane = iota((16, 128), 1)
    out = xt[0:16]
    for m in range(1, 4):
        out = jnp.where(lane >> 4 == m, pltpu.roll(xt[16 * m : 16 * (m + 1)], 16 * m, 1), out)
    o_ref[...] = out


def split3(x):
    hi = x.astype(jnp.bfloat16)
    rest = x - hi.astype(jnp.float32)
    mid = rest.astype(jnp.bfloat16)
    low = (rest - mid.astype(jnp.float32)).astype(jnp.bfloat16)
    return hi, mid, low


def dot(a, b, dims):
    return lax.dot_general(a, b, (dims, ((), ())), preferred_element_type=jnp.float32)


def score_kernel(
    len_hbm, mate_len_hbm, code_ref, q0_hbm, q1_ref, q2_ref, q3_ref, p_hbm, mate_ref, o_ref,
    len_ref, q_ref, p_ref, plan, plan_s, onehot, best, sem, sems,
):
    moves = [(p_hbm, p_ref.at[pl.ds(0, BLK)]), (mate_ref, p_ref.at[pl.ds(BLK, BLK)])]
    for d, ref in enumerate((q0_hbm, q1_ref, q2_ref, q3_ref)):
        moves.append((ref, q_ref.at[pl.ds(QL * d, QL)]))
    moves += [(len_hbm, len_ref.at[0]), (mate_len_hbm, len_ref.at[1])]
    moves = [pltpu.make_async_copy(a, b, sems.at[i]) for i, (a, b) in enumerate(moves)]
    for move in moves:
        move.start()
    lane8 = iota((8, 128), 1)
    code = jnp.where(lane8 < 64, code_ref[0:8, :], pltpu.roll(code_ref[8:16, :], 64, 1))
    valid = code >= 0
    me = lax.axis_index("query")
    other = ((lane8 >> 4) ^ me) & 1
    block = jnp.where(valid, (other << 6) + (code & 63), BLOCKS)
    piece = ((me >> 1) - iota((8, 128), 0)) & (X - 1)
    query = jnp.where(valid, (code >> 6) + QL * piece, 0)

    b_iota = iota((BLOCKS, 128), 0)
    hits = [block[q : q + 1, :] == b_iota for q in range(8)]
    hit = jnp.concatenate([h.astype(jnp.float32) for h in hits], axis=0).astype(jnp.bfloat16)
    r_i, c_i = iota((128, 128), 0), iota((128, 128), 1)
    earlier = jnp.concatenate(
        [(r_i < c_i).astype(jnp.float32), jnp.ones((128, 128), jnp.float32)], axis=1
    ).astype(jnp.bfloat16)
    sums = dot(hit, earlier, ((1,), (0,)))
    base = jnp.zeros((BLOCKS, 128), jnp.float32)
    bases = []
    for q in range(8):
        bases.append(base + sums[BLOCKS * q : BLOCKS * (q + 1), :128])
        base = base + sums[BLOCKS * q : BLOCKS * (q + 1), 128:]
    groups = ((base.astype(jnp.int32) + (GROUP - 1)) >> 3).astype(jnp.float32)
    l_i, m_i = iota((BLOCKS, BLOCKS), 0), iota((BLOCKS, BLOCKS), 1)
    before = dot(
        (m_i < l_i).astype(jnp.float32).astype(jnp.bfloat16),
        groups.astype(jnp.bfloat16),
        ((1,), (0,)),
    )
    ends = (before + groups).astype(jnp.int32)
    dest = jnp.concatenate(
        [
            jnp.sum(jnp.where(hits[q], GROUP * before + bases[q], 0.0), axis=0, keepdims=True)
            for q in range(8)
        ],
        axis=0,
    ).astype(jnp.int32)

    g_iota = iota((GMAX, 128), 0)
    c_iota = iota((GROUP, 128), 0)
    named = []
    for q in range(8):
        d = dest[q : q + 1, :]
        onehot[:, 128 * q : 128 * (q + 1)] = (
            ((d >> 3) == g_iota).astype(jnp.float32).astype(jnp.bfloat16)
        )
        here = ((d & 7) == c_iota) & valid[q : q + 1, :]
        named.append(jnp.where(here, query[q : q + 1, :], 0).astype(jnp.float32))
    lists = dot(
        jnp.concatenate(named, axis=1).astype(jnp.bfloat16), onehot[...], ((1,), (1,))
    )
    plan[0:GROUP, 0:GMAX] = lists.astype(jnp.int32)
    g_lane = iota((BLOCKS, 256), 1)
    ends2 = jnp.concatenate([ends, ends], axis=1)
    owner_block = jnp.minimum(
        jnp.sum((ends2 <= g_lane).astype(jnp.int32), axis=0, keepdims=True), BLOCKS - 1
    )
    total = jnp.broadcast_to(ends2[BLOCKS - 1 : BLOCKS, :], (1, 256))
    plan[GROUP : 2 * GROUP, :] = jnp.where(
        iota((GROUP, 256), 0) == 0,
        jnp.broadcast_to(owner_block, (GROUP, 256)),
        jnp.broadcast_to(total, (GROUP, 256)),
    )
    copy = pltpu.make_async_copy(plan, plan_s, sem)
    copy.start()
    best[...] = jnp.zeros((GMAX, GROUP * T), jnp.float32)
    copy.wait()
    for move in moves:
        move.wait()

    token = iota((PT, GROUP * T), 0)

    def step(it, carry):
        rows = []
        for u in range(UNROLL):
            g = it * UNROLL + u
            b = plan_s[GROUP, g]
            rows_q = jnp.concatenate([q_ref[plan_s[c, g]] for c in range(GROUP)], axis=0)
            similar = dot(p_ref[b], rows_q, ((1,), (1,)))
            similar = jnp.where(token < len_ref[b >> 6, b & 63], similar, -jnp.inf)
            rows.append(jnp.max(similar, axis=0, keepdims=True))
        best[pl.ds(pl.multiple_of(it * UNROLL, UNROLL), UNROLL), :] = jnp.concatenate(rows, axis=0)
        return carry

    lax.fori_loop(0, (plan_s[GROUP + 1, 0] + (UNROLL - 1)) // UNROLL, step, 0)

    w = (iota((GROUP, GROUP * T), 0) == (iota((GROUP, GROUP * T), 1) >> 5)).astype(jnp.float32)
    w = w.astype(jnp.bfloat16)
    means = sum(dot(w, part, ((1,), (1,))) for part in split3(best[...])) * (1.0 / T)
    picked = dot(jnp.concatenate(split3(means), axis=0), onehot[...], ((1,), (0,)))
    picked = picked[0:GROUP] + picked[GROUP : 2 * GROUP] + picked[2 * GROUP : 3 * GROUP]
    out = []
    for q in range(8):
        here = (dest[q : q + 1, :] & 7) == c_iota
        out.append(
            jnp.sum(jnp.where(here, picked[:, 128 * q : 128 * (q + 1)], 0.0), axis=0, keepdims=True)
        )
    out = jnp.concatenate(out, axis=0)
    o_ref[0:8, :] = out
    o_ref[8:16, :] = pltpu.roll(out, 64, 1)


def place_kernel(cand_ref, key_ref, x_ref, o_ref):
    cand = jnp.concatenate([cand_ref[...], jnp.zeros((CL, 128 - QL), jnp.int32)], axis=1)
    lane = iota((1, 128), 1)
    turned = [cand] + [pltpu.roll(cand, 32 * i, 1) for i in range(1, 4)]
    segs = []
    for t in range(4):
        seg = turned[0][4 * t : 4 * t + 1, :]
        for i in range(1, 4):
            seg = jnp.where(lane >> 5 == i, turned[i][4 * t + i : 4 * t + i + 1, :], seg)
        segs.append(seg)
    asked = jnp.concatenate(segs, axis=1)
    place = iota((1, QL * CL), 1)
    own_key = ((place & 31) << 10) + ((place >> 5) << 6) + (asked & 63)
    owner = place_of(asked)
    lane_z = iota((Z, 128), 1)
    x = jnp.where(lane_z < 2 * PLANE, x_ref[...], 0.0)
    key = jnp.where(lane_z < PLANE, key_ref[...], 0)
    key_high = pltpu.roll(key >> 8, 2 * PLANE, 1).astype(jnp.float32)
    key_low = pltpu.roll(key & 255, 3 * PLANE, 1).astype(jnp.float32)
    high, mid, low = split3(x)
    high = jnp.where(
        lane_z < 2 * PLANE,
        high.astype(jnp.float32),
        jnp.where(lane_z < 3 * PLANE, key_high, key_low),
    ).astype(jnp.bfloat16)
    tables = jnp.concatenate([high, mid, low], axis=1)
    on_z = ((owner >> 5) == iota((Z, QL * CL), 0)).astype(jnp.float32).astype(jnp.bfloat16)
    found = dot(tables, on_z, ((0,), (0,)))
    on_plane = (owner & 31) == iota((PLANE, QL * CL), 0)

    def pick(rows):
        return jnp.sum(jnp.where(on_plane, rows, 0.0), axis=0, keepdims=True)

    score = found[0 : 2 * PLANE] + found[128 : 128 + 2 * PLANE] + found[256 : 256 + 2 * PLANE]
    first = pick(found[2 * PLANE : 3 * PLANE] * 256.0 + found[3 * PLANE : 4 * PLANE])
    out = jnp.where(
        first.astype(jnp.int32) == own_key, pick(score[0:PLANE]), pick(score[PLANE : 2 * PLANE])
    )
    row = iota((CL, 128), 0)
    res = jnp.zeros((CL, 128), jnp.float32)
    for i in range(4):
        for t in range(4):
            seg = jnp.broadcast_to(out[:, 128 * t : 128 * (t + 1)], (CL, 128))
            seg = pltpu.roll(seg, 128 - 32 * i, 1) if i else seg
            res = jnp.where(row == 4 * t + i, seg, res)
    o_ref[...] = res[:, :QL]


VMEM = pl.BlockSpec(memory_space=pltpu.VMEM)


def small_call(kernel, out_shape, *args):
    return pl.pallas_call(
        kernel,
        out_shape=out_shape,
        in_specs=[VMEM] * len(args),
        out_specs=jax.tree.map(lambda _: VMEM, out_shape),
    )(*[pltpu.with_memory_space_constraint(a, pltpu.VMEM) for a in args])


def shards(queries, passages, lengths, candidates):
    same = [queries] + [
        lax.ppermute(queries, "query", [(k, (k + C * d) % (X * C)) for k in range(X * C)])
        for d in range(1, X)
    ]
    cand = candidates.T
    table, keys = small_call(
        request_kernel,
        (pltpu.VMEM((Z, 128), jnp.int32), pltpu.VMEM((Z, 128), jnp.int32)),
        cand,
    )
    mates = [(k, k ^ 1) for k in range(X * C)]
    mate = lax.ppermute(passages, "query", mates)
    mate_len = lax.ppermute(lengths, "query", mates)
    got = exchange(table, Z_GROUPS)
    got, mate, mate_len, *same = lax.optimization_barrier((got, mate, mate_len, *same))
    got = small_call(turn_kernel, pltpu.VMEM((YX, 128), jnp.int32), got)
    codes = exchange(got, YX_GROUPS)
    hbm = pl.BlockSpec(memory_space=pltpu.HBM)

    def at(x, space):
        return pltpu.with_memory_space_constraint(x, space)

    scores = pl.pallas_call(
        score_kernel,
        out_shape=pltpu.VMEM((YX, 128), jnp.float32),
        in_specs=[hbm, hbm, VMEM, hbm, VMEM, VMEM, VMEM, hbm, VMEM],
        out_specs=VMEM,
        scratch_shapes=[
            pltpu.SMEM((C, BLK), jnp.int32),
            pltpu.VMEM((X * QL, T, D), jnp.bfloat16),
            pltpu.VMEM((BLOCKS, PT, D), jnp.bfloat16),
            pltpu.VMEM((2 * GROUP, 256), jnp.int32),
            pltpu.SMEM((2 * GROUP, 256), jnp.int32),
            pltpu.VMEM((GMAX, 1024), jnp.bfloat16),
            pltpu.VMEM((GMAX, GROUP * T), jnp.float32),
            pltpu.SemaphoreType.DMA,
            pltpu.SemaphoreType.DMA((8,)),
        ],
        compiler_params=pltpu.CompilerParams(vmem_limit_bytes=32 << 20),
    )(
        at(lengths, pltpu.HBM), at(mate_len, pltpu.HBM), at(codes, pltpu.VMEM),
        at(queries, pltpu.HBM), *[at(x, pltpu.VMEM) for x in same[1:]],
        at(passages, pltpu.HBM), at(mate, pltpu.VMEM),
    )
    back = exchange(scores, YX_GROUPS)
    back = small_call(turn_kernel, pltpu.VMEM((Z, 128), jnp.float32), back)
    back = exchange(back, Z_GROUPS)
    out = small_call(
        place_kernel, jax.ShapeDtypeStruct((CL, QL), jnp.float32), cand, keys, back
    )
    return out.T


def solution(mesh):
    in_specs = (
        P("query", None, None),
        P(("index", "query"), None, None),
        P(("index", "query")),
        P("query", "index"),
    )
    return jax.shard_map(
        shards, mesh=mesh, in_specs=in_specs, out_specs=P("query", "index"), check_vma=False
    )
```

```python
import jax
import jax.numpy as jnp
from jax import lax
from jax.experimental import pallas as pl
from jax.experimental.pallas import tpu as pltpu
from jax.sharding import PartitionSpec as P

Z, Y, Q = 16, 4, 8
YQ = Y * Q
OWNERS = Z * YQ
BLK = 64
QL, CL = 32, 16
NQ = Q * QL
T, D, PT = 32, 128, 128
GROUP = 8
GMAX = 192
UNROLL = 32
BIG = 1 << 30

Z_GROUPS = [[r + YQ * z for z in range(Z)] for r in range(YQ)]
YQ_GROUPS = [[YQ * z + r for r in range(YQ)] for z in range(Z)]


def iota(shape, axis):
    return lax.broadcasted_iota(jnp.int32, shape, axis)


def exchange(x, groups):
    return lax.all_to_all(
        x, ("index", "query"), split_axis=0, concat_axis=0, tiled=True,
        axis_index_groups=groups,
    )


def spread(rows, row, lane):
    out = jnp.zeros((Z, 128), jnp.int32)
    for k, slot in enumerate(rows):
        for j in range(4):
            shift = (32 * k - 32 * j) % 128
            for t in range(4):
                seg = jnp.broadcast_to(slot[:, 128 * t : 128 * (t + 1)], (Z, 128))
                seg = pltpu.roll(seg, shift, 1) if shift else seg
                out = jnp.where((row == 4 * t + j) & (lane >> 5 == k), seg, out)
    return out


def request_kernel(cand_hbm, code_ref, key_ref, cand_ref, sem):
    copy = pltpu.make_async_copy(cand_hbm, cand_ref, sem)
    copy.start()
    copy.wait()
    cand = cand_ref[...]
    lane_owner = iota((CL, OWNERS), 1)
    sub = iota((CL, 1), 0)
    low = jnp.full((CL, OWNERS), BIG, jnp.int32)
    high = jnp.full((CL, OWNERS), -1, jnp.int32)
    for q in range(QL):
        col = cand[:, q : q + 1]
        key = (q << 10) + (sub << 6) + (col & 63)
        match = (col >> 6) == lane_owner
        low = jnp.minimum(low, jnp.where(match, key, BIG))
        high = jnp.maximum(high, jnp.where(match, key, -1))
    last = jnp.max(high, axis=0, keepdims=True)
    first = jnp.where(last >= 0, jnp.min(low, axis=0, keepdims=True), -1)
    last = jnp.where(last != first, last, -1)
    row = iota((Z, 128), 0)
    lane = iota((Z, 128), 1)
    key = spread((first, last), row, lane)
    key_ref[...] = key
    code_ref[...] = jnp.where(
        (key >= 0) & (lane < 2 * YQ), ((key >> 10) << 6) + (key & 63), -1
    )


def turn_kernel(x_ref, o_ref):
    x = jnp.concatenate([x_ref[...], jnp.zeros((112, 128), jnp.int32)], axis=0)
    xt = jnp.transpose(x)
    lane = iota((YQ, 128), 1)
    o_ref[...] = jnp.where(lane < Z, xt[:YQ], pltpu.roll(xt[YQ : 2 * YQ], Z, 1))


def back_kernel(x_ref, o_ref):
    x = jnp.concatenate([x_ref[...], jnp.zeros((96, 128), jnp.float32)], axis=0)
    xt = jnp.transpose(x)
    lane = iota((Z, 128), 1)
    o_ref[...] = jnp.where(lane < YQ, xt[:Z], pltpu.roll(xt[Z : 2 * Z], YQ, 1))


def split3(x):
    hi = x.astype(jnp.bfloat16)
    rest = x - hi.astype(jnp.float32)
    mid = rest.astype(jnp.bfloat16)
    low = (rest - mid.astype(jnp.float32)).astype(jnp.bfloat16)
    return hi, mid, low


def dot(a, b, dims):
    return lax.dot_general(a, b, (dims, ((), ())), preferred_element_type=jnp.float32)


def score_kernel(
    len_hbm, code_ref, same_ref, other_ref, p_hbm, o_ref,
    len_ref, q_ref, p_ref, plan, plan_s, onehot, best, sem, len_sem, same_sem, other_sem, p_sem,
):
    len_copy = pltpu.make_async_copy(len_hbm, len_ref, len_sem)
    len_copy.start()
    p_copy = pltpu.make_async_copy(p_hbm, p_ref, p_sem)
    p_copy.start()
    half = NQ // 2
    same_copy = pltpu.make_async_copy(same_ref, q_ref.at[pl.ds(0, half)], same_sem)
    same_copy.start()
    other_copy = pltpu.make_async_copy(other_ref, q_ref.at[pl.ds(half, half)], other_sem)
    other_copy.start()
    code = jnp.full((Q, 128), -1, jnp.int32)
    lane8 = iota((Q, 128), 1)
    for y in range(Y):
        part = code_ref[Q * y : Q * (y + 1), :]
        part = pltpu.roll(part, 32 * y, 1) if y else part
        code = jnp.where(lane8 >> 5 == y, part, code)
    valid = code >= 0
    block = jnp.where(valid, code & 63, BLK)
    me = lax.axis_index("query")
    source = iota((Q, 128), 0)
    piece = (((source ^ me) & 1) << 2) + (((me >> 1) - (source >> 1)) & 3)
    query = jnp.where(valid, (code >> 6) + QL * piece, 0)

    b_iota = iota((BLK, 128), 0)
    hits = [block[q : q + 1, :] == b_iota for q in range(Q)]
    hit = jnp.concatenate([h.astype(jnp.float32) for h in hits], axis=0).astype(jnp.bfloat16)
    r_i, c_i = iota((128, 128), 0), iota((128, 128), 1)
    earlier = jnp.concatenate(
        [(r_i < c_i).astype(jnp.float32), jnp.ones((128, 128), jnp.float32)], axis=1
    ).astype(jnp.bfloat16)
    sums = dot(hit, earlier, ((1,), (0,)))
    base = jnp.zeros((BLK, 128), jnp.float32)
    bases = []
    for q in range(Q):
        bases.append(base + sums[BLK * q : BLK * (q + 1), :128])
        base = base + sums[BLK * q : BLK * (q + 1), 128:]
    groups = ((base.astype(jnp.int32) + (GROUP - 1)) >> 3).astype(jnp.float32)
    l_i, m_i = iota((BLK, BLK), 0), iota((BLK, BLK), 1)
    before = dot(
        (m_i < l_i).astype(jnp.float32).astype(jnp.bfloat16),
        groups.astype(jnp.bfloat16),
        ((1,), (0,)),
    )
    ends = (before + groups).astype(jnp.int32)
    dest = jnp.concatenate(
        [
            jnp.sum(jnp.where(hits[q], GROUP * before + bases[q], 0.0), axis=0, keepdims=True)
            for q in range(Q)
        ],
        axis=0,
    ).astype(jnp.int32)

    g_iota = iota((GMAX, 128), 0)
    c_iota = iota((GROUP, 128), 0)
    named = []
    for q in range(Q):
        d = dest[q : q + 1, :]
        onehot[:, 128 * q : 128 * (q + 1)] = (
            ((d >> 3) == g_iota).astype(jnp.float32).astype(jnp.bfloat16)
        )
        here = ((d & 7) == c_iota) & valid[q : q + 1, :]
        named.append(jnp.where(here, query[q : q + 1, :], 0).astype(jnp.float32))
    lists = dot(
        jnp.concatenate(named, axis=1).astype(jnp.bfloat16), onehot[...], ((1,), (1,))
    )
    plan[0:GROUP, 0:GMAX] = lists.astype(jnp.int32)
    g_lane = iota((BLK, 256), 1)
    ends2 = jnp.concatenate([ends, ends], axis=1)
    owner_block = jnp.minimum(
        jnp.sum((ends2 <= g_lane).astype(jnp.int32), axis=0, keepdims=True), BLK - 1
    )
    total = jnp.broadcast_to(ends2[BLK - 1 : BLK, :], (1, 256))
    plan[GROUP : 2 * GROUP, :] = jnp.where(
        iota((GROUP, 256), 0) == 0,
        jnp.broadcast_to(owner_block, (GROUP, 256)),
        jnp.broadcast_to(total, (GROUP, 256)),
    )
    copy = pltpu.make_async_copy(plan, plan_s, sem)
    copy.start()
    best[...] = jnp.zeros((GMAX, GROUP * T), jnp.float32)
    copy.wait()
    len_copy.wait()
    p_copy.wait()
    same_copy.wait()
    other_copy.wait()

    token = iota((PT, GROUP * T), 0)

    def step(it, carry):
        rows = []
        for u in range(UNROLL):
            g = it * UNROLL + u
            b = plan_s[GROUP, g]
            rows_q = jnp.concatenate([q_ref[plan_s[c, g]] for c in range(GROUP)], axis=0)
            similar = dot(p_ref[b], rows_q, ((1,), (1,)))
            similar = jnp.where(token < len_ref[b], similar, -jnp.inf)
            rows.append(jnp.max(similar, axis=0, keepdims=True))
        best[pl.ds(pl.multiple_of(it * UNROLL, UNROLL), UNROLL), :] = jnp.concatenate(rows, axis=0)
        return carry

    lax.fori_loop(0, (plan_s[GROUP + 1, 0] + (UNROLL - 1)) // UNROLL, step, 0)

    w = (iota((GROUP, GROUP * T), 0) == (iota((GROUP, GROUP * T), 1) >> 5)).astype(jnp.float32)
    w = w.astype(jnp.bfloat16)
    means = sum(dot(w, part, ((1,), (1,))) for part in split3(best[...])) * (1.0 / T)
    picked = dot(jnp.concatenate(split3(means), axis=0), onehot[...], ((1,), (0,)))
    picked = picked[0:GROUP] + picked[GROUP : 2 * GROUP] + picked[2 * GROUP : 3 * GROUP]
    out = []
    for q in range(Q):
        here = (dest[q : q + 1, :] & 7) == c_iota
        out.append(
            jnp.sum(jnp.where(here, picked[:, 128 * q : 128 * (q + 1)], 0.0), axis=0, keepdims=True)
        )
    out = jnp.concatenate(out, axis=0)
    for y in range(Y):
        shift = (128 - 32 * y) % 128
        o_ref[Q * y : Q * (y + 1), :] = pltpu.roll(out, shift, 1) if shift else out


def place_kernel(cand_ref, key_ref, x_ref, o_ref):
    cand = jnp.concatenate([cand_ref[...], jnp.zeros((CL, 128 - QL), jnp.int32)], axis=1)
    lane = iota((1, 128), 1)
    turned = [cand] + [pltpu.roll(cand, 32 * i, 1) for i in range(1, 4)]
    segs = []
    for t in range(4):
        seg = turned[0][4 * t : 4 * t + 1, :]
        for i in range(1, 4):
            seg = jnp.where(lane >> 5 == i, turned[i][4 * t + i : 4 * t + i + 1, :], seg)
        segs.append(seg)
    asked = jnp.concatenate(segs, axis=1)
    place = iota((1, QL * CL), 1)
    own_key = ((place & 31) << 10) + ((place >> 5) << 6) + (asked & 63)
    owner = asked >> 6
    lane_z = iota((Z, 128), 1)
    x = jnp.where(lane_z < 2 * YQ, x_ref[...], 0.0)
    key = jnp.where(lane_z < YQ, key_ref[...], 0)
    key_high = pltpu.roll(key >> 8, 2 * YQ, 1).astype(jnp.float32)
    key_low = pltpu.roll(key & 255, 3 * YQ, 1).astype(jnp.float32)
    high, mid, low = split3(x)
    high = jnp.where(
        lane_z < 2 * YQ,
        high.astype(jnp.float32),
        jnp.where(lane_z < 3 * YQ, key_high, key_low),
    ).astype(jnp.bfloat16)
    tables = jnp.concatenate([high, mid, low], axis=1)
    on_z = ((owner >> 5) == iota((Z, QL * CL), 0)).astype(jnp.float32).astype(jnp.bfloat16)
    found = dot(tables, on_z, ((0,), (0,)))
    on_yq = (owner & 31) == iota((YQ, QL * CL), 0)

    def pick(rows):
        return jnp.sum(jnp.where(on_yq, rows, 0.0), axis=0, keepdims=True)

    score = found[0 : 2 * YQ] + found[128 : 128 + 2 * YQ] + found[256 : 256 + 2 * YQ]
    first = pick(found[2 * YQ : 3 * YQ] * 256.0 + found[3 * YQ : 4 * YQ])
    out = jnp.where(
        first.astype(jnp.int32) == own_key, pick(score[0:YQ]), pick(score[YQ : 2 * YQ])
    )
    row = iota((CL, 128), 0)
    res = jnp.zeros((CL, 128), jnp.float32)
    for i in range(4):
        for t in range(4):
            seg = jnp.broadcast_to(out[:, 128 * t : 128 * (t + 1)], (CL, 128))
            seg = pltpu.roll(seg, 128 - 32 * i, 1) if i else seg
            res = jnp.where(row == 4 * t + i, seg, res)
    o_ref[...] = res[:, :QL]


VMEM = pl.BlockSpec(memory_space=pltpu.VMEM)


def small_call(kernel, out_shape, *args):
    return pl.pallas_call(
        kernel,
        out_shape=out_shape,
        in_specs=[VMEM] * len(args),
        out_specs=jax.tree.map(lambda _: VMEM, out_shape),
    )(*[pltpu.with_memory_space_constraint(a, pltpu.VMEM) for a in args])


def shards(queries, passages, lengths, candidates):
    same = [queries] + [
        lax.ppermute(queries, "query", [(k, (k + 2 * d) % Q) for k in range(Q)])
        for d in range(1, Q // 2)
    ]
    cand = candidates.T
    table, keys = pl.pallas_call(
        request_kernel,
        out_shape=(pltpu.VMEM((Z, 128), jnp.int32), pltpu.VMEM((Z, 128), jnp.int32)),
        in_specs=[pl.BlockSpec(memory_space=pltpu.HBM)],
        out_specs=(VMEM, VMEM),
        scratch_shapes=[pltpu.VMEM((CL, QL), jnp.int32), pltpu.SemaphoreType.DMA],
    )(pltpu.with_memory_space_constraint(cand, pltpu.HBM))
    got = exchange(table, Z_GROUPS)
    same = jnp.concatenate(same, axis=0)
    got, same = lax.optimization_barrier((got, same))
    other = lax.ppermute(same, "query", [(k, k ^ 1) for k in range(Q)])
    got = small_call(turn_kernel, pltpu.VMEM((YQ, 128), jnp.int32), got)
    codes = exchange(got, YQ_GROUPS)
    hbm = pl.BlockSpec(memory_space=pltpu.HBM)
    scores = pl.pallas_call(
        score_kernel,
        out_shape=jax.ShapeDtypeStruct((YQ, 128), jnp.float32),
        in_specs=[hbm, VMEM, VMEM, VMEM, hbm],
        out_specs=VMEM,
        scratch_shapes=[
            pltpu.SMEM((BLK,), jnp.int32),
            pltpu.VMEM((NQ, T, D), jnp.bfloat16),
            pltpu.VMEM((BLK, PT, D), jnp.bfloat16),
            pltpu.VMEM((2 * GROUP, 256), jnp.int32),
            pltpu.SMEM((2 * GROUP, 256), jnp.int32),
            pltpu.VMEM((GMAX, Q * 128), jnp.bfloat16),
            pltpu.VMEM((GMAX, GROUP * T), jnp.float32),
            pltpu.SemaphoreType.DMA,
            pltpu.SemaphoreType.DMA,
            pltpu.SemaphoreType.DMA,
            pltpu.SemaphoreType.DMA,
            pltpu.SemaphoreType.DMA,
        ],
        compiler_params=pltpu.CompilerParams(vmem_limit_bytes=32 << 20),
    )(
        pltpu.with_memory_space_constraint(lengths, pltpu.HBM),
        pltpu.with_memory_space_constraint(codes, pltpu.VMEM),
        pltpu.with_memory_space_constraint(same, pltpu.VMEM),
        pltpu.with_memory_space_constraint(other, pltpu.VMEM),
        pltpu.with_memory_space_constraint(passages, pltpu.HBM),
    )
    back = exchange(scores, YQ_GROUPS)
    back = small_call(back_kernel, pltpu.VMEM((Z, 128), jnp.float32), back)
    back = exchange(back, Z_GROUPS)
    out = small_call(
        place_kernel, jax.ShapeDtypeStruct((CL, QL), jnp.float32), cand, keys, back
    )
    return out.T


def solution(mesh):
    in_specs = (
        P("query", None, None),
        P(("index", "query"), None, None),
        P(("index", "query")),
        P("query", "index"),
    )
    return jax.shard_map(
        shards, mesh=mesh, in_specs=in_specs, out_specs=P("query", "index"), check_vma=False
    )
```

```python
import jax
import jax.numpy as jnp
from jax import lax
from jax.experimental import pallas as pl
from jax.experimental.pallas import tpu as pltpu
from jax.sharding import PartitionSpec as P

Z, Y, Q = 16, 4, 8
YQ = Y * Q
OWNERS = Z * YQ
BLK = 64
QL, CL = 32, 16
NQ = Q * QL
T, D, PT = 32, 128, 128
GROUP = 8
GMAX = 192
UNROLL = 32
BIG = 1 << 30

Z_GROUPS = [[r + YQ * z for z in range(Z)] for r in range(YQ)]
YQ_GROUPS = [[YQ * z + r for r in range(YQ)] for z in range(Z)]


def iota(shape, axis):
    return lax.broadcasted_iota(jnp.int32, shape, axis)


def exchange(x, groups):
    return lax.all_to_all(
        x, ("index", "query"), split_axis=0, concat_axis=0, tiled=True,
        axis_index_groups=groups,
    )


def spread(rows, row, lane):
    out = jnp.zeros((Z, 128), jnp.int32)
    for k, slot in enumerate(rows):
        for j in range(4):
            shift = (32 * k - 32 * j) % 128
            for t in range(4):
                seg = jnp.broadcast_to(slot[:, 128 * t : 128 * (t + 1)], (Z, 128))
                seg = pltpu.roll(seg, shift, 1) if shift else seg
                out = jnp.where((row == 4 * t + j) & (lane >> 5 == k), seg, out)
    return out


def by_plane(x):
    xt = jnp.transpose(jnp.concatenate([x, jnp.zeros((112, 128), x.dtype)], axis=0))
    lane = iota((YQ, 128), 1)
    return jnp.where(lane < Z, xt[:YQ], pltpu.roll(xt[YQ : 2 * YQ], Z, 1))


def by_z(x):
    xt = jnp.transpose(jnp.concatenate([x, jnp.zeros((96, 128), x.dtype)], axis=0))
    lane = iota((Z, 128), 1)
    return jnp.where(lane < YQ, xt[:Z], pltpu.roll(xt[Z : 2 * Z], YQ, 1))


def by_plane_kernel(x_ref, o_ref):
    o_ref[...] = by_plane(x_ref[...])


def by_z_kernel(x_ref, o_ref):
    o_ref[...] = by_z(x_ref[...])


def request_kernel(cand_ref, code_ref, key_ref):
    cand = cand_ref[...]
    lane_owner = iota((CL, OWNERS), 1)
    sub = iota((CL, 1), 0)
    low = jnp.full((CL, OWNERS), BIG, jnp.int32)
    high = jnp.full((CL, OWNERS), -1, jnp.int32)
    for q in range(QL):
        col = cand[:, q : q + 1]
        key = (q << 10) + (sub << 6) + (col & 63)
        match = (col >> 6) == lane_owner
        low = jnp.minimum(low, jnp.where(match, key, BIG))
        high = jnp.maximum(high, jnp.where(match, key, -1))
    last = jnp.max(high, axis=0, keepdims=True)
    first = jnp.where(last >= 0, jnp.min(low, axis=0, keepdims=True), -1)
    last = jnp.where(last != first, last, -1)
    row = iota((Z, 128), 0)
    lane = iota((Z, 128), 1)
    key = spread((first, last), row, lane)
    key_ref[...] = key
    code = jnp.where((key >= 0) & (lane < 2 * YQ), ((key >> 10) << 6) + (key & 63), -1)
    code_ref[...] = by_plane(code)


def split3(x):
    hi = x.astype(jnp.bfloat16)
    rest = x - hi.astype(jnp.float32)
    mid = rest.astype(jnp.bfloat16)
    low = (rest - mid.astype(jnp.float32)).astype(jnp.bfloat16)
    return hi, mid, low


def dot(a, b, dims):
    return lax.dot_general(a, b, (dims, ((), ())), preferred_element_type=jnp.float32)


def score_kernel(
    len_hbm, code_ref, same_ref, other_ref, p_hbm, o_ref,
    len_ref, q_ref, p_ref, plan, plan_s, onehot, best, sem, len_sem, same_sem, other_sem, p_sem,
):
    len_copy = pltpu.make_async_copy(len_hbm, len_ref, len_sem)
    len_copy.start()
    p_copy = pltpu.make_async_copy(p_hbm, p_ref, p_sem)
    p_copy.start()
    half = NQ // 2
    same_copy = pltpu.make_async_copy(same_ref, q_ref.at[pl.ds(0, half)], same_sem)
    same_copy.start()
    other_copy = pltpu.make_async_copy(other_ref, q_ref.at[pl.ds(half, half)], other_sem)
    other_copy.start()
    lane8 = iota((Q, 128), 1)
    code = jnp.where(lane8 < 64, code_ref[0:8, :], pltpu.roll(code_ref[8:16, :], 64, 1))
    valid = code >= 0
    block = jnp.where(valid, code & 63, BLK)
    me = lax.axis_index("query")
    source = lane8 & (Q - 1)
    piece = (((source ^ me) & 1) << 2) + (((me >> 1) - (source >> 1)) & 3)
    query = jnp.where(valid, (code >> 6) + QL * piece, 0)

    b_iota = iota((BLK, 128), 0)
    hits = [block[q : q + 1, :] == b_iota for q in range(Q)]
    hit = jnp.concatenate([h.astype(jnp.float32) for h in hits], axis=0).astype(jnp.bfloat16)
    r_i, c_i = iota((128, 128), 0), iota((128, 128), 1)
    earlier = jnp.concatenate(
        [(r_i < c_i).astype(jnp.float32), jnp.ones((128, 128), jnp.float32)], axis=1
    ).astype(jnp.bfloat16)
    sums = dot(hit, earlier, ((1,), (0,)))
    base = jnp.zeros((BLK, 128), jnp.float32)
    bases = []
    for q in range(Q):
        bases.append(base + sums[BLK * q : BLK * (q + 1), :128])
        base = base + sums[BLK * q : BLK * (q + 1), 128:]
    groups = ((base.astype(jnp.int32) + (GROUP - 1)) >> 3).astype(jnp.float32)
    l_i, m_i = iota((BLK, BLK), 0), iota((BLK, BLK), 1)
    before = dot(
        (m_i < l_i).astype(jnp.float32).astype(jnp.bfloat16),
        groups.astype(jnp.bfloat16),
        ((1,), (0,)),
    )
    ends = (before + groups).astype(jnp.int32)
    dest = jnp.concatenate(
        [
            jnp.sum(jnp.where(hits[q], GROUP * before + bases[q], 0.0), axis=0, keepdims=True)
            for q in range(Q)
        ],
        axis=0,
    ).astype(jnp.int32)

    g_iota = iota((GMAX, 128), 0)
    c_iota = iota((GROUP, 128), 0)
    named = []
    for q in range(Q):
        d = dest[q : q + 1, :]
        onehot[:, 128 * q : 128 * (q + 1)] = (
            ((d >> 3) == g_iota).astype(jnp.float32).astype(jnp.bfloat16)
        )
        here = ((d & 7) == c_iota) & valid[q : q + 1, :]
        named.append(jnp.where(here, query[q : q + 1, :], 0).astype(jnp.float32))
    lists = dot(
        jnp.concatenate(named, axis=1).astype(jnp.bfloat16), onehot[...], ((1,), (1,))
    )
    plan[0:GROUP, 0:GMAX] = lists.astype(jnp.int32)
    g_lane = iota((BLK, 256), 1)
    ends2 = jnp.concatenate([ends, ends], axis=1)
    owner_block = jnp.minimum(
        jnp.sum((ends2 <= g_lane).astype(jnp.int32), axis=0, keepdims=True), BLK - 1
    )
    total = jnp.broadcast_to(ends2[BLK - 1 : BLK, :], (1, 256))
    plan[GROUP : 2 * GROUP, :] = jnp.where(
        iota((GROUP, 256), 0) == 0,
        jnp.broadcast_to(owner_block, (GROUP, 256)),
        jnp.broadcast_to(total, (GROUP, 256)),
    )
    copy = pltpu.make_async_copy(plan, plan_s, sem)
    copy.start()
    best[...] = jnp.zeros((GMAX, GROUP * T), jnp.float32)
    copy.wait()
    len_copy.wait()
    p_copy.wait()
    same_copy.wait()
    other_copy.wait()

    token = iota((PT, GROUP * T), 0)

    def step(it, carry):
        rows = []
        for u in range(UNROLL):
            g = it * UNROLL + u
            b = plan_s[GROUP, g]
            rows_q = jnp.concatenate([q_ref[plan_s[c, g]] for c in range(GROUP)], axis=0)
            similar = dot(p_ref[b], rows_q, ((1,), (1,)))
            similar = jnp.where(token < len_ref[b], similar, -jnp.inf)
            rows.append(jnp.max(similar, axis=0, keepdims=True))
        best[pl.ds(pl.multiple_of(it * UNROLL, UNROLL), UNROLL), :] = jnp.concatenate(rows, axis=0)
        return carry

    lax.fori_loop(0, (plan_s[GROUP + 1, 0] + (UNROLL - 1)) // UNROLL, step, 0)

    w = (iota((GROUP, GROUP * T), 0) == (iota((GROUP, GROUP * T), 1) >> 5)).astype(jnp.float32)
    w = w.astype(jnp.bfloat16)
    means = sum(dot(w, part, ((1,), (1,))) for part in split3(best[...])) * (1.0 / T)
    picked = dot(jnp.concatenate(split3(means), axis=0), onehot[...], ((1,), (0,)))
    picked = picked[0:GROUP] + picked[GROUP : 2 * GROUP] + picked[2 * GROUP : 3 * GROUP]
    out = []
    for q in range(Q):
        here = (dest[q : q + 1, :] & 7) == c_iota
        out.append(
            jnp.sum(jnp.where(here, picked[:, 128 * q : 128 * (q + 1)], 0.0), axis=0, keepdims=True)
        )
    out = jnp.concatenate(out, axis=0)
    o_ref[0:8, :] = out
    o_ref[8:16, :] = pltpu.roll(out, 64, 1)


def place_kernel(cand_ref, key_ref, x_ref, o_ref):
    cand = jnp.concatenate([cand_ref[...], jnp.zeros((CL, 128 - QL), jnp.int32)], axis=1)
    lane = iota((1, 128), 1)
    turned = [cand] + [pltpu.roll(cand, 32 * i, 1) for i in range(1, 4)]
    segs = []
    for t in range(4):
        seg = turned[0][4 * t : 4 * t + 1, :]
        for i in range(1, 4):
            seg = jnp.where(lane >> 5 == i, turned[i][4 * t + i : 4 * t + i + 1, :], seg)
        segs.append(seg)
    asked = jnp.concatenate(segs, axis=1)
    place = iota((1, QL * CL), 1)
    own_key = ((place & 31) << 10) + ((place >> 5) << 6) + (asked & 63)
    owner = asked >> 6
    lane_z = iota((Z, 128), 1)
    x = jnp.where(lane_z < 2 * YQ, x_ref[...], 0.0)
    key = jnp.where(lane_z < YQ, key_ref[...], 0)
    key_high = pltpu.roll(key >> 8, 2 * YQ, 1).astype(jnp.float32)
    key_low = pltpu.roll(key & 255, 3 * YQ, 1).astype(jnp.float32)
    high, mid, low = split3(x)
    high = jnp.where(
        lane_z < 2 * YQ,
        high.astype(jnp.float32),
        jnp.where(lane_z < 3 * YQ, key_high, key_low),
    ).astype(jnp.bfloat16)
    tables = jnp.concatenate([high, mid, low], axis=1)
    on_z = ((owner >> 5) == iota((Z, QL * CL), 0)).astype(jnp.float32).astype(jnp.bfloat16)
    found = dot(tables, on_z, ((0,), (0,)))
    on_yq = (owner & 31) == iota((YQ, QL * CL), 0)

    def pick(rows):
        return jnp.sum(jnp.where(on_yq, rows, 0.0), axis=0, keepdims=True)

    score = found[0 : 2 * YQ] + found[128 : 128 + 2 * YQ] + found[256 : 256 + 2 * YQ]
    first = pick(found[2 * YQ : 3 * YQ] * 256.0 + found[3 * YQ : 4 * YQ])
    out = jnp.where(
        first.astype(jnp.int32) == own_key, pick(score[0:YQ]), pick(score[YQ : 2 * YQ])
    )
    row = iota((CL, 128), 0)
    res = jnp.zeros((CL, 128), jnp.float32)
    for i in range(4):
        for t in range(4):
            seg = jnp.broadcast_to(out[:, 128 * t : 128 * (t + 1)], (CL, 128))
            seg = pltpu.roll(seg, 128 - 32 * i, 1) if i else seg
            res = jnp.where(row == 4 * t + i, seg, res)
    o_ref[...] = res[:, :QL]


VMEM = pl.BlockSpec(memory_space=pltpu.VMEM)


def small_call(kernel, out_shape, *args, hint=None):
    return pl.pallas_call(
        kernel,
        cost_estimate=hint,
        out_shape=out_shape,
        in_specs=[VMEM] * len(args),
        out_specs=jax.tree.map(lambda _: VMEM, out_shape),
    )(*[pltpu.with_memory_space_constraint(a, pltpu.VMEM) for a in args])


def shards(queries, passages, lengths, candidates):
    same = [queries] + [
        lax.ppermute(queries, "query", [(k, (k + 2 * d) % Q) for k in range(Q)])
        for d in range(1, Q // 2)
    ]
    cand = candidates.T
    table, keys = small_call(
        request_kernel,
        (pltpu.VMEM((YQ, 128), jnp.int32), pltpu.VMEM((Z, 128), jnp.int32)),
        cand,
    )
    got = exchange(table, YQ_GROUPS)
    hint = pl.CostEstimate(flops=10**11, transcendentals=0, bytes_accessed=2**20)
    got = small_call(by_z_kernel, pltpu.VMEM((Z, 128), jnp.int32), got, hint=hint)
    codes = exchange(got, Z_GROUPS)
    same = jnp.concatenate(same, axis=0)
    codes, same = lax.optimization_barrier((codes, same))
    other = lax.ppermute(same, "query", [(k, k ^ 1) for k in range(Q)])
    hbm = pl.BlockSpec(memory_space=pltpu.HBM)
    scores = pl.pallas_call(
        score_kernel,
        out_shape=pltpu.VMEM((Z, 128), jnp.float32),
        in_specs=[hbm, VMEM, VMEM, VMEM, hbm],
        out_specs=VMEM,
        scratch_shapes=[
            pltpu.SMEM((BLK,), jnp.int32),
            pltpu.VMEM((NQ, T, D), jnp.bfloat16),
            pltpu.VMEM((BLK, PT, D), jnp.bfloat16),
            pltpu.VMEM((2 * GROUP, 256), jnp.int32),
            pltpu.SMEM((2 * GROUP, 256), jnp.int32),
            pltpu.VMEM((GMAX, Q * 128), jnp.bfloat16),
            pltpu.VMEM((GMAX, GROUP * T), jnp.float32),
            pltpu.SemaphoreType.DMA,
            pltpu.SemaphoreType.DMA,
            pltpu.SemaphoreType.DMA,
            pltpu.SemaphoreType.DMA,
            pltpu.SemaphoreType.DMA,
        ],
        compiler_params=pltpu.CompilerParams(vmem_limit_bytes=32 << 20),
    )(
        pltpu.with_memory_space_constraint(lengths, pltpu.HBM),
        pltpu.with_memory_space_constraint(codes, pltpu.VMEM),
        pltpu.with_memory_space_constraint(same, pltpu.VMEM),
        pltpu.with_memory_space_constraint(other, pltpu.VMEM),
        pltpu.with_memory_space_constraint(passages, pltpu.HBM),
    )
    back = small_call(by_plane_kernel, pltpu.VMEM((YQ, 128), jnp.float32), scores)
    back = exchange(back, YQ_GROUPS)
    back = small_call(by_z_kernel, pltpu.VMEM((Z, 128), jnp.float32), back)
    back = exchange(back, Z_GROUPS)
    out = small_call(
        place_kernel, jax.ShapeDtypeStruct((CL, QL), jnp.float32), cand, keys, back
    )
    return out.T


def solution(mesh):
    in_specs = (
        P("query", None, None),
        P(("index", "query"), None, None),
        P(("index", "query")),
        P("query", "index"),
    )
    return jax.shard_map(
        shards, mesh=mesh, in_specs=in_specs, out_specs=P("query", "index"), check_vma=False
    )
```

```python
import jax
import jax.numpy as jnp
from jax import lax
from jax.experimental import pallas as pl
from jax.experimental.pallas import tpu as pltpu
from jax.sharding import PartitionSpec as P

Z, Y, Q = 16, 4, 8
YQ = Y * Q
OWNERS = Z * YQ
BLK = 64
QL, CL = 32, 16
NQ = Q * QL
T, D, PT = 32, 128, 128
GROUP = 8
GMAX = 192
UNROLL = 32
BIG = 1 << 30

Z_GROUPS = [[r + YQ * z for z in range(Z)] for r in range(YQ)]
YQ_GROUPS = [[YQ * z + r for r in range(YQ)] for z in range(Z)]


def iota(shape, axis):
    return lax.broadcasted_iota(jnp.int32, shape, axis)


def exchange(x, groups):
    return lax.all_to_all(
        x, ("index", "query"), split_axis=0, concat_axis=0, tiled=True,
        axis_index_groups=groups,
    )


def spread(rows, row, lane):
    out = jnp.zeros((Z, 128), jnp.int32)
    for k, slot in enumerate(rows):
        for j in range(4):
            shift = (32 * k - 32 * j) % 128
            for t in range(4):
                seg = jnp.broadcast_to(slot[:, 128 * t : 128 * (t + 1)], (Z, 128))
                seg = pltpu.roll(seg, shift, 1) if shift else seg
                out = jnp.where((row == 4 * t + j) & (lane >> 5 == k), seg, out)
    return out


def by_plane(x):
    xt = jnp.transpose(jnp.concatenate([x, jnp.zeros((112, 128), x.dtype)], axis=0))
    lane = iota((YQ, 128), 1)
    return jnp.where(lane < Z, xt[:YQ], pltpu.roll(xt[YQ : 2 * YQ], Z, 1))


def by_z(x):
    xt = jnp.transpose(jnp.concatenate([x, jnp.zeros((96, 128), x.dtype)], axis=0))
    lane = iota((Z, 128), 1)
    return jnp.where(lane < YQ, xt[:Z], pltpu.roll(xt[Z : 2 * Z], YQ, 1))


def by_plane_kernel(x_ref, o_ref):
    o_ref[...] = by_plane(x_ref[...])


def by_z_kernel(x_ref, o_ref):
    o_ref[...] = by_z(x_ref[...])


def request_kernel(cand_ref, code_ref, key_ref):
    cand = cand_ref[...]
    lane_owner = iota((CL, OWNERS), 1)
    sub = iota((CL, 1), 0)
    low = jnp.full((CL, OWNERS), BIG, jnp.int32)
    high = jnp.full((CL, OWNERS), -1, jnp.int32)
    for q in range(QL):
        col = cand[:, q : q + 1]
        key = (q << 10) + (sub << 6) + (col & 63)
        match = (col >> 6) == lane_owner
        low = jnp.minimum(low, jnp.where(match, key, BIG))
        high = jnp.maximum(high, jnp.where(match, key, -1))
    last = jnp.max(high, axis=0, keepdims=True)
    first = jnp.where(last >= 0, jnp.min(low, axis=0, keepdims=True), -1)
    last = jnp.where(last != first, last, -1)
    row = iota((Z, 128), 0)
    lane = iota((Z, 128), 1)
    key = spread((first, last), row, lane)
    key_ref[...] = key
    code = jnp.where((key >= 0) & (lane < 2 * YQ), ((key >> 10) << 6) + (key & 63), -1)
    code_ref[...] = by_plane(code)


def split3(x):
    hi = x.astype(jnp.bfloat16)
    rest = x - hi.astype(jnp.float32)
    mid = rest.astype(jnp.bfloat16)
    low = (rest - mid.astype(jnp.float32)).astype(jnp.bfloat16)
    return hi, mid, low


def dot(a, b, dims):
    return lax.dot_general(a, b, (dims, ((), ())), preferred_element_type=jnp.float32)


def sort_kernel(code_ref, p_hbm, plan_ref, dest_ref, p_ref, p_sem):
    p_copy = pltpu.make_async_copy(p_hbm, p_ref, p_sem)
    p_copy.start()
    lane8 = iota((Q, 128), 1)
    code = jnp.where(lane8 < 64, code_ref[0:8, :], pltpu.roll(code_ref[8:16, :], 64, 1))
    valid = code >= 0
    block = jnp.where(valid, code & 63, BLK)
    me = lax.axis_index("query")
    source = lane8 & (Q - 1)
    piece = (((source ^ me) & 1) << 2) + (((me >> 1) - (source >> 1)) & 3)
    query = jnp.where(valid, (code >> 6) + QL * piece, 0)

    b_iota = iota((BLK, 128), 0)
    hits = [block[q : q + 1, :] == b_iota for q in range(Q)]
    hit = jnp.concatenate([h.astype(jnp.float32) for h in hits], axis=0).astype(jnp.bfloat16)
    r_i, c_i = iota((128, 128), 0), iota((128, 128), 1)
    earlier = jnp.concatenate(
        [(r_i < c_i).astype(jnp.float32), jnp.ones((128, 128), jnp.float32)], axis=1
    ).astype(jnp.bfloat16)
    sums = dot(hit, earlier, ((1,), (0,)))
    base = jnp.zeros((BLK, 128), jnp.float32)
    bases = []
    for q in range(Q):
        bases.append(base + sums[BLK * q : BLK * (q + 1), :128])
        base = base + sums[BLK * q : BLK * (q + 1), 128:]
    groups = ((base.astype(jnp.int32) + (GROUP - 1)) >> 3).astype(jnp.float32)
    l_i, m_i = iota((BLK, BLK), 0), iota((BLK, BLK), 1)
    before = dot(
        (m_i < l_i).astype(jnp.float32).astype(jnp.bfloat16),
        groups.astype(jnp.bfloat16),
        ((1,), (0,)),
    )
    ends = (before + groups).astype(jnp.int32)
    dest = jnp.concatenate(
        [
            jnp.sum(jnp.where(hits[q], GROUP * before + bases[q], 0.0), axis=0, keepdims=True)
            for q in range(Q)
        ],
        axis=0,
    ).astype(jnp.int32)

    dest_ref[...] = dest
    c_iota = iota((GROUP, 128), 0)
    named = []
    for q in range(Q):
        here = ((dest[q : q + 1, :] & 7) == c_iota) & valid[q : q + 1, :]
        named.append(jnp.where(here, query[q : q + 1, :], 0).astype(jnp.float32))
    lists = dot(
        jnp.concatenate(named, axis=1).astype(jnp.bfloat16), in_group(dest), ((1,), (1,))
    )
    plan_ref[0:GROUP, 0:GMAX] = lists.astype(jnp.int32)
    plan_ref[0:GROUP, GMAX:256] = jnp.zeros((GROUP, 256 - GMAX), jnp.int32)
    g_lane = iota((BLK, 256), 1)
    ends2 = jnp.concatenate([ends, ends], axis=1)
    owner_block = jnp.minimum(
        jnp.sum((ends2 <= g_lane).astype(jnp.int32), axis=0, keepdims=True), BLK - 1
    )
    total = jnp.broadcast_to(ends2[BLK - 1 : BLK, :], (1, 256))
    plan_ref[GROUP : 2 * GROUP, :] = jnp.where(
        iota((GROUP, 256), 0) == 0,
        jnp.broadcast_to(owner_block, (GROUP, 256)),
        jnp.broadcast_to(total, (GROUP, 256)),
    )
    p_copy.wait()


def in_group(dest):
    g_iota = iota((GMAX, 128), 0)
    return jnp.concatenate(
        [((dest[q : q + 1, :] >> 3) == g_iota).astype(jnp.float32) for q in range(Q)], axis=1
    ).astype(jnp.bfloat16)


def score_kernel(
    len_hbm, plan, dest_ref, same_ref, other_ref, p_ref, o_ref, len_ref, plan_s, best, sem, len_sem
):
    len_copy = pltpu.make_async_copy(len_hbm, len_ref, len_sem)
    len_copy.start()
    copy = pltpu.make_async_copy(plan, plan_s, sem)
    copy.start()
    dest = dest_ref[...]
    c_iota = iota((GROUP, 128), 0)
    best[...] = jnp.zeros((GMAX, GROUP * T), jnp.float32)
    copy.wait()
    len_copy.wait()
    half = NQ // 2

    def rows_of(i):
        return jnp.where(i < half, same_ref[i & (half - 1)], other_ref[i & (half - 1)])

    token = iota((PT, GROUP * T), 0)

    def step(it, carry):
        rows = []
        for u in range(UNROLL):
            g = it * UNROLL + u
            b = plan_s[GROUP, g]
            rows_q = jnp.concatenate([rows_of(plan_s[c, g]) for c in range(GROUP)], axis=0)
            similar = dot(p_ref[b], rows_q, ((1,), (1,)))
            similar = jnp.where(token < len_ref[b], similar, -jnp.inf)
            rows.append(jnp.max(similar, axis=0, keepdims=True))
        best[pl.ds(pl.multiple_of(it * UNROLL, UNROLL), UNROLL), :] = jnp.concatenate(rows, axis=0)
        return carry

    lax.fori_loop(0, (plan_s[GROUP + 1, 0] + (UNROLL - 1)) // UNROLL, step, 0)

    w = (iota((GROUP, GROUP * T), 0) == (iota((GROUP, GROUP * T), 1) >> 5)).astype(jnp.float32)
    w = w.astype(jnp.bfloat16)
    means = sum(dot(w, part, ((1,), (1,))) for part in split3(best[...])) * (1.0 / T)
    picked = dot(jnp.concatenate(split3(means), axis=0), in_group(dest), ((1,), (0,)))
    picked = picked[0:GROUP] + picked[GROUP : 2 * GROUP] + picked[2 * GROUP : 3 * GROUP]
    out = []
    for q in range(Q):
        here = (dest[q : q + 1, :] & 7) == c_iota
        out.append(
            jnp.sum(jnp.where(here, picked[:, 128 * q : 128 * (q + 1)], 0.0), axis=0, keepdims=True)
        )
    out = jnp.concatenate(out, axis=0)
    o_ref[0:8, :] = out
    o_ref[8:16, :] = pltpu.roll(out, 64, 1)


def place_kernel(cand_ref, key_ref, x_ref, o_ref):
    cand = jnp.concatenate([cand_ref[...], jnp.zeros((CL, 128 - QL), jnp.int32)], axis=1)
    lane = iota((1, 128), 1)
    turned = [cand] + [pltpu.roll(cand, 32 * i, 1) for i in range(1, 4)]
    segs = []
    for t in range(4):
        seg = turned[0][4 * t : 4 * t + 1, :]
        for i in range(1, 4):
            seg = jnp.where(lane >> 5 == i, turned[i][4 * t + i : 4 * t + i + 1, :], seg)
        segs.append(seg)
    asked = jnp.concatenate(segs, axis=1)
    place = iota((1, QL * CL), 1)
    own_key = ((place & 31) << 10) + ((place >> 5) << 6) + (asked & 63)
    owner = asked >> 6
    lane_z = iota((Z, 128), 1)
    x = jnp.where(lane_z < 2 * YQ, x_ref[...], 0.0)
    key = jnp.where(lane_z < YQ, key_ref[...], 0)
    key_high = pltpu.roll(key >> 8, 2 * YQ, 1).astype(jnp.float32)
    key_low = pltpu.roll(key & 255, 3 * YQ, 1).astype(jnp.float32)
    high, mid, low = split3(x)
    high = jnp.where(
        lane_z < 2 * YQ,
        high.astype(jnp.float32),
        jnp.where(lane_z < 3 * YQ, key_high, key_low),
    ).astype(jnp.bfloat16)
    tables = jnp.concatenate([high, mid, low], axis=1)
    on_z = ((owner >> 5) == iota((Z, QL * CL), 0)).astype(jnp.float32).astype(jnp.bfloat16)
    found = dot(tables, on_z, ((0,), (0,)))
    on_yq = (owner & 31) == iota((YQ, QL * CL), 0)

    def pick(rows):
        return jnp.sum(jnp.where(on_yq, rows, 0.0), axis=0, keepdims=True)

    score = found[0 : 2 * YQ] + found[128 : 128 + 2 * YQ] + found[256 : 256 + 2 * YQ]
    first = pick(found[2 * YQ : 3 * YQ] * 256.0 + found[3 * YQ : 4 * YQ])
    out = jnp.where(
        first.astype(jnp.int32) == own_key, pick(score[0:YQ]), pick(score[YQ : 2 * YQ])
    )
    row = iota((CL, 128), 0)
    res = jnp.zeros((CL, 128), jnp.float32)
    for i in range(4):
        for t in range(4):
            seg = jnp.broadcast_to(out[:, 128 * t : 128 * (t + 1)], (CL, 128))
            seg = pltpu.roll(seg, 128 - 32 * i, 1) if i else seg
            res = jnp.where(row == 4 * t + i, seg, res)
    o_ref[...] = res[:, :QL]


VMEM = pl.BlockSpec(memory_space=pltpu.VMEM)


def small_call(kernel, out_shape, *args, hint=None):
    return pl.pallas_call(
        kernel,
        cost_estimate=hint,
        out_shape=out_shape,
        in_specs=[VMEM] * len(args),
        out_specs=jax.tree.map(lambda _: VMEM, out_shape),
    )(*[pltpu.with_memory_space_constraint(a, pltpu.VMEM) for a in args])


def shards(queries, passages, lengths, candidates):
    same = [queries] + [
        lax.ppermute(queries, "query", [(k, (k + 2 * d) % Q) for k in range(Q)])
        for d in range(1, Q // 2)
    ]
    cand = candidates.T
    table, keys = small_call(
        request_kernel,
        (pltpu.VMEM((YQ, 128), jnp.int32), pltpu.VMEM((Z, 128), jnp.int32)),
        cand,
    )
    got = exchange(table, YQ_GROUPS)
    hint = pl.CostEstimate(flops=10**11, transcendentals=0, bytes_accessed=2**20)
    got = small_call(by_z_kernel, pltpu.VMEM((Z, 128), jnp.int32), got, hint=hint)
    codes = exchange(got, Z_GROUPS)
    _, *same = lax.optimization_barrier((got, *same))
    same = jnp.concatenate(same, axis=0)
    other = lax.ppermute(same, "query", [(k, k ^ 1) for k in range(Q)])
    at = pltpu.with_memory_space_constraint
    hbm = pl.BlockSpec(memory_space=pltpu.HBM)
    plan, dest, blocks = pl.pallas_call(
        sort_kernel,
        out_shape=(
            pltpu.VMEM((2 * GROUP, 256), jnp.int32),
            pltpu.VMEM((Q, 128), jnp.int32),
            pltpu.VMEM(passages.shape, passages.dtype),
        ),
        in_specs=[VMEM, hbm],
        out_specs=(VMEM, VMEM, VMEM),
        scratch_shapes=[pltpu.SemaphoreType.DMA],
        cost_estimate=pl.CostEstimate(flops=10**11, transcendentals=0, bytes_accessed=2**22),
        compiler_params=pltpu.CompilerParams(vmem_limit_bytes=32 << 20),
    )(at(codes, pltpu.VMEM), at(passages, pltpu.HBM))
    scores = pl.pallas_call(
        score_kernel,
        out_shape=pltpu.VMEM((Z, 128), jnp.float32),
        in_specs=[hbm] + [VMEM] * 5,
        out_specs=VMEM,
        scratch_shapes=[
            pltpu.SMEM((BLK,), jnp.int32),
            pltpu.SMEM((2 * GROUP, 256), jnp.int32),
            pltpu.VMEM((GMAX, GROUP * T), jnp.float32),
            pltpu.SemaphoreType.DMA,
            pltpu.SemaphoreType.DMA,
        ],
        compiler_params=pltpu.CompilerParams(vmem_limit_bytes=32 << 20),
    )(
        at(lengths, pltpu.HBM),
        *[at(x, pltpu.VMEM) for x in (plan, dest, same, other, blocks)],
    )
    back = small_call(by_plane_kernel, pltpu.VMEM((YQ, 128), jnp.float32), scores)
    back = exchange(back, YQ_GROUPS)
    back = small_call(by_z_kernel, pltpu.VMEM((Z, 128), jnp.float32), back)
    back = exchange(back, Z_GROUPS)
    out = small_call(
        place_kernel, jax.ShapeDtypeStruct((CL, QL), jnp.float32), cand, keys, back
    )
    return out.T


def solution(mesh):
    in_specs = (
        P("query", None, None),
        P(("index", "query"), None, None),
        P(("index", "query")),
        P("query", "index"),
    )
    return jax.shard_map(
        shards, mesh=mesh, in_specs=in_specs, out_specs=P("query", "index"), check_vma=False
    )
```

```python
import jax
import jax.numpy as jnp
from jax import lax
from jax.experimental import pallas as pl
from jax.experimental.pallas import tpu as pltpu
from jax.sharding import PartitionSpec as P

Z, Y, Q = 16, 4, 8
YQ = Y * Q
OWNERS = Z * YQ
BLK = 64
QL, CL = 32, 16
NQ = Q * QL
T, D, PT = 32, 128, 128
GROUP = 8
GMAX = 192
UNROLL = 32
BIG = 1 << 30

Z_GROUPS = [[r + YQ * z for z in range(Z)] for r in range(YQ)]
YQ_GROUPS = [[YQ * z + r for r in range(YQ)] for z in range(Z)]


def iota(shape, axis):
    return lax.broadcasted_iota(jnp.int32, shape, axis)


def exchange(x, groups):
    return lax.all_to_all(
        x, ("index", "query"), split_axis=0, concat_axis=0, tiled=True,
        axis_index_groups=groups,
    )


def spread(rows, row, lane):
    out = jnp.zeros((Z, 128), jnp.int32)
    for k, slot in enumerate(rows):
        for j in range(4):
            shift = (32 * k - 32 * j) % 128
            for t in range(4):
                seg = jnp.broadcast_to(slot[:, 128 * t : 128 * (t + 1)], (Z, 128))
                seg = pltpu.roll(seg, shift, 1) if shift else seg
                out = jnp.where((row == 4 * t + j) & (lane >> 5 == k), seg, out)
    return out


def by_plane(x):
    xt = jnp.transpose(jnp.concatenate([x, jnp.zeros((112, 128), x.dtype)], axis=0))
    lane = iota((YQ, 128), 1)
    return jnp.where(lane < Z, xt[:YQ], pltpu.roll(xt[YQ : 2 * YQ], Z, 1))


def by_z(x):
    xt = jnp.transpose(jnp.concatenate([x, jnp.zeros((96, 128), x.dtype)], axis=0))
    lane = iota((Z, 128), 1)
    return jnp.where(lane < YQ, xt[:Z], pltpu.roll(xt[Z : 2 * Z], YQ, 1))


def by_plane_kernel(x_ref, o_ref):
    o_ref[...] = by_plane(x_ref[...])


def by_z_kernel(x_ref, o_ref):
    o_ref[...] = by_z(x_ref[...])


def request_kernel(cand_ref, code_ref, key_ref):
    cand = cand_ref[...]
    lane_owner = iota((CL, OWNERS), 1)
    sub = iota((CL, 1), 0)
    low = jnp.full((CL, OWNERS), BIG, jnp.int32)
    high = jnp.full((CL, OWNERS), -1, jnp.int32)
    for q in range(QL):
        col = cand[:, q : q + 1]
        key = (q << 10) + (sub << 6) + (col & 63)
        match = (col >> 6) == lane_owner
        low = jnp.minimum(low, jnp.where(match, key, BIG))
        high = jnp.maximum(high, jnp.where(match, key, -1))
    last = jnp.max(high, axis=0, keepdims=True)
    first = jnp.where(last >= 0, jnp.min(low, axis=0, keepdims=True), -1)
    last = jnp.where(last != first, last, -1)
    row = iota((Z, 128), 0)
    lane = iota((Z, 128), 1)
    key = spread((first, last), row, lane)
    key_ref[...] = key
    code = jnp.where((key >= 0) & (lane < 2 * YQ), ((key >> 10) << 6) + (key & 63), -1)
    code_ref[...] = by_plane(code)


def split3(x):
    hi = x.astype(jnp.bfloat16)
    rest = x - hi.astype(jnp.float32)
    mid = rest.astype(jnp.bfloat16)
    low = (rest - mid.astype(jnp.float32)).astype(jnp.bfloat16)
    return hi, mid, low


def dot(a, b, dims):
    return lax.dot_general(a, b, (dims, ((), ())), preferred_element_type=jnp.float32)


def sort_kernel(
    code_ref, p_hbm, same_ref, plan_ref, dest_ref, onehot_ref, p_ref, q_ref, p_sem, q_sem
):
    q_copy = pltpu.make_async_copy(same_ref, q_ref.at[pl.ds(0, NQ // 2)], q_sem)
    q_copy.start()
    p_copy = pltpu.make_async_copy(p_hbm, p_ref, p_sem)
    p_copy.start()
    lane8 = iota((Q, 128), 1)
    code = jnp.where(lane8 < 64, code_ref[0:8, :], pltpu.roll(code_ref[8:16, :], 64, 1))
    valid = code >= 0
    block = jnp.where(valid, code & 63, BLK)
    me = lax.axis_index("query")
    source = lane8 & (Q - 1)
    piece = (((source ^ me) & 1) << 2) + (((me >> 1) - (source >> 1)) & 3)
    query = jnp.where(valid, (code >> 6) + QL * piece, 0)

    b_iota = iota((BLK, 128), 0)
    hits = [block[q : q + 1, :] == b_iota for q in range(Q)]
    hit = jnp.concatenate([h.astype(jnp.float32) for h in hits], axis=0).astype(jnp.bfloat16)
    r_i, c_i = iota((128, 128), 0), iota((128, 128), 1)
    earlier = jnp.concatenate(
        [(r_i < c_i).astype(jnp.float32), jnp.ones((128, 128), jnp.float32)], axis=1
    ).astype(jnp.bfloat16)
    sums = dot(hit, earlier, ((1,), (0,)))
    base = jnp.zeros((BLK, 128), jnp.float32)
    bases = []
    for q in range(Q):
        bases.append(base + sums[BLK * q : BLK * (q + 1), :128])
        base = base + sums[BLK * q : BLK * (q + 1), 128:]
    groups = ((base.astype(jnp.int32) + (GROUP - 1)) >> 3).astype(jnp.float32)
    l_i, m_i = iota((BLK, BLK), 0), iota((BLK, BLK), 1)
    before = dot(
        (m_i < l_i).astype(jnp.float32).astype(jnp.bfloat16),
        groups.astype(jnp.bfloat16),
        ((1,), (0,)),
    )
    ends = (before + groups).astype(jnp.int32)
    dest = jnp.concatenate(
        [
            jnp.sum(jnp.where(hits[q], GROUP * before + bases[q], 0.0), axis=0, keepdims=True)
            for q in range(Q)
        ],
        axis=0,
    ).astype(jnp.int32)

    dest_ref[...] = dest
    c_iota = iota((GROUP, 128), 0)
    named = []
    for q in range(Q):
        here = ((dest[q : q + 1, :] & 7) == c_iota) & valid[q : q + 1, :]
        named.append(jnp.where(here, query[q : q + 1, :], 0).astype(jnp.float32))
    onehot = in_group(dest)
    onehot_ref[...] = onehot
    lists = dot(
        jnp.concatenate(named, axis=1).astype(jnp.bfloat16), onehot, ((1,), (1,))
    )
    plan_ref[0:GROUP, 0:GMAX] = lists.astype(jnp.int32)
    plan_ref[0:GROUP, GMAX:256] = jnp.zeros((GROUP, 256 - GMAX), jnp.int32)
    g_lane = iota((BLK, 256), 1)
    ends2 = jnp.concatenate([ends, ends], axis=1)
    owner_block = jnp.minimum(
        jnp.sum((ends2 <= g_lane).astype(jnp.int32), axis=0, keepdims=True), BLK - 1
    )
    total = jnp.broadcast_to(ends2[BLK - 1 : BLK, :], (1, 256))
    plan_ref[GROUP : 2 * GROUP, :] = jnp.where(
        iota((GROUP, 256), 0) == 0,
        jnp.broadcast_to(owner_block, (GROUP, 256)),
        jnp.broadcast_to(total, (GROUP, 256)),
    )
    p_copy.wait()
    q_copy.wait()


def in_group(dest):
    g_iota = iota((GMAX, 128), 0)
    return jnp.concatenate(
        [((dest[q : q + 1, :] >> 3) == g_iota).astype(jnp.float32) for q in range(Q)], axis=1
    ).astype(jnp.bfloat16)


def score_kernel(
    len_hbm, plan, dest_ref, onehot_ref, other_ref, p_ref, _, o_ref, q_ref,
    len_ref, plan_s, best, sem, len_sem, q_sem,
):
    half = NQ // 2
    q_copy = pltpu.make_async_copy(other_ref, q_ref.at[pl.ds(half, half)], q_sem)
    q_copy.start()
    len_copy = pltpu.make_async_copy(len_hbm, len_ref, len_sem)
    len_copy.start()
    copy = pltpu.make_async_copy(plan, plan_s, sem)
    copy.start()
    dest = dest_ref[...]
    c_iota = iota((GROUP, 128), 0)
    best[...] = jnp.zeros((GMAX, GROUP * T), jnp.float32)
    copy.wait()
    len_copy.wait()
    q_copy.wait()

    token = iota((PT, GROUP * T), 0)

    def step(it, carry):
        rows = []
        for u in range(UNROLL):
            g = it * UNROLL + u
            b = plan_s[GROUP, g]
            rows_q = jnp.concatenate([q_ref[plan_s[c, g]] for c in range(GROUP)], axis=0)
            similar = dot(p_ref[b], rows_q, ((1,), (1,)))
            similar = jnp.where(token < len_ref[b], similar, -jnp.inf)
            rows.append(jnp.max(similar, axis=0, keepdims=True))
        best[pl.ds(pl.multiple_of(it * UNROLL, UNROLL), UNROLL), :] = jnp.concatenate(rows, axis=0)
        return carry

    lax.fori_loop(0, (plan_s[GROUP + 1, 0] + (UNROLL - 1)) // UNROLL, step, 0)

    w = (iota((GROUP, GROUP * T), 0) == (iota((GROUP, GROUP * T), 1) >> 5)).astype(jnp.float32)
    w = w.astype(jnp.bfloat16)
    means = sum(dot(w, part, ((1,), (1,))) for part in split3(best[...])) * (1.0 / T)
    picked = dot(jnp.concatenate(split3(means), axis=0), onehot_ref[...], ((1,), (0,)))
    picked = picked[0:GROUP] + picked[GROUP : 2 * GROUP] + picked[2 * GROUP : 3 * GROUP]
    out = []
    for q in range(Q):
        here = (dest[q : q + 1, :] & 7) == c_iota
        out.append(
            jnp.sum(jnp.where(here, picked[:, 128 * q : 128 * (q + 1)], 0.0), axis=0, keepdims=True)
        )
    out = jnp.concatenate(out, axis=0)
    o_ref[0:8, :] = out
    o_ref[8:16, :] = pltpu.roll(out, 64, 1)


def place_kernel(cand_ref, key_ref, x_ref, o_ref):
    cand = jnp.concatenate([cand_ref[...], jnp.zeros((CL, 128 - QL), jnp.int32)], axis=1)
    lane = iota((1, 128), 1)
    turned = [cand] + [pltpu.roll(cand, 32 * i, 1) for i in range(1, 4)]
    segs = []
    for t in range(4):
        seg = turned[0][4 * t : 4 * t + 1, :]
        for i in range(1, 4):
            seg = jnp.where(lane >> 5 == i, turned[i][4 * t + i : 4 * t + i + 1, :], seg)
        segs.append(seg)
    asked = jnp.concatenate(segs, axis=1)
    place = iota((1, QL * CL), 1)
    own_key = ((place & 31) << 10) + ((place >> 5) << 6) + (asked & 63)
    owner = asked >> 6
    lane_z = iota((Z, 128), 1)
    x = jnp.where(lane_z < 2 * YQ, x_ref[...], 0.0)
    key = jnp.where(lane_z < YQ, key_ref[...], 0)
    key_high = pltpu.roll(key >> 8, 2 * YQ, 1).astype(jnp.float32)
    key_low = pltpu.roll(key & 255, 3 * YQ, 1).astype(jnp.float32)
    high, mid, low = split3(x)
    high = jnp.where(
        lane_z < 2 * YQ,
        high.astype(jnp.float32),
        jnp.where(lane_z < 3 * YQ, key_high, key_low),
    ).astype(jnp.bfloat16)
    tables = jnp.concatenate([high, mid, low], axis=1)
    on_z = ((owner >> 5) == iota((Z, QL * CL), 0)).astype(jnp.float32).astype(jnp.bfloat16)
    found = dot(tables, on_z, ((0,), (0,)))
    on_yq = (owner & 31) == iota((YQ, QL * CL), 0)

    def pick(rows):
        return jnp.sum(jnp.where(on_yq, rows, 0.0), axis=0, keepdims=True)

    score = found[0 : 2 * YQ] + found[128 : 128 + 2 * YQ] + found[256 : 256 + 2 * YQ]
    first = pick(found[2 * YQ : 3 * YQ] * 256.0 + found[3 * YQ : 4 * YQ])
    out = jnp.where(
        first.astype(jnp.int32) == own_key, pick(score[0:YQ]), pick(score[YQ : 2 * YQ])
    )
    row = iota((CL, 128), 0)
    res = jnp.zeros((CL, 128), jnp.float32)
    for i in range(4):
        for t in range(4):
            seg = jnp.broadcast_to(out[:, 128 * t : 128 * (t + 1)], (CL, 128))
            seg = pltpu.roll(seg, 128 - 32 * i, 1) if i else seg
            res = jnp.where(row == 4 * t + i, seg, res)
    o_ref[...] = res[:, :QL]


VMEM = pl.BlockSpec(memory_space=pltpu.VMEM)


def small_call(kernel, out_shape, *args, hint=None):
    return pl.pallas_call(
        kernel,
        cost_estimate=hint,
        out_shape=out_shape,
        in_specs=[VMEM] * len(args),
        out_specs=jax.tree.map(lambda _: VMEM, out_shape),
    )(*[pltpu.with_memory_space_constraint(a, pltpu.VMEM) for a in args])


def shards(queries, passages, lengths, candidates):
    same = [queries] + [
        lax.ppermute(queries, "query", [(k, (k + 2 * d) % Q) for k in range(Q)])
        for d in range(1, Q // 2)
    ]
    cand = candidates.T
    table, keys = small_call(
        request_kernel,
        (pltpu.VMEM((YQ, 128), jnp.int32), pltpu.VMEM((Z, 128), jnp.int32)),
        cand,
    )
    got = exchange(table, YQ_GROUPS)
    hint = pl.CostEstimate(flops=10**11, transcendentals=0, bytes_accessed=2**20)
    got = small_call(by_z_kernel, pltpu.VMEM((Z, 128), jnp.int32), got, hint=hint)
    codes = exchange(got, Z_GROUPS)
    _, *same = lax.optimization_barrier((got, *same))
    same = jnp.concatenate(same, axis=0)
    other = lax.ppermute(same, "query", [(k, k ^ 1) for k in range(Q)])
    at = pltpu.with_memory_space_constraint
    hbm = pl.BlockSpec(memory_space=pltpu.HBM)
    every = pltpu.VMEM((NQ, T, D), queries.dtype)
    plan, dest, onehot, blocks, gathered = pl.pallas_call(
        sort_kernel,
        out_shape=(
            pltpu.VMEM((2 * GROUP, 256), jnp.int32),
            pltpu.VMEM((Q, 128), jnp.int32),
            pltpu.VMEM((GMAX, Q * 128), jnp.bfloat16),
            pltpu.VMEM(passages.shape, passages.dtype),
            every,
        ),
        in_specs=[VMEM, hbm, VMEM],
        out_specs=(VMEM,) * 5,
        scratch_shapes=[pltpu.SemaphoreType.DMA, pltpu.SemaphoreType.DMA],
        cost_estimate=pl.CostEstimate(flops=10**11, transcendentals=0, bytes_accessed=2**22),
        compiler_params=pltpu.CompilerParams(vmem_limit_bytes=32 << 20),
    )(at(codes, pltpu.VMEM), at(passages, pltpu.HBM), at(same, pltpu.VMEM))
    scores, _ = pl.pallas_call(
        score_kernel,
        out_shape=(pltpu.VMEM((Z, 128), jnp.float32), every),
        in_specs=[hbm] + [VMEM] * 6,
        out_specs=(VMEM, VMEM),
        input_output_aliases={6: 1},
        scratch_shapes=[
            pltpu.SMEM((BLK,), jnp.int32),
            pltpu.SMEM((2 * GROUP, 256), jnp.int32),
            pltpu.VMEM((GMAX, GROUP * T), jnp.float32),
            pltpu.SemaphoreType.DMA,
            pltpu.SemaphoreType.DMA,
            pltpu.SemaphoreType.DMA,
        ],
        compiler_params=pltpu.CompilerParams(vmem_limit_bytes=32 << 20),
    )(
        at(lengths, pltpu.HBM),
        *[at(x, pltpu.VMEM) for x in (plan, dest, onehot, other, blocks, gathered)],
    )
    back = small_call(by_plane_kernel, pltpu.VMEM((YQ, 128), jnp.float32), scores)
    back = exchange(back, YQ_GROUPS)
    back = small_call(by_z_kernel, pltpu.VMEM((Z, 128), jnp.float32), back)
    back = exchange(back, Z_GROUPS)
    out = small_call(
        place_kernel, jax.ShapeDtypeStruct((CL, QL), jnp.float32), cand, keys, back
    )
    return out.T


def solution(mesh):
    in_specs = (
        P("query", None, None),
        P(("index", "query"), None, None),
        P(("index", "query")),
        P("query", "index"),
    )
    return jax.shard_map(
        shards, mesh=mesh, in_specs=in_specs, out_specs=P("query", "index"), check_vma=False
    )
```

```python
import jax
import jax.numpy as jnp
from jax import lax
from jax.experimental import pallas as pl
from jax.experimental.pallas import tpu as pltpu
from jax.sharding import PartitionSpec as P

Z, Y, Q = 16, 4, 8
YQ = Y * Q
OWNERS = Z * YQ
BLK = 64
QL, CL = 32, 16
NQ = Q * QL
T, D, PT = 32, 128, 128
GROUP = 8
GMAX = 192
UNROLL = 32
BIG = 1 << 30

FIRST_Z, FIRST_YQ = Z // 2, (Y // 2) * Q + Q // 2
FIRST = FIRST_Z * YQ + FIRST_YQ
Z_GROUPS = [[r + YQ * (z ^ FIRST_Z) for z in range(Z)] for r in range(YQ)]
YQ_GROUPS = [[YQ * z + (r ^ FIRST_YQ) for r in range(YQ)] for z in range(Z)]


def iota(shape, axis):
    return lax.broadcasted_iota(jnp.int32, shape, axis)


def exchange(x, groups):
    return lax.all_to_all(
        x, ("index", "query"), split_axis=0, concat_axis=0, tiled=True,
        axis_index_groups=groups,
    )


def spread(rows, row, lane):
    out = jnp.zeros((Z, 128), jnp.int32)
    for k, slot in enumerate(rows):
        for j in range(4):
            shift = (32 * k - 32 * j) % 128
            for t in range(4):
                seg = jnp.broadcast_to(slot[:, 128 * t : 128 * (t + 1)], (Z, 128))
                seg = pltpu.roll(seg, shift, 1) if shift else seg
                out = jnp.where((row == 4 * t + j) & (lane >> 5 == k), seg, out)
    return out


def by_plane(x):
    xt = jnp.transpose(jnp.concatenate([x, jnp.zeros((112, 128), x.dtype)], axis=0))
    lane = iota((YQ, 128), 1)
    return jnp.where(lane < Z, xt[:YQ], pltpu.roll(xt[YQ : 2 * YQ], Z, 1))


def by_z(x):
    xt = jnp.transpose(jnp.concatenate([x, jnp.zeros((96, 128), x.dtype)], axis=0))
    lane = iota((Z, 128), 1)
    return jnp.where(lane < YQ, xt[:Z], pltpu.roll(xt[Z : 2 * Z], YQ, 1))


def by_plane_kernel(x_ref, o_ref):
    o_ref[...] = by_plane(x_ref[...])


def by_z_kernel(x_ref, o_ref):
    o_ref[...] = by_z(x_ref[...])


def request_kernel(cand_ref, code_ref, key_ref):
    cand = cand_ref[...]
    lane_owner = iota((CL, OWNERS), 1)
    sub = iota((CL, 1), 0)
    low = jnp.full((CL, OWNERS), BIG, jnp.int32)
    high = jnp.full((CL, OWNERS), -1, jnp.int32)
    for q in range(QL):
        col = cand[:, q : q + 1]
        key = (q << 10) + (sub << 6) + (col & 63)
        match = ((col >> 6) ^ FIRST) == lane_owner
        low = jnp.minimum(low, jnp.where(match, key, BIG))
        high = jnp.maximum(high, jnp.where(match, key, -1))
    last = jnp.max(high, axis=0, keepdims=True)
    first = jnp.where(last >= 0, jnp.min(low, axis=0, keepdims=True), -1)
    last = jnp.where(last != first, last, -1)
    row = iota((Z, 128), 0)
    lane = iota((Z, 128), 1)
    key = spread((first, last), row, lane)
    key_ref[...] = key
    code = jnp.where((key >= 0) & (lane < 2 * YQ), ((key >> 10) << 6) + (key & 63), -1)
    code_ref[...] = by_plane(code)


def split3(x):
    hi = x.astype(jnp.bfloat16)
    rest = x - hi.astype(jnp.float32)
    mid = rest.astype(jnp.bfloat16)
    low = (rest - mid.astype(jnp.float32)).astype(jnp.bfloat16)
    return hi, mid, low


def dot(a, b, dims):
    return lax.dot_general(a, b, (dims, ((), ())), preferred_element_type=jnp.float32)


def sort_kernel(
    code_ref, p_hbm, same_ref, plan_ref, dest_ref, onehot_ref, p_ref, q_ref, p_sem, q_sem
):
    q_copy = pltpu.make_async_copy(same_ref, q_ref.at[pl.ds(0, NQ // 2)], q_sem)
    q_copy.start()
    p_copy = pltpu.make_async_copy(p_hbm, p_ref, p_sem)
    p_copy.start()
    lane8 = iota((Q, 128), 1)
    code = jnp.where(lane8 < 64, code_ref[0:8, :], pltpu.roll(code_ref[8:16, :], 64, 1))
    valid = code >= 0
    block = jnp.where(valid, code & 63, BLK)
    me = lax.axis_index("query")
    source = (lane8 ^ FIRST_YQ) & (Q - 1)
    piece = (((source ^ me) & 1) << 2) + (((me >> 1) - (source >> 1)) & 3)
    query = jnp.where(valid, (code >> 6) + QL * piece, 0)

    b_iota = iota((BLK, 128), 0)
    hits = [block[q : q + 1, :] == b_iota for q in range(Q)]
    hit = jnp.concatenate([h.astype(jnp.float32) for h in hits], axis=0).astype(jnp.bfloat16)
    r_i, c_i = iota((128, 128), 0), iota((128, 128), 1)
    earlier = jnp.concatenate(
        [(r_i < c_i).astype(jnp.float32), jnp.ones((128, 128), jnp.float32)], axis=1
    ).astype(jnp.bfloat16)
    sums = dot(hit, earlier, ((1,), (0,)))
    base = jnp.zeros((BLK, 128), jnp.float32)
    bases = []
    for q in range(Q):
        bases.append(base + sums[BLK * q : BLK * (q + 1), :128])
        base = base + sums[BLK * q : BLK * (q + 1), 128:]
    groups = ((base.astype(jnp.int32) + (GROUP - 1)) >> 3).astype(jnp.float32)
    l_i, m_i = iota((BLK, BLK), 0), iota((BLK, BLK), 1)
    before = dot(
        (m_i < l_i).astype(jnp.float32).astype(jnp.bfloat16),
        groups.astype(jnp.bfloat16),
        ((1,), (0,)),
    )
    ends = (before + groups).astype(jnp.int32)
    dest = jnp.concatenate(
        [
            jnp.sum(jnp.where(hits[q], GROUP * before + bases[q], 0.0), axis=0, keepdims=True)
            for q in range(Q)
        ],
        axis=0,
    ).astype(jnp.int32)

    dest_ref[...] = dest
    c_iota = iota((GROUP, 128), 0)
    named = []
    for q in range(Q):
        here = ((dest[q : q + 1, :] & 7) == c_iota) & valid[q : q + 1, :]
        named.append(jnp.where(here, query[q : q + 1, :], 0).astype(jnp.float32))
    onehot = in_group(dest)
    onehot_ref[...] = onehot
    lists = dot(
        jnp.concatenate(named, axis=1).astype(jnp.bfloat16), onehot, ((1,), (1,))
    )
    plan_ref[0:GROUP, 0:GMAX] = lists.astype(jnp.int32)
    plan_ref[0:GROUP, GMAX:256] = jnp.zeros((GROUP, 256 - GMAX), jnp.int32)
    g_lane = iota((BLK, 256), 1)
    ends2 = jnp.concatenate([ends, ends], axis=1)
    owner_block = jnp.minimum(
        jnp.sum((ends2 <= g_lane).astype(jnp.int32), axis=0, keepdims=True), BLK - 1
    )
    total = jnp.broadcast_to(ends2[BLK - 1 : BLK, :], (1, 256))
    plan_ref[GROUP : 2 * GROUP, :] = jnp.where(
        iota((GROUP, 256), 0) == 0,
        jnp.broadcast_to(owner_block, (GROUP, 256)),
        jnp.broadcast_to(total, (GROUP, 256)),
    )
    p_copy.wait()
    q_copy.wait()


def in_group(dest):
    g_iota = iota((GMAX, 128), 0)
    return jnp.concatenate(
        [((dest[q : q + 1, :] >> 3) == g_iota).astype(jnp.float32) for q in range(Q)], axis=1
    ).astype(jnp.bfloat16)


def score_kernel(
    len_hbm, plan, dest_ref, onehot_ref, other_ref, p_ref, _, o_ref, q_ref,
    len_ref, plan_s, best, sem, len_sem, q_sem,
):
    half = NQ // 2
    q_copy = pltpu.make_async_copy(other_ref, q_ref.at[pl.ds(half, half)], q_sem)
    q_copy.start()
    len_copy = pltpu.make_async_copy(len_hbm, len_ref, len_sem)
    len_copy.start()
    copy = pltpu.make_async_copy(plan, plan_s, sem)
    copy.start()
    dest = dest_ref[...]
    c_iota = iota((GROUP, 128), 0)
    best[...] = jnp.zeros((GMAX, GROUP * T), jnp.float32)
    copy.wait()
    len_copy.wait()
    q_copy.wait()

    token = iota((PT, GROUP * T), 0)

    def step(it, carry):
        rows = []
        for u in range(UNROLL):
            g = it * UNROLL + u
            b = plan_s[GROUP, g]
            rows_q = jnp.concatenate([q_ref[plan_s[c, g]] for c in range(GROUP)], axis=0)
            similar = dot(p_ref[b], rows_q, ((1,), (1,)))
            similar = jnp.where(token < len_ref[b], similar, -jnp.inf)
            rows.append(jnp.max(similar, axis=0, keepdims=True))
        best[pl.ds(pl.multiple_of(it * UNROLL, UNROLL), UNROLL), :] = jnp.concatenate(rows, axis=0)
        return carry

    lax.fori_loop(0, (plan_s[GROUP + 1, 0] + (UNROLL - 1)) // UNROLL, step, 0)

    w = (iota((GROUP, GROUP * T), 0) == (iota((GROUP, GROUP * T), 1) >> 5)).astype(jnp.float32)
    w = w.astype(jnp.bfloat16)
    means = sum(dot(w, part, ((1,), (1,))) for part in split3(best[...])) * (1.0 / T)
    picked = dot(jnp.concatenate(split3(means), axis=0), onehot_ref[...], ((1,), (0,)))
    picked = picked[0:GROUP] + picked[GROUP : 2 * GROUP] + picked[2 * GROUP : 3 * GROUP]
    out = []
    for q in range(Q):
        here = (dest[q : q + 1, :] & 7) == c_iota
        out.append(
            jnp.sum(jnp.where(here, picked[:, 128 * q : 128 * (q + 1)], 0.0), axis=0, keepdims=True)
        )
    out = jnp.concatenate(out, axis=0)
    o_ref[0:8, :] = out
    o_ref[8:16, :] = pltpu.roll(out, 64, 1)


def place_kernel(cand_ref, key_ref, x_ref, o_ref):
    cand = jnp.concatenate([cand_ref[...], jnp.zeros((CL, 128 - QL), jnp.int32)], axis=1)
    lane = iota((1, 128), 1)
    turned = [cand] + [pltpu.roll(cand, 32 * i, 1) for i in range(1, 4)]
    segs = []
    for t in range(4):
        seg = turned[0][4 * t : 4 * t + 1, :]
        for i in range(1, 4):
            seg = jnp.where(lane >> 5 == i, turned[i][4 * t + i : 4 * t + i + 1, :], seg)
        segs.append(seg)
    asked = jnp.concatenate(segs, axis=1)
    place = iota((1, QL * CL), 1)
    own_key = ((place & 31) << 10) + ((place >> 5) << 6) + (asked & 63)
    owner = (asked >> 6) ^ FIRST
    lane_z = iota((Z, 128), 1)
    x = jnp.where(lane_z < 2 * YQ, x_ref[...], 0.0)
    key = jnp.where(lane_z < YQ, key_ref[...], 0)
    key_high = pltpu.roll(key >> 8, 2 * YQ, 1).astype(jnp.float32)
    key_low = pltpu.roll(key & 255, 3 * YQ, 1).astype(jnp.float32)
    high, mid, low = split3(x)
    high = jnp.where(
        lane_z < 2 * YQ,
        high.astype(jnp.float32),
        jnp.where(lane_z < 3 * YQ, key_high, key_low),
    ).astype(jnp.bfloat16)
    tables = jnp.concatenate([high, mid, low], axis=1)
    on_z = ((owner >> 5) == iota((Z, QL * CL), 0)).astype(jnp.float32).astype(jnp.bfloat16)
    found = dot(tables, on_z, ((0,), (0,)))
    on_yq = (owner & 31) == iota((YQ, QL * CL), 0)

    def pick(rows):
        return jnp.sum(jnp.where(on_yq, rows, 0.0), axis=0, keepdims=True)

    score = found[0 : 2 * YQ] + found[128 : 128 + 2 * YQ] + found[256 : 256 + 2 * YQ]
    first = pick(found[2 * YQ : 3 * YQ] * 256.0 + found[3 * YQ : 4 * YQ])
    out = jnp.where(
        first.astype(jnp.int32) == own_key, pick(score[0:YQ]), pick(score[YQ : 2 * YQ])
    )
    row = iota((CL, 128), 0)
    res = jnp.zeros((CL, 128), jnp.float32)
    for i in range(4):
        for t in range(4):
            seg = jnp.broadcast_to(out[:, 128 * t : 128 * (t + 1)], (CL, 128))
            seg = pltpu.roll(seg, 128 - 32 * i, 1) if i else seg
            res = jnp.where(row == 4 * t + i, seg, res)
    o_ref[...] = res[:, :QL]


VMEM = pl.BlockSpec(memory_space=pltpu.VMEM)


def small_call(kernel, out_shape, *args, hint=None):
    return pl.pallas_call(
        kernel,
        cost_estimate=hint,
        out_shape=out_shape,
        in_specs=[VMEM] * len(args),
        out_specs=jax.tree.map(lambda _: VMEM, out_shape),
    )(*[pltpu.with_memory_space_constraint(a, pltpu.VMEM) for a in args])


def shards(queries, passages, lengths, candidates):
    same = [queries] + [
        lax.ppermute(queries, "query", [(k, (k + 2 * d) % Q) for k in range(Q)])
        for d in range(1, Q // 2)
    ]
    cand = candidates.T
    table, keys = small_call(
        request_kernel,
        (pltpu.VMEM((YQ, 128), jnp.int32), pltpu.VMEM((Z, 128), jnp.int32)),
        cand,
    )
    got = exchange(table, YQ_GROUPS)
    hint = pl.CostEstimate(flops=10**11, transcendentals=0, bytes_accessed=2**20)
    got = small_call(by_z_kernel, pltpu.VMEM((Z, 128), jnp.int32), got, hint=hint)
    codes = exchange(got, Z_GROUPS)
    _, *same = lax.optimization_barrier((got, *same))
    same = jnp.concatenate(same, axis=0)
    other = lax.ppermute(same, "query", [(k, k ^ 1) for k in range(Q)])
    at = pltpu.with_memory_space_constraint
    hbm = pl.BlockSpec(memory_space=pltpu.HBM)
    every = pltpu.VMEM((NQ, T, D), queries.dtype)
    plan, dest, onehot, blocks, gathered = pl.pallas_call(
        sort_kernel,
        out_shape=(
            pltpu.VMEM((2 * GROUP, 256), jnp.int32),
            pltpu.VMEM((Q, 128), jnp.int32),
            pltpu.VMEM((GMAX, Q * 128), jnp.bfloat16),
            pltpu.VMEM(passages.shape, passages.dtype),
            every,
        ),
        in_specs=[VMEM, hbm, VMEM],
        out_specs=(VMEM,) * 5,
        scratch_shapes=[pltpu.SemaphoreType.DMA, pltpu.SemaphoreType.DMA],
        cost_estimate=pl.CostEstimate(flops=10**11, transcendentals=0, bytes_accessed=2**22),
        compiler_params=pltpu.CompilerParams(vmem_limit_bytes=32 << 20),
    )(at(codes, pltpu.VMEM), at(passages, pltpu.HBM), at(same, pltpu.VMEM))
    scores, _ = pl.pallas_call(
        score_kernel,
        out_shape=(pltpu.VMEM((Z, 128), jnp.float32), every),
        in_specs=[hbm] + [VMEM] * 6,
        out_specs=(VMEM, VMEM),
        input_output_aliases={6: 1},
        scratch_shapes=[
            pltpu.SMEM((BLK,), jnp.int32),
            pltpu.SMEM((2 * GROUP, 256), jnp.int32),
            pltpu.VMEM((GMAX, GROUP * T), jnp.float32),
            pltpu.SemaphoreType.DMA,
            pltpu.SemaphoreType.DMA,
            pltpu.SemaphoreType.DMA,
        ],
        compiler_params=pltpu.CompilerParams(vmem_limit_bytes=32 << 20),
    )(
        at(lengths, pltpu.HBM),
        *[at(x, pltpu.VMEM) for x in (plan, dest, onehot, other, blocks, gathered)],
    )
    back = small_call(by_plane_kernel, pltpu.VMEM((YQ, 128), jnp.float32), scores)
    back = exchange(back, YQ_GROUPS)
    back = small_call(by_z_kernel, pltpu.VMEM((Z, 128), jnp.float32), back)
    back = exchange(back, Z_GROUPS)
    out = small_call(
        place_kernel, jax.ShapeDtypeStruct((CL, QL), jnp.float32), cand, keys, back
    )
    return out.T


def solution(mesh):
    in_specs = (
        P("query", None, None),
        P(("index", "query"), None, None),
        P(("index", "query")),
        P("query", "index"),
    )
    return jax.shard_map(
        shards, mesh=mesh, in_specs=in_specs, out_specs=P("query", "index"), check_vma=False
    )
```

```python
import jax
import jax.numpy as jnp
from jax import lax
from jax.experimental import pallas as pl
from jax.experimental.pallas import tpu as pltpu
from jax.sharding import PartitionSpec as P

Z, Y, Q = 16, 4, 8
YQ = Y * Q
OWNERS = Z * YQ
BLK = 64
QL, CL = 32, 16
NQ = Q * QL
T, D, PT = 32, 128, 128
GROUP = 8
GMAX = 192
UNROLL = 32
BIG = 1 << 30

FIRST_Z, FIRST_YQ = Z // 2, (Y // 2) * Q + Q // 2 + 1
FIRST = FIRST_Z * YQ + FIRST_YQ
Z_GROUPS = [[r + YQ * (z ^ FIRST_Z) for z in range(Z)] for r in range(YQ)]
YQ_GROUPS = [[YQ * z + (r ^ FIRST_YQ) for r in range(YQ)] for z in range(Z)]


def iota(shape, axis):
    return lax.broadcasted_iota(jnp.int32, shape, axis)


def exchange(x, groups):
    return lax.all_to_all(
        x, ("index", "query"), split_axis=0, concat_axis=0, tiled=True,
        axis_index_groups=groups,
    )


def spread(rows, row, lane):
    out = jnp.zeros((Z, 128), jnp.int32)
    for k, slot in enumerate(rows):
        for j in range(4):
            shift = (32 * k - 32 * j) % 128
            for t in range(4):
                seg = jnp.broadcast_to(slot[:, 128 * t : 128 * (t + 1)], (Z, 128))
                seg = pltpu.roll(seg, shift, 1) if shift else seg
                out = jnp.where((row == 4 * t + j) & (lane >> 5 == k), seg, out)
    return out


def by_plane(x):
    xt = jnp.transpose(jnp.concatenate([x, jnp.zeros((112, 128), x.dtype)], axis=0))
    lane = iota((YQ, 128), 1)
    return jnp.where(lane < Z, xt[:YQ], pltpu.roll(xt[YQ : 2 * YQ], Z, 1))


def by_z(x):
    xt = jnp.transpose(jnp.concatenate([x, jnp.zeros((96, 128), x.dtype)], axis=0))
    lane = iota((Z, 128), 1)
    return jnp.where(lane < YQ, xt[:Z], pltpu.roll(xt[Z : 2 * Z], YQ, 1))


def by_plane_kernel(x_ref, o_ref):
    o_ref[...] = by_plane(x_ref[...])


def by_z_kernel(x_ref, o_ref):
    o_ref[...] = by_z(x_ref[...])


def request_kernel(cand_ref, code_ref, key_ref):
    cand = cand_ref[...]
    lane_owner = iota((CL, OWNERS), 1)
    sub = iota((CL, 1), 0)
    low = jnp.full((CL, OWNERS), BIG, jnp.int32)
    high = jnp.full((CL, OWNERS), -1, jnp.int32)
    for q in range(QL):
        col = cand[:, q : q + 1]
        key = (q << 10) + (sub << 6) + (col & 63)
        match = ((col >> 6) ^ FIRST) == lane_owner
        low = jnp.minimum(low, jnp.where(match, key, BIG))
        high = jnp.maximum(high, jnp.where(match, key, -1))
    last = jnp.max(high, axis=0, keepdims=True)
    first = jnp.where(last >= 0, jnp.min(low, axis=0, keepdims=True), -1)
    last = jnp.where(last != first, last, -1)
    row = iota((Z, 128), 0)
    lane = iota((Z, 128), 1)
    key = spread((first, last), row, lane)
    key_ref[...] = key
    code_ref[...] = jnp.where(
        (key >= 0) & (lane < 2 * YQ), ((key >> 10) << 6) + (key & 63), -1
    )


def split3(x):
    hi = x.astype(jnp.bfloat16)
    rest = x - hi.astype(jnp.float32)
    mid = rest.astype(jnp.bfloat16)
    low = (rest - mid.astype(jnp.float32)).astype(jnp.bfloat16)
    return hi, mid, low


def dot(a, b, dims):
    return lax.dot_general(a, b, (dims, ((), ())), preferred_element_type=jnp.float32)


def sort_kernel(
    code_ref, p_hbm, same_ref, plan_ref, dest_ref, onehot_ref, p_ref, q_ref, p_sem, q_sem
):
    q_copy = pltpu.make_async_copy(same_ref, q_ref.at[pl.ds(0, NQ // 2)], q_sem)
    q_copy.start()
    p_copy = pltpu.make_async_copy(p_hbm, p_ref, p_sem)
    p_copy.start()
    code = jnp.full((Q, 128), -1, jnp.int32)
    lane8 = iota((Q, 128), 1)
    for y in range(Y):
        part = code_ref[Q * y : Q * (y + 1), :]
        part = pltpu.roll(part, 32 * y, 1) if y else part
        code = jnp.where(lane8 >> 5 == y, part, code)
    valid = code >= 0
    block = jnp.where(valid, code & 63, BLK)
    me = lax.axis_index("query")
    source = iota((Q, 128), 0) ^ (FIRST_YQ & (Q - 1))
    piece = (((source ^ me) & 1) << 2) + (((me >> 1) - (source >> 1)) & 3)
    query = jnp.where(valid, (code >> 6) + QL * piece, 0)

    b_iota = iota((BLK, 128), 0)
    hits = [block[q : q + 1, :] == b_iota for q in range(Q)]
    hit = jnp.concatenate([h.astype(jnp.float32) for h in hits], axis=0).astype(jnp.bfloat16)
    r_i, c_i = iota((128, 128), 0), iota((128, 128), 1)
    earlier = jnp.concatenate(
        [(r_i < c_i).astype(jnp.float32), jnp.ones((128, 128), jnp.float32)], axis=1
    ).astype(jnp.bfloat16)
    sums = dot(hit, earlier, ((1,), (0,)))
    base = jnp.zeros((BLK, 128), jnp.float32)
    bases = []
    for q in range(Q):
        bases.append(base + sums[BLK * q : BLK * (q + 1), :128])
        base = base + sums[BLK * q : BLK * (q + 1), 128:]
    groups = ((base.astype(jnp.int32) + (GROUP - 1)) >> 3).astype(jnp.float32)
    l_i, m_i = iota((BLK, BLK), 0), iota((BLK, BLK), 1)
    before = dot(
        (m_i < l_i).astype(jnp.float32).astype(jnp.bfloat16),
        groups.astype(jnp.bfloat16),
        ((1,), (0,)),
    )
    ends = (before + groups).astype(jnp.int32)
    dest = jnp.concatenate(
        [
            jnp.sum(jnp.where(hits[q], GROUP * before + bases[q], 0.0), axis=0, keepdims=True)
            for q in range(Q)
        ],
        axis=0,
    ).astype(jnp.int32)

    dest_ref[...] = dest
    c_iota = iota((GROUP, 128), 0)
    named = []
    for q in range(Q):
        here = ((dest[q : q + 1, :] & 7) == c_iota) & valid[q : q + 1, :]
        named.append(jnp.where(here, query[q : q + 1, :], 0).astype(jnp.float32))
    onehot = in_group(dest)
    onehot_ref[...] = onehot
    lists = dot(
        jnp.concatenate(named, axis=1).astype(jnp.bfloat16), onehot, ((1,), (1,))
    )
    plan_ref[0:GROUP, 0:GMAX] = lists.astype(jnp.int32)
    plan_ref[0:GROUP, GMAX:256] = jnp.zeros((GROUP, 256 - GMAX), jnp.int32)
    g_lane = iota((BLK, 256), 1)
    ends2 = jnp.concatenate([ends, ends], axis=1)
    owner_block = jnp.minimum(
        jnp.sum((ends2 <= g_lane).astype(jnp.int32), axis=0, keepdims=True), BLK - 1
    )
    total = jnp.broadcast_to(ends2[BLK - 1 : BLK, :], (1, 256))
    plan_ref[GROUP : 2 * GROUP, :] = jnp.where(
        iota((GROUP, 256), 0) == 0,
        jnp.broadcast_to(owner_block, (GROUP, 256)),
        jnp.broadcast_to(total, (GROUP, 256)),
    )
    p_copy.wait()
    q_copy.wait()


def in_group(dest):
    g_iota = iota((GMAX, 128), 0)
    return jnp.concatenate(
        [((dest[q : q + 1, :] >> 3) == g_iota).astype(jnp.float32) for q in range(Q)], axis=1
    ).astype(jnp.bfloat16)


def score_kernel(
    len_hbm, plan, dest_ref, onehot_ref, other_ref, p_ref, _, o_ref, q_ref,
    len_ref, plan_s, best, sem, len_sem, q_sem,
):
    half = NQ // 2
    q_copy = pltpu.make_async_copy(other_ref, q_ref.at[pl.ds(half, half)], q_sem)
    q_copy.start()
    len_copy = pltpu.make_async_copy(len_hbm, len_ref, len_sem)
    len_copy.start()
    copy = pltpu.make_async_copy(plan, plan_s, sem)
    copy.start()
    dest = dest_ref[...]
    c_iota = iota((GROUP, 128), 0)
    best[...] = jnp.zeros((GMAX, GROUP * T), jnp.float32)
    copy.wait()
    len_copy.wait()
    q_copy.wait()

    token = iota((PT, GROUP * T), 0)

    def step(it, carry):
        rows = []
        for u in range(UNROLL):
            g = it * UNROLL + u
            b = plan_s[GROUP, g]
            rows_q = jnp.concatenate([q_ref[plan_s[c, g]] for c in range(GROUP)], axis=0)
            similar = dot(p_ref[b], rows_q, ((1,), (1,)))
            similar = jnp.where(token < len_ref[b], similar, -jnp.inf)
            rows.append(jnp.max(similar, axis=0, keepdims=True))
        best[pl.ds(pl.multiple_of(it * UNROLL, UNROLL), UNROLL), :] = jnp.concatenate(rows, axis=0)
        return carry

    lax.fori_loop(0, (plan_s[GROUP + 1, 0] + (UNROLL - 1)) // UNROLL, step, 0)

    w = (iota((GROUP, GROUP * T), 0) == (iota((GROUP, GROUP * T), 1) >> 5)).astype(jnp.float32)
    w = w.astype(jnp.bfloat16)
    means = sum(dot(w, part, ((1,), (1,))) for part in split3(best[...])) * (1.0 / T)
    picked = dot(jnp.concatenate(split3(means), axis=0), onehot_ref[...], ((1,), (0,)))
    picked = picked[0:GROUP] + picked[GROUP : 2 * GROUP] + picked[2 * GROUP : 3 * GROUP]
    out = []
    for q in range(Q):
        here = (dest[q : q + 1, :] & 7) == c_iota
        out.append(
            jnp.sum(jnp.where(here, picked[:, 128 * q : 128 * (q + 1)], 0.0), axis=0, keepdims=True)
        )
    out = jnp.concatenate(out, axis=0)
    for y in range(Y):
        shift = (128 - 32 * y) % 128
        o_ref[Q * y : Q * (y + 1), :] = pltpu.roll(out, shift, 1) if shift else out


def place_kernel(cand_ref, key_ref, x_ref, o_ref):
    cand = jnp.concatenate([cand_ref[...], jnp.zeros((CL, 128 - QL), jnp.int32)], axis=1)
    lane = iota((1, 128), 1)
    turned = [cand] + [pltpu.roll(cand, 32 * i, 1) for i in range(1, 4)]
    segs = []
    for t in range(4):
        seg = turned[0][4 * t : 4 * t + 1, :]
        for i in range(1, 4):
            seg = jnp.where(lane >> 5 == i, turned[i][4 * t + i : 4 * t + i + 1, :], seg)
        segs.append(seg)
    asked = jnp.concatenate(segs, axis=1)
    place = iota((1, QL * CL), 1)
    own_key = ((place & 31) << 10) + ((place >> 5) << 6) + (asked & 63)
    owner = (asked >> 6) ^ FIRST
    lane_z = iota((Z, 128), 1)
    x = jnp.where(lane_z < 2 * YQ, x_ref[...], 0.0)
    key = jnp.where(lane_z < YQ, key_ref[...], 0)
    key_high = pltpu.roll(key >> 8, 2 * YQ, 1).astype(jnp.float32)
    key_low = pltpu.roll(key & 255, 3 * YQ, 1).astype(jnp.float32)
    high, mid, low = split3(x)
    high = jnp.where(
        lane_z < 2 * YQ,
        high.astype(jnp.float32),
        jnp.where(lane_z < 3 * YQ, key_high, key_low),
    ).astype(jnp.bfloat16)
    tables = jnp.concatenate([high, mid, low], axis=1)
    on_z = ((owner >> 5) == iota((Z, QL * CL), 0)).astype(jnp.float32).astype(jnp.bfloat16)
    found = dot(tables, on_z, ((0,), (0,)))
    on_yq = (owner & 31) == iota((YQ, QL * CL), 0)

    def pick(rows):
        return jnp.sum(jnp.where(on_yq, rows, 0.0), axis=0, keepdims=True)

    score = found[0 : 2 * YQ] + found[128 : 128 + 2 * YQ] + found[256 : 256 + 2 * YQ]
    first = pick(found[2 * YQ : 3 * YQ] * 256.0 + found[3 * YQ : 4 * YQ])
    out = jnp.where(
        first.astype(jnp.int32) == own_key, pick(score[0:YQ]), pick(score[YQ : 2 * YQ])
    )
    row = iota((CL, 128), 0)
    res = jnp.zeros((CL, 128), jnp.float32)
    for i in range(4):
        for t in range(4):
            seg = jnp.broadcast_to(out[:, 128 * t : 128 * (t + 1)], (CL, 128))
            seg = pltpu.roll(seg, 128 - 32 * i, 1) if i else seg
            res = jnp.where(row == 4 * t + i, seg, res)
    o_ref[...] = res[:, :QL]


VMEM = pl.BlockSpec(memory_space=pltpu.VMEM)


def small_call(kernel, out_shape, *args, hint=None):
    return pl.pallas_call(
        kernel,
        cost_estimate=hint,
        out_shape=out_shape,
        in_specs=[VMEM] * len(args),
        out_specs=jax.tree.map(lambda _: VMEM, out_shape),
    )(*[pltpu.with_memory_space_constraint(a, pltpu.VMEM) for a in args])


def shards(queries, passages, lengths, candidates):
    same = [queries] + [
        lax.ppermute(queries, "query", [(k, (k + 2 * d) % Q) for k in range(Q)])
        for d in range(1, Q // 2)
    ]
    cand = candidates.T
    table, keys = small_call(
        request_kernel,
        (pltpu.VMEM((Z, 128), jnp.int32), pltpu.VMEM((Z, 128), jnp.int32)),
        cand,
    )
    got = exchange(table, Z_GROUPS)
    hint = pl.CostEstimate(flops=10**11, transcendentals=0, bytes_accessed=2**20)
    got = small_call(by_plane_kernel, pltpu.VMEM((YQ, 128), jnp.int32), got, hint=hint)
    codes = exchange(got, YQ_GROUPS)
    _, *same = lax.optimization_barrier((got, *same))
    same = jnp.concatenate(same, axis=0)
    other = lax.ppermute(same, "query", [(k, k ^ 1) for k in range(Q)])
    at = pltpu.with_memory_space_constraint
    hbm = pl.BlockSpec(memory_space=pltpu.HBM)
    every = pltpu.VMEM((NQ, T, D), queries.dtype)
    plan, dest, onehot, blocks, gathered = pl.pallas_call(
        sort_kernel,
        out_shape=(
            pltpu.VMEM((2 * GROUP, 256), jnp.int32),
            pltpu.VMEM((Q, 128), jnp.int32),
            pltpu.VMEM((GMAX, Q * 128), jnp.bfloat16),
            pltpu.VMEM(passages.shape, passages.dtype),
            every,
        ),
        in_specs=[VMEM, hbm, VMEM],
        out_specs=(VMEM,) * 5,
        scratch_shapes=[pltpu.SemaphoreType.DMA, pltpu.SemaphoreType.DMA],
        cost_estimate=pl.CostEstimate(flops=10**11, transcendentals=0, bytes_accessed=2**22),
        compiler_params=pltpu.CompilerParams(vmem_limit_bytes=32 << 20),
    )(at(codes, pltpu.VMEM), at(passages, pltpu.HBM), at(same, pltpu.VMEM))
    scores, _ = pl.pallas_call(
        score_kernel,
        out_shape=(pltpu.VMEM((YQ, 128), jnp.float32), every),
        in_specs=[hbm] + [VMEM] * 6,
        out_specs=(VMEM, VMEM),
        input_output_aliases={6: 1},
        scratch_shapes=[
            pltpu.SMEM((BLK,), jnp.int32),
            pltpu.SMEM((2 * GROUP, 256), jnp.int32),
            pltpu.VMEM((GMAX, GROUP * T), jnp.float32),
            pltpu.SemaphoreType.DMA,
            pltpu.SemaphoreType.DMA,
            pltpu.SemaphoreType.DMA,
        ],
        compiler_params=pltpu.CompilerParams(vmem_limit_bytes=32 << 20),
    )(
        at(lengths, pltpu.HBM),
        *[at(x, pltpu.VMEM) for x in (plan, dest, onehot, other, blocks, gathered)],
    )
    back = exchange(scores, YQ_GROUPS)
    back = small_call(by_z_kernel, pltpu.VMEM((Z, 128), jnp.float32), back)
    back = exchange(back, Z_GROUPS)
    out = small_call(
        place_kernel, jax.ShapeDtypeStruct((CL, QL), jnp.float32), cand, keys, back
    )
    return out.T


def solution(mesh):
    in_specs = (
        P("query", None, None),
        P(("index", "query"), None, None),
        P(("index", "query")),
        P("query", "index"),
    )
    return jax.shard_map(
        shards, mesh=mesh, in_specs=in_specs, out_specs=P("query", "index"), check_vma=False
    )
```

```python
import jax
import jax.numpy as jnp
from jax import lax
from jax.experimental import pallas as pl
from jax.experimental.pallas import tpu as pltpu
from jax.sharding import PartitionSpec as P

Z, Y, Q = 16, 4, 8
YQ = Y * Q
OWNERS = Z * YQ
BLK = 64
QL, CL = 32, 16
NQ = Q * QL
T, D, PT = 32, 128, 128
GROUP = 8
GMAX = 192
UNROLL = 32
BIG = 1 << 30

FIRST_Z, FIRST_YQ = Z // 2, (Y // 2) * Q + Q // 2 + 1
FIRST = FIRST_Z * YQ + FIRST_YQ
Z_GROUPS = [[r + YQ * (z ^ FIRST_Z) for z in range(Z)] for r in range(YQ)]
YQ_GROUPS = [[YQ * z + (r ^ FIRST_YQ) for r in range(YQ)] for z in range(Z)]


def iota(shape, axis):
    return lax.broadcasted_iota(jnp.int32, shape, axis)


def exchange(x, groups):
    return lax.all_to_all(
        x, ("index", "query"), split_axis=0, concat_axis=0, tiled=True,
        axis_index_groups=groups,
    )


def spread(rows, row, lane):
    out = jnp.zeros((Z, 128), jnp.int32)
    for k, slot in enumerate(rows):
        for j in range(4):
            shift = (32 * k - 32 * j) % 128
            for t in range(4):
                seg = jnp.broadcast_to(slot[:, 128 * t : 128 * (t + 1)], (Z, 128))
                seg = pltpu.roll(seg, shift, 1) if shift else seg
                out = jnp.where((row == 4 * t + j) & (lane >> 5 == k), seg, out)
    return out


def by_plane(x):
    xt = jnp.transpose(jnp.concatenate([x, jnp.zeros((112, 128), x.dtype)], axis=0))
    lane = iota((YQ, 128), 1)
    return jnp.where(lane < Z, xt[:YQ], pltpu.roll(xt[YQ : 2 * YQ], Z, 1))


def by_z(x):
    xt = jnp.transpose(jnp.concatenate([x, jnp.zeros((96, 128), x.dtype)], axis=0))
    lane = iota((Z, 128), 1)
    return jnp.where(lane < YQ, xt[:Z], pltpu.roll(xt[Z : 2 * Z], YQ, 1))


def by_plane_kernel(x_ref, o_ref):
    o_ref[...] = by_plane(x_ref[...])


def by_z_kernel(x_ref, o_ref):
    o_ref[...] = by_z(x_ref[...])


def request_kernel(cand_ref, code_ref, key_ref):
    cand = cand_ref[...]
    lane_owner = iota((CL, OWNERS), 1)
    sub = iota((CL, 1), 0)
    low = jnp.full((CL, OWNERS), BIG, jnp.int32)
    high = jnp.full((CL, OWNERS), -1, jnp.int32)
    for q in range(QL):
        col = cand[:, q : q + 1]
        key = (q << 10) + (sub << 6) + (col & 63)
        match = ((col >> 6) ^ FIRST) == lane_owner
        low = jnp.minimum(low, jnp.where(match, key, BIG))
        high = jnp.maximum(high, jnp.where(match, key, -1))
    last = jnp.max(high, axis=0, keepdims=True)
    first = jnp.where(last >= 0, jnp.min(low, axis=0, keepdims=True), -1)
    last = jnp.where(last != first, last, -1)
    row = iota((Z, 128), 0)
    lane = iota((Z, 128), 1)
    key = spread((first, last), row, lane)
    key_ref[...] = key
    code = jnp.where((key >= 0) & (lane < 2 * YQ), ((key >> 10) << 6) + (key & 63), -1)
    code_ref[...] = by_plane(code)


def split3(x):
    hi = x.astype(jnp.bfloat16)
    rest = x - hi.astype(jnp.float32)
    mid = rest.astype(jnp.bfloat16)
    low = (rest - mid.astype(jnp.float32)).astype(jnp.bfloat16)
    return hi, mid, low


def dot(a, b, dims):
    return lax.dot_general(a, b, (dims, ((), ())), preferred_element_type=jnp.float32)


def sort_kernel(
    code_ref, p_hbm, same_ref, len_hbm, plan_ref, dest_ref, onehot_ref, p_ref, q_ref,
    len_ref, p_sem, q_sem, len_sem,
):
    len_copy = pltpu.make_async_copy(len_hbm, len_ref, len_sem)
    len_copy.start()
    q_copy = pltpu.make_async_copy(same_ref, q_ref.at[pl.ds(0, NQ // 2)], q_sem)
    q_copy.start()
    p_copy = pltpu.make_async_copy(p_hbm, p_ref, p_sem)
    p_copy.start()
    lane8 = iota((Q, 128), 1)
    code = jnp.where(lane8 < 64, code_ref[0:8, :], pltpu.roll(code_ref[8:16, :], 64, 1))
    valid = code >= 0
    block = jnp.where(valid, code & 63, BLK)
    me = lax.axis_index("query")
    source = (lane8 ^ FIRST_YQ) & (Q - 1)
    piece = (((source ^ me) & 1) << 2) + (((me >> 1) - (source >> 1)) & 3)
    query = jnp.where(valid, (code >> 6) + QL * piece, 0)

    b_iota = iota((BLK, 128), 0)
    hits = [block[q : q + 1, :] == b_iota for q in range(Q)]
    hit = jnp.concatenate([h.astype(jnp.float32) for h in hits], axis=0).astype(jnp.bfloat16)
    r_i, c_i = iota((128, 128), 0), iota((128, 128), 1)
    earlier = jnp.concatenate(
        [(r_i < c_i).astype(jnp.float32), jnp.ones((128, 128), jnp.float32)], axis=1
    ).astype(jnp.bfloat16)
    sums = dot(hit, earlier, ((1,), (0,)))
    base = jnp.zeros((BLK, 128), jnp.float32)
    bases = []
    for q in range(Q):
        bases.append(base + sums[BLK * q : BLK * (q + 1), :128])
        base = base + sums[BLK * q : BLK * (q + 1), 128:]
    groups = ((base.astype(jnp.int32) + (GROUP - 1)) >> 3).astype(jnp.float32)
    l_i, m_i = iota((BLK, BLK), 0), iota((BLK, BLK), 1)
    before = dot(
        (m_i < l_i).astype(jnp.float32).astype(jnp.bfloat16),
        groups.astype(jnp.bfloat16),
        ((1,), (0,)),
    )
    ends = (before + groups).astype(jnp.int32)
    dest = jnp.concatenate(
        [
            jnp.sum(jnp.where(hits[q], GROUP * before + bases[q], 0.0), axis=0, keepdims=True)
            for q in range(Q)
        ],
        axis=0,
    ).astype(jnp.int32)

    dest_ref[...] = dest
    c_iota = iota((GROUP, 128), 0)
    named = []
    for q in range(Q):
        here = ((dest[q : q + 1, :] & 7) == c_iota) & valid[q : q + 1, :]
        named.append(jnp.where(here, query[q : q + 1, :], 0).astype(jnp.float32))
    onehot = in_group(dest)
    onehot_ref[...] = onehot
    lists = dot(
        jnp.concatenate(named, axis=1).astype(jnp.bfloat16), onehot, ((1,), (1,))
    )
    plan_ref[0:GROUP, 0:GMAX] = lists.astype(jnp.int32)
    plan_ref[0:GROUP, GMAX:256] = jnp.zeros((GROUP, 256 - GMAX), jnp.int32)
    g_lane = iota((BLK, 256), 1)
    ends2 = jnp.concatenate([ends, ends], axis=1)
    owner_block = jnp.minimum(
        jnp.sum((ends2 <= g_lane).astype(jnp.int32), axis=0, keepdims=True), BLK - 1
    )
    total = jnp.broadcast_to(ends2[BLK - 1 : BLK, :], (1, 256))
    len_copy.wait()
    live = jnp.concatenate([len_ref[...], jnp.zeros((1, 256 - BLK), jnp.int32)], axis=1)
    row = iota((GROUP, 256), 0)
    plan_ref[GROUP : 2 * GROUP, :] = jnp.where(
        row == 0,
        jnp.broadcast_to(owner_block, (GROUP, 256)),
        jnp.where(
            row == 1,
            jnp.broadcast_to(total, (GROUP, 256)),
            jnp.broadcast_to(live, (GROUP, 256)),
        ),
    )
    p_copy.wait()
    q_copy.wait()


def in_group(dest):
    g_iota = iota((GMAX, 128), 0)
    return jnp.concatenate(
        [((dest[q : q + 1, :] >> 3) == g_iota).astype(jnp.float32) for q in range(Q)], axis=1
    ).astype(jnp.bfloat16)


def score_kernel(
    plan, dest_ref, onehot_ref, other_ref, p_ref, _, o_ref, q_ref, plan_s, best, sem, q_sem
):
    half = NQ // 2
    q_copy = pltpu.make_async_copy(other_ref, q_ref.at[pl.ds(half, half)], q_sem)
    q_copy.start()
    copy = pltpu.make_async_copy(plan, plan_s, sem)
    copy.start()
    dest = dest_ref[...]
    c_iota = iota((GROUP, 128), 0)
    best[...] = jnp.zeros((GMAX, GROUP * T), jnp.float32)
    copy.wait()
    q_copy.wait()

    token = iota((PT, GROUP * T), 0)

    def step(it, carry):
        rows = []
        for u in range(UNROLL):
            g = it * UNROLL + u
            b = plan_s[GROUP, g]
            rows_q = jnp.concatenate([q_ref[plan_s[c, g]] for c in range(GROUP)], axis=0)
            similar = dot(p_ref[b], rows_q, ((1,), (1,)))
            similar = jnp.where(token < plan_s[GROUP + 2, b], similar, -jnp.inf)
            rows.append(jnp.max(similar, axis=0, keepdims=True))
        best[pl.ds(pl.multiple_of(it * UNROLL, UNROLL), UNROLL), :] = jnp.concatenate(rows, axis=0)
        return carry

    lax.fori_loop(0, (plan_s[GROUP + 1, 0] + (UNROLL - 1)) // UNROLL, step, 0)

    w = (iota((GROUP, GROUP * T), 0) == (iota((GROUP, GROUP * T), 1) >> 5)).astype(jnp.float32)
    w = w.astype(jnp.bfloat16)
    means = sum(dot(w, part, ((1,), (1,))) for part in split3(best[...])) * (1.0 / T)
    picked = dot(jnp.concatenate(split3(means), axis=0), onehot_ref[...], ((1,), (0,)))
    picked = picked[0:GROUP] + picked[GROUP : 2 * GROUP] + picked[2 * GROUP : 3 * GROUP]
    out = []
    for q in range(Q):
        here = (dest[q : q + 1, :] & 7) == c_iota
        out.append(
            jnp.sum(jnp.where(here, picked[:, 128 * q : 128 * (q + 1)], 0.0), axis=0, keepdims=True)
        )
    out = jnp.concatenate(out, axis=0)
    o_ref[0:8, :] = out
    o_ref[8:16, :] = pltpu.roll(out, 64, 1)


def place_kernel(cand_ref, key_ref, x_ref, o_ref):
    cand = jnp.concatenate([cand_ref[...], jnp.zeros((CL, 128 - QL), jnp.int32)], axis=1)
    lane = iota((1, 128), 1)
    turned = [cand] + [pltpu.roll(cand, 32 * i, 1) for i in range(1, 4)]
    segs = []
    for t in range(4):
        seg = turned[0][4 * t : 4 * t + 1, :]
        for i in range(1, 4):
            seg = jnp.where(lane >> 5 == i, turned[i][4 * t + i : 4 * t + i + 1, :], seg)
        segs.append(seg)
    asked = jnp.concatenate(segs, axis=1)
    place = iota((1, QL * CL), 1)
    own_key = ((place & 31) << 10) + ((place >> 5) << 6) + (asked & 63)
    owner = (asked >> 6) ^ FIRST
    lane_z = iota((Z, 128), 1)
    x = jnp.where(lane_z < 2 * YQ, x_ref[...], 0.0)
    key = jnp.where(lane_z < YQ, key_ref[...], 0)
    key_high = pltpu.roll(key >> 8, 2 * YQ, 1).astype(jnp.float32)
    key_low = pltpu.roll(key & 255, 3 * YQ, 1).astype(jnp.float32)
    high, mid, low = split3(x)
    high = jnp.where(
        lane_z < 2 * YQ,
        high.astype(jnp.float32),
        jnp.where(lane_z < 3 * YQ, key_high, key_low),
    ).astype(jnp.bfloat16)
    tables = jnp.concatenate([high, mid, low], axis=1)
    on_z = ((owner >> 5) == iota((Z, QL * CL), 0)).astype(jnp.float32).astype(jnp.bfloat16)
    found = dot(tables, on_z, ((0,), (0,)))
    on_yq = (owner & 31) == iota((YQ, QL * CL), 0)

    def pick(rows):
        return jnp.sum(jnp.where(on_yq, rows, 0.0), axis=0, keepdims=True)

    score = found[0 : 2 * YQ] + found[128 : 128 + 2 * YQ] + found[256 : 256 + 2 * YQ]
    first = pick(found[2 * YQ : 3 * YQ] * 256.0 + found[3 * YQ : 4 * YQ])
    out = jnp.where(
        first.astype(jnp.int32) == own_key, pick(score[0:YQ]), pick(score[YQ : 2 * YQ])
    )
    row = iota((CL, 128), 0)
    res = jnp.zeros((CL, 128), jnp.float32)
    for i in range(4):
        for t in range(4):
            seg = jnp.broadcast_to(out[:, 128 * t : 128 * (t + 1)], (CL, 128))
            seg = pltpu.roll(seg, 128 - 32 * i, 1) if i else seg
            res = jnp.where(row == 4 * t + i, seg, res)
    o_ref[...] = res[:, :QL]


VMEM = pl.BlockSpec(memory_space=pltpu.VMEM)


def small_call(kernel, out_shape, *args, hint=None):
    return pl.pallas_call(
        kernel,
        cost_estimate=hint,
        out_shape=out_shape,
        in_specs=[VMEM] * len(args),
        out_specs=jax.tree.map(lambda _: VMEM, out_shape),
    )(*[pltpu.with_memory_space_constraint(a, pltpu.VMEM) for a in args])


def shards(queries, passages, lengths, candidates):
    same = [queries] + [
        lax.ppermute(queries, "query", [(k, (k + 2 * d) % Q) for k in range(Q)])
        for d in range(1, Q // 2)
    ]
    cand = candidates.T
    table, keys = small_call(
        request_kernel,
        (pltpu.VMEM((YQ, 128), jnp.int32), pltpu.VMEM((Z, 128), jnp.int32)),
        cand,
    )
    got = exchange(table, YQ_GROUPS)
    hint = pl.CostEstimate(flops=10**11, transcendentals=0, bytes_accessed=2**20)
    got = small_call(by_z_kernel, pltpu.VMEM((Z, 128), jnp.int32), got, hint=hint)
    codes = exchange(got, Z_GROUPS)
    _, *same = lax.optimization_barrier((got, *same))
    same = jnp.concatenate(same, axis=0)
    other = lax.ppermute(same, "query", [(k, k ^ 1) for k in range(Q)])
    at = pltpu.with_memory_space_constraint
    hbm = pl.BlockSpec(memory_space=pltpu.HBM)
    every = pltpu.VMEM((NQ, T, D), queries.dtype)
    plan, dest, onehot, blocks, gathered = pl.pallas_call(
        sort_kernel,
        out_shape=(
            pltpu.VMEM((2 * GROUP, 256), jnp.int32),
            pltpu.VMEM((Q, 128), jnp.int32),
            pltpu.VMEM((GMAX, Q * 128), jnp.bfloat16),
            pltpu.VMEM(passages.shape, passages.dtype),
            every,
        ),
        in_specs=[VMEM, hbm, VMEM, hbm],
        out_specs=(VMEM,) * 5,
        scratch_shapes=[pltpu.VMEM((1, BLK), jnp.int32)] + [pltpu.SemaphoreType.DMA] * 3,
        cost_estimate=pl.CostEstimate(flops=10**11, transcendentals=0, bytes_accessed=2**22),
        compiler_params=pltpu.CompilerParams(vmem_limit_bytes=32 << 20),
    )(
        at(codes, pltpu.VMEM),
        at(passages, pltpu.HBM),
        at(same, pltpu.VMEM),
        at(lengths.reshape(1, BLK), pltpu.HBM),
    )
    scores, _ = pl.pallas_call(
        score_kernel,
        out_shape=(pltpu.VMEM((Z, 128), jnp.float32), every),
        in_specs=[VMEM] * 6,
        out_specs=(VMEM, VMEM),
        input_output_aliases={5: 1},
        scratch_shapes=[
            pltpu.SMEM((2 * GROUP, 256), jnp.int32),
            pltpu.VMEM((GMAX, GROUP * T), jnp.float32),
            pltpu.SemaphoreType.DMA,
            pltpu.SemaphoreType.DMA,
        ],
        compiler_params=pltpu.CompilerParams(vmem_limit_bytes=32 << 20),
    )(
        *[at(x, pltpu.VMEM) for x in (plan, dest, onehot, other, blocks, gathered)],
    )
    back = small_call(by_plane_kernel, pltpu.VMEM((YQ, 128), jnp.float32), scores)
    back = exchange(back, YQ_GROUPS)
    back = small_call(by_z_kernel, pltpu.VMEM((Z, 128), jnp.float32), back)
    back = exchange(back, Z_GROUPS)
    out = small_call(
        place_kernel, jax.ShapeDtypeStruct((CL, QL), jnp.float32), cand, keys, back
    )
    return out.T


def solution(mesh):
    in_specs = (
        P("query", None, None),
        P(("index", "query"), None, None),
        P(("index", "query")),
        P("query", "index"),
    )
    return jax.shard_map(
        shards, mesh=mesh, in_specs=in_specs, out_specs=P("query", "index"), check_vma=False
    )
```

```python
import jax
import jax.numpy as jnp
from jax import lax
from jax.experimental import pallas as pl
from jax.experimental.pallas import tpu as pltpu
from jax.sharding import PartitionSpec as P

Z, Y, Q = 16, 4, 8
YQ = Y * Q
OWNERS = Z * YQ
BLK = 64
QL, CL = 32, 16
NQ = Q * QL
T, D, PT = 32, 128, 128
GROUP = 8
GMAX = 192
UNROLL = 32
BIG = 1 << 30

FIRST_Z, FIRST_YQ = Z // 2, (Y // 2) * Q + Q // 2 + 1
FIRST = FIRST_Z * YQ + FIRST_YQ
Z_GROUPS = [[r + YQ * (z ^ FIRST_Z) for z in range(Z)] for r in range(YQ)]
YQ_GROUPS = [[YQ * z + (r ^ FIRST_YQ) for r in range(YQ)] for z in range(Z)]


def iota(shape, axis):
    return lax.broadcasted_iota(jnp.int32, shape, axis)


def exchange(x, groups):
    return lax.all_to_all(
        x, ("index", "query"), split_axis=0, concat_axis=0, tiled=True,
        axis_index_groups=groups,
    )


def spread(rows, row, lane):
    out = jnp.zeros((Z, 128), jnp.int32)
    for k, slot in enumerate(rows):
        for j in range(4):
            shift = (32 * k - 32 * j) % 128
            for t in range(4):
                seg = jnp.broadcast_to(slot[:, 128 * t : 128 * (t + 1)], (Z, 128))
                seg = pltpu.roll(seg, shift, 1) if shift else seg
                out = jnp.where((row == 4 * t + j) & (lane >> 5 == k), seg, out)
    return out


def by_plane(x):
    xt = jnp.transpose(jnp.concatenate([x, jnp.zeros((112, 128), x.dtype)], axis=0))
    lane = iota((YQ, 128), 1)
    return jnp.where(lane < Z, xt[:YQ], pltpu.roll(xt[YQ : 2 * YQ], Z, 1))


def by_z(x):
    xt = jnp.transpose(jnp.concatenate([x, jnp.zeros((96, 128), x.dtype)], axis=0))
    lane = iota((Z, 128), 1)
    return jnp.where(lane < YQ, xt[:Z], pltpu.roll(xt[Z : 2 * Z], YQ, 1))


def by_plane_kernel(x_ref, o_ref):
    o_ref[...] = by_plane(x_ref[...])


def by_z_kernel(x_ref, o_ref):
    o_ref[...] = by_z(x_ref[...])


def request_kernel(cand_ref, code_ref, key_ref):
    cand = cand_ref[...]
    lane_owner = iota((CL, OWNERS), 1)
    sub = iota((CL, 1), 0)
    low = jnp.full((CL, OWNERS), BIG, jnp.int32)
    high = jnp.full((CL, OWNERS), -1, jnp.int32)
    for q in range(QL):
        col = cand[:, q : q + 1]
        key = (q << 10) + (sub << 6) + (col & 63)
        match = ((col >> 6) ^ FIRST) == lane_owner
        low = jnp.minimum(low, jnp.where(match, key, BIG))
        high = jnp.maximum(high, jnp.where(match, key, -1))
    last = jnp.max(high, axis=0, keepdims=True)
    first = jnp.where(last >= 0, jnp.min(low, axis=0, keepdims=True), -1)
    last = jnp.where(last != first, last, -1)
    row = iota((Z, 128), 0)
    lane = iota((Z, 128), 1)
    key = spread((first, last), row, lane)
    key_ref[...] = key
    code = jnp.where((key >= 0) & (lane < 2 * YQ), ((key >> 10) << 6) + (key & 63), -1)
    code_ref[...] = by_plane(code)


def split3(x):
    hi = x.astype(jnp.bfloat16)
    rest = x - hi.astype(jnp.float32)
    mid = rest.astype(jnp.bfloat16)
    low = (rest - mid.astype(jnp.float32)).astype(jnp.bfloat16)
    return hi, mid, low


def dot(a, b, dims):
    return lax.dot_general(a, b, (dims, ((), ())), preferred_element_type=jnp.float32)


def sort_kernel(
    code_ref, same_ref, len_hbm, plan_ref, dest_ref, onehot_ref, q_ref, len_ref, q_sem, len_sem
):
    len_copy = pltpu.make_async_copy(len_hbm, len_ref, len_sem)
    len_copy.start()
    q_copy = pltpu.make_async_copy(same_ref, q_ref.at[pl.ds(0, NQ // 2)], q_sem)
    q_copy.start()
    lane8 = iota((Q, 128), 1)
    code = jnp.where(lane8 < 64, code_ref[0:8, :], pltpu.roll(code_ref[8:16, :], 64, 1))
    valid = code >= 0
    block = jnp.where(valid, code & 63, BLK)
    me = lax.axis_index("query")
    source = (lane8 ^ FIRST_YQ) & (Q - 1)
    piece = (((source ^ me) & 1) << 2) + (((me >> 1) - (source >> 1)) & 3)
    query = jnp.where(valid, (code >> 6) + QL * piece, 0)

    b_iota = iota((BLK, 128), 0)
    hits = [block[q : q + 1, :] == b_iota for q in range(Q)]
    hit = jnp.concatenate([h.astype(jnp.float32) for h in hits], axis=0).astype(jnp.bfloat16)
    r_i, c_i = iota((128, 128), 0), iota((128, 128), 1)
    earlier = jnp.concatenate(
        [(r_i < c_i).astype(jnp.float32), jnp.ones((128, 128), jnp.float32)], axis=1
    ).astype(jnp.bfloat16)
    sums = dot(hit, earlier, ((1,), (0,)))
    base = jnp.zeros((BLK, 128), jnp.float32)
    bases = []
    for q in range(Q):
        bases.append(base + sums[BLK * q : BLK * (q + 1), :128])
        base = base + sums[BLK * q : BLK * (q + 1), 128:]
    groups = ((base.astype(jnp.int32) + (GROUP - 1)) >> 3).astype(jnp.float32)
    l_i, m_i = iota((BLK, BLK), 0), iota((BLK, BLK), 1)
    before = dot(
        (m_i < l_i).astype(jnp.float32).astype(jnp.bfloat16),
        groups.astype(jnp.bfloat16),
        ((1,), (0,)),
    )
    ends = (before + groups).astype(jnp.int32)
    dest = jnp.concatenate(
        [
            jnp.sum(jnp.where(hits[q], GROUP * before + bases[q], 0.0), axis=0, keepdims=True)
            for q in range(Q)
        ],
        axis=0,
    ).astype(jnp.int32)

    dest_ref[...] = dest
    c_iota = iota((GROUP, 128), 0)
    named = []
    for q in range(Q):
        here = ((dest[q : q + 1, :] & 7) == c_iota) & valid[q : q + 1, :]
        named.append(jnp.where(here, query[q : q + 1, :], 0).astype(jnp.float32))
    onehot = in_group(dest)
    onehot_ref[...] = onehot
    lists = dot(
        jnp.concatenate(named, axis=1).astype(jnp.bfloat16), onehot, ((1,), (1,))
    )
    plan_ref[0:GROUP, 0:GMAX] = lists.astype(jnp.int32)
    plan_ref[0:GROUP, GMAX:256] = jnp.zeros((GROUP, 256 - GMAX), jnp.int32)
    g_lane = iota((BLK, 256), 1)
    ends2 = jnp.concatenate([ends, ends], axis=1)
    owner_block = jnp.minimum(
        jnp.sum((ends2 <= g_lane).astype(jnp.int32), axis=0, keepdims=True), BLK - 1
    )
    total = jnp.broadcast_to(ends2[BLK - 1 : BLK, :], (1, 256))
    len_copy.wait()
    live = jnp.concatenate([len_ref[...], jnp.zeros((1, 256 - BLK), jnp.int32)], axis=1)
    row = iota((GROUP, 256), 0)
    plan_ref[GROUP : 2 * GROUP, :] = jnp.where(
        row == 0,
        jnp.broadcast_to(owner_block, (GROUP, 256)),
        jnp.where(
            row == 1,
            jnp.broadcast_to(total, (GROUP, 256)),
            jnp.broadcast_to(live, (GROUP, 256)),
        ),
    )
    q_copy.wait()


def fetch_kernel(_, p_hbm, p_ref, sem):
    copy = pltpu.make_async_copy(p_hbm, p_ref, sem)
    copy.start()
    copy.wait()


def in_group(dest):
    g_iota = iota((GMAX, 128), 0)
    return jnp.concatenate(
        [((dest[q : q + 1, :] >> 3) == g_iota).astype(jnp.float32) for q in range(Q)], axis=1
    ).astype(jnp.bfloat16)


def score_kernel(
    plan, dest_ref, onehot_ref, other_ref, p_ref, _, o_ref, q_ref, plan_s, best, sem, q_sem
):
    half = NQ // 2
    q_copy = pltpu.make_async_copy(other_ref, q_ref.at[pl.ds(half, half)], q_sem)
    q_copy.start()
    copy = pltpu.make_async_copy(plan, plan_s, sem)
    copy.start()
    dest = dest_ref[...]
    c_iota = iota((GROUP, 128), 0)
    best[...] = jnp.zeros((GMAX, GROUP * T), jnp.float32)
    copy.wait()
    q_copy.wait()

    token = iota((PT, GROUP * T), 0)

    def step(it, carry):
        rows = []
        for u in range(UNROLL):
            g = it * UNROLL + u
            b = plan_s[GROUP, g]
            rows_q = jnp.concatenate([q_ref[plan_s[c, g]] for c in range(GROUP)], axis=0)
            similar = dot(p_ref[b], rows_q, ((1,), (1,)))
            similar = jnp.where(token < plan_s[GROUP + 2, b], similar, -jnp.inf)
            rows.append(jnp.max(similar, axis=0, keepdims=True))
        best[pl.ds(pl.multiple_of(it * UNROLL, UNROLL), UNROLL), :] = jnp.concatenate(rows, axis=0)
        return carry

    lax.fori_loop(0, (plan_s[GROUP + 1, 0] + (UNROLL - 1)) // UNROLL, step, 0)

    w = (iota((GROUP, GROUP * T), 0) == (iota((GROUP, GROUP * T), 1) >> 5)).astype(jnp.float32)
    w = w.astype(jnp.bfloat16)
    means = sum(dot(w, part, ((1,), (1,))) for part in split3(best[...])) * (1.0 / T)
    picked = dot(jnp.concatenate(split3(means), axis=0), onehot_ref[...], ((1,), (0,)))
    picked = picked[0:GROUP] + picked[GROUP : 2 * GROUP] + picked[2 * GROUP : 3 * GROUP]
    out = []
    for q in range(Q):
        here = (dest[q : q + 1, :] & 7) == c_iota
        out.append(
            jnp.sum(jnp.where(here, picked[:, 128 * q : 128 * (q + 1)], 0.0), axis=0, keepdims=True)
        )
    out = jnp.concatenate(out, axis=0)
    o_ref[0:8, :] = out
    o_ref[8:16, :] = pltpu.roll(out, 64, 1)


def place_kernel(cand_ref, key_ref, x_ref, o_ref):
    cand = jnp.concatenate([cand_ref[...], jnp.zeros((CL, 128 - QL), jnp.int32)], axis=1)
    lane = iota((1, 128), 1)
    turned = [cand] + [pltpu.roll(cand, 32 * i, 1) for i in range(1, 4)]
    segs = []
    for t in range(4):
        seg = turned[0][4 * t : 4 * t + 1, :]
        for i in range(1, 4):
            seg = jnp.where(lane >> 5 == i, turned[i][4 * t + i : 4 * t + i + 1, :], seg)
        segs.append(seg)
    asked = jnp.concatenate(segs, axis=1)
    place = iota((1, QL * CL), 1)
    own_key = ((place & 31) << 10) + ((place >> 5) << 6) + (asked & 63)
    owner = (asked >> 6) ^ FIRST
    lane_z = iota((Z, 128), 1)
    x = jnp.where(lane_z < 2 * YQ, x_ref[...], 0.0)
    key = jnp.where(lane_z < YQ, key_ref[...], 0)
    key_high = pltpu.roll(key >> 8, 2 * YQ, 1).astype(jnp.float32)
    key_low = pltpu.roll(key & 255, 3 * YQ, 1).astype(jnp.float32)
    high, mid, low = split3(x)
    high = jnp.where(
        lane_z < 2 * YQ,
        high.astype(jnp.float32),
        jnp.where(lane_z < 3 * YQ, key_high, key_low),
    ).astype(jnp.bfloat16)
    tables = jnp.concatenate([high, mid, low], axis=1)
    on_z = ((owner >> 5) == iota((Z, QL * CL), 0)).astype(jnp.float32).astype(jnp.bfloat16)
    found = dot(tables, on_z, ((0,), (0,)))
    on_yq = (owner & 31) == iota((YQ, QL * CL), 0)

    def pick(rows):
        return jnp.sum(jnp.where(on_yq, rows, 0.0), axis=0, keepdims=True)

    score = found[0 : 2 * YQ] + found[128 : 128 + 2 * YQ] + found[256 : 256 + 2 * YQ]
    first = pick(found[2 * YQ : 3 * YQ] * 256.0 + found[3 * YQ : 4 * YQ])
    out = jnp.where(
        first.astype(jnp.int32) == own_key, pick(score[0:YQ]), pick(score[YQ : 2 * YQ])
    )
    row = iota((CL, 128), 0)
    res = jnp.zeros((CL, 128), jnp.float32)
    for i in range(4):
        for t in range(4):
            seg = jnp.broadcast_to(out[:, 128 * t : 128 * (t + 1)], (CL, 128))
            seg = pltpu.roll(seg, 128 - 32 * i, 1) if i else seg
            res = jnp.where(row == 4 * t + i, seg, res)
    o_ref[...] = res[:, :QL]


VMEM = pl.BlockSpec(memory_space=pltpu.VMEM)


def small_call(kernel, out_shape, *args, hint=None):
    return pl.pallas_call(
        kernel,
        cost_estimate=hint,
        out_shape=out_shape,
        in_specs=[VMEM] * len(args),
        out_specs=jax.tree.map(lambda _: VMEM, out_shape),
    )(*[pltpu.with_memory_space_constraint(a, pltpu.VMEM) for a in args])


def shards(queries, passages, lengths, candidates):
    same = [queries] + [
        lax.ppermute(queries, "query", [(k, (k + 2 * d) % Q) for k in range(Q)])
        for d in range(1, Q // 2)
    ]
    cand = candidates.T
    table, keys = small_call(
        request_kernel,
        (pltpu.VMEM((YQ, 128), jnp.int32), pltpu.VMEM((Z, 128), jnp.int32)),
        cand,
    )
    got = exchange(table, YQ_GROUPS)
    hint = pl.CostEstimate(flops=10**11, transcendentals=0, bytes_accessed=2**20)
    got = small_call(by_z_kernel, pltpu.VMEM((Z, 128), jnp.int32), got, hint=hint)
    codes = exchange(got, Z_GROUPS)
    blocks = pl.pallas_call(
        fetch_kernel,
        out_shape=pltpu.VMEM(passages.shape, passages.dtype),
        in_specs=[VMEM, pl.BlockSpec(memory_space=pltpu.HBM)],
        out_specs=VMEM,
        scratch_shapes=[pltpu.SemaphoreType.DMA],
    )(
        pltpu.with_memory_space_constraint(got, pltpu.VMEM),
        pltpu.with_memory_space_constraint(passages, pltpu.HBM),
    )
    _, *same = lax.optimization_barrier((got, *same))
    same = jnp.concatenate(same, axis=0)
    other = lax.ppermute(same, "query", [(k, k ^ 1) for k in range(Q)])
    at = pltpu.with_memory_space_constraint
    hbm = pl.BlockSpec(memory_space=pltpu.HBM)
    every = pltpu.VMEM((NQ, T, D), queries.dtype)
    plan, dest, onehot, gathered = pl.pallas_call(
        sort_kernel,
        out_shape=(
            pltpu.VMEM((2 * GROUP, 256), jnp.int32),
            pltpu.VMEM((Q, 128), jnp.int32),
            pltpu.VMEM((GMAX, Q * 128), jnp.bfloat16),
            every,
        ),
        in_specs=[VMEM, VMEM, hbm],
        out_specs=(VMEM,) * 4,
        scratch_shapes=[pltpu.VMEM((1, BLK), jnp.int32)] + [pltpu.SemaphoreType.DMA] * 2,
        cost_estimate=pl.CostEstimate(flops=10**11, transcendentals=0, bytes_accessed=2**22),
        compiler_params=pltpu.CompilerParams(vmem_limit_bytes=32 << 20),
    )(
        at(codes, pltpu.VMEM),
        at(same, pltpu.VMEM),
        at(lengths.reshape(1, BLK), pltpu.HBM),
    )
    scores, _ = pl.pallas_call(
        score_kernel,
        out_shape=(pltpu.VMEM((Z, 128), jnp.float32), every),
        in_specs=[VMEM] * 6,
        out_specs=(VMEM, VMEM),
        input_output_aliases={5: 1},
        scratch_shapes=[
            pltpu.SMEM((2 * GROUP, 256), jnp.int32),
            pltpu.VMEM((GMAX, GROUP * T), jnp.float32),
            pltpu.SemaphoreType.DMA,
            pltpu.SemaphoreType.DMA,
        ],
        compiler_params=pltpu.CompilerParams(vmem_limit_bytes=32 << 20),
    )(
        *[at(x, pltpu.VMEM) for x in (plan, dest, onehot, other, blocks, gathered)],
    )
    back = small_call(by_plane_kernel, pltpu.VMEM((YQ, 128), jnp.float32), scores)
    back = exchange(back, YQ_GROUPS)
    back = small_call(by_z_kernel, pltpu.VMEM((Z, 128), jnp.float32), back)
    back = exchange(back, Z_GROUPS)
    out = small_call(
        place_kernel, jax.ShapeDtypeStruct((CL, QL), jnp.float32), cand, keys, back
    )
    return out.T


def solution(mesh):
    in_specs = (
        P("query", None, None),
        P(("index", "query"), None, None),
        P(("index", "query")),
        P("query", "index"),
    )
    return jax.shard_map(
        shards, mesh=mesh, in_specs=in_specs, out_specs=P("query", "index"), check_vma=False
    )
```

```python
import jax
import jax.numpy as jnp
from jax import lax
from jax.experimental import pallas as pl
from jax.experimental.pallas import tpu as pltpu
from jax.sharding import PartitionSpec as P

Z, Y, Q = 16, 4, 8
YQ = Y * Q
OWNERS = Z * YQ
BLK = 64
QL, CL = 32, 16
NQ = Q * QL
T, D, PT = 32, 128, 128
GROUP = 8
GMAX = 192
UNROLL = 32
BIG = 1 << 30

FIRST_Z, FIRST_YQ = Z // 2, (Y // 2) * Q + Q // 2 + 1
FIRST = FIRST_Z * YQ + FIRST_YQ
Z_GROUPS = [[r + YQ * (z ^ FIRST_Z) for z in range(Z)] for r in range(YQ)]
YQ_GROUPS = [[YQ * z + (r ^ FIRST_YQ) for r in range(YQ)] for z in range(Z)]


def iota(shape, axis):
    return lax.broadcasted_iota(jnp.int32, shape, axis)


def exchange(x, groups):
    return lax.all_to_all(
        x, ("index", "query"), split_axis=0, concat_axis=0, tiled=True,
        axis_index_groups=groups,
    )


def spread(rows, row, lane):
    out = jnp.zeros((Z, 128), jnp.int32)
    for k, slot in enumerate(rows):
        for j in range(4):
            shift = (32 * k - 32 * j) % 128
            for t in range(4):
                seg = jnp.broadcast_to(slot[:, 128 * t : 128 * (t + 1)], (Z, 128))
                seg = pltpu.roll(seg, shift, 1) if shift else seg
                out = jnp.where((row == 4 * t + j) & (lane >> 5 == k), seg, out)
    return out


def by_plane(x):
    xt = jnp.transpose(jnp.concatenate([x, jnp.zeros((112, 128), x.dtype)], axis=0))
    lane = iota((YQ, 128), 1)
    return jnp.where(lane < Z, xt[:YQ], pltpu.roll(xt[YQ : 2 * YQ], Z, 1))


def by_z(x):
    xt = jnp.transpose(jnp.concatenate([x, jnp.zeros((96, 128), x.dtype)], axis=0))
    lane = iota((Z, 128), 1)
    return jnp.where(lane < YQ, xt[:Z], pltpu.roll(xt[Z : 2 * Z], YQ, 1))


def by_plane_kernel(x_ref, o_ref):
    o_ref[...] = by_plane(x_ref[...])


def by_z_kernel(x_ref, o_ref):
    o_ref[...] = by_z(x_ref[...])


def request_kernel(cand_ref, code_ref, key_ref):
    cand = cand_ref[...]
    lane_owner = iota((CL, OWNERS), 1)
    sub = iota((CL, 1), 0)
    low = jnp.full((CL, OWNERS), BIG, jnp.int32)
    high = jnp.full((CL, OWNERS), -1, jnp.int32)
    for q in range(QL):
        col = cand[:, q : q + 1]
        key = (q << 10) + (sub << 6) + (col & 63)
        match = ((col >> 6) ^ FIRST) == lane_owner
        low = jnp.minimum(low, jnp.where(match, key, BIG))
        high = jnp.maximum(high, jnp.where(match, key, -1))
    last = jnp.max(high, axis=0, keepdims=True)
    first = jnp.where(last >= 0, jnp.min(low, axis=0, keepdims=True), -1)
    last = jnp.where(last != first, last, -1)
    row = iota((Z, 128), 0)
    lane = iota((Z, 128), 1)
    key = spread((first, last), row, lane)
    key_ref[...] = key
    code = jnp.where((key >= 0) & (lane < 2 * YQ), ((key >> 10) << 6) + (key & 63), -1)
    code_ref[...] = by_plane(code)


def split3(x):
    hi = x.astype(jnp.bfloat16)
    rest = x - hi.astype(jnp.float32)
    mid = rest.astype(jnp.bfloat16)
    low = (rest - mid.astype(jnp.float32)).astype(jnp.bfloat16)
    return hi, mid, low


def dot(a, b, dims):
    return lax.dot_general(a, b, (dims, ((), ())), preferred_element_type=jnp.float32)


def pass_kernel(x_ref, o_ref):
    o_ref[...] = x_ref[...]


def score_kernel(
    len_hbm, code_ref, same_ref, other_ref, p_hbm, o_ref,
    len_ref, q_ref, p_ref, plan, plan_s, onehot, best, sem, len_sem, same_sem, other_sem, p_sem,
):
    len_copy = pltpu.make_async_copy(len_hbm, len_ref, len_sem)
    len_copy.start()
    p_copy = pltpu.make_async_copy(p_hbm, p_ref, p_sem)
    p_copy.start()
    half = NQ // 2
    same_copy = pltpu.make_async_copy(same_ref, q_ref.at[pl.ds(0, half)], same_sem)
    same_copy.start()
    other_copy = pltpu.make_async_copy(other_ref, q_ref.at[pl.ds(half, half)], other_sem)
    other_copy.start()
    lane8 = iota((Q, 128), 1)
    code = jnp.where(lane8 < 64, code_ref[0:8, :], pltpu.roll(code_ref[8:16, :], 64, 1))
    valid = code >= 0
    block = jnp.where(valid, code & 63, BLK)
    me = lax.axis_index("query")
    source = (lane8 ^ FIRST_YQ) & (Q - 1)
    piece = (((source ^ me) & 1) << 2) + (((me >> 1) - (source >> 1)) & 3)
    query = jnp.where(valid, (code >> 6) + QL * piece, 0)

    b_iota = iota((BLK, 128), 0)
    hits = [block[q : q + 1, :] == b_iota for q in range(Q)]
    hit = jnp.concatenate([h.astype(jnp.float32) for h in hits], axis=0).astype(jnp.bfloat16)
    r_i, c_i = iota((128, 128), 0), iota((128, 128), 1)
    earlier = jnp.concatenate(
        [(r_i < c_i).astype(jnp.float32), jnp.ones((128, 128), jnp.float32)], axis=1
    ).astype(jnp.bfloat16)
    sums = dot(hit, earlier, ((1,), (0,)))
    base = jnp.zeros((BLK, 128), jnp.float32)
    bases = []
    for q in range(Q):
        bases.append(base + sums[BLK * q : BLK * (q + 1), :128])
        base = base + sums[BLK * q : BLK * (q + 1), 128:]
    groups = ((base.astype(jnp.int32) + (GROUP - 1)) >> 3).astype(jnp.float32)
    l_i, m_i = iota((BLK, BLK), 0), iota((BLK, BLK), 1)
    before = dot(
        (m_i < l_i).astype(jnp.float32).astype(jnp.bfloat16),
        groups.astype(jnp.bfloat16),
        ((1,), (0,)),
    )
    ends = (before + groups).astype(jnp.int32)
    dest = jnp.concatenate(
        [
            jnp.sum(jnp.where(hits[q], GROUP * before + bases[q], 0.0), axis=0, keepdims=True)
            for q in range(Q)
        ],
        axis=0,
    ).astype(jnp.int32)

    g_iota = iota((GMAX, 128), 0)
    c_iota = iota((GROUP, 128), 0)
    named = []
    for q in range(Q):
        d = dest[q : q + 1, :]
        onehot[:, 128 * q : 128 * (q + 1)] = (
            ((d >> 3) == g_iota).astype(jnp.float32).astype(jnp.bfloat16)
        )
        here = ((d & 7) == c_iota) & valid[q : q + 1, :]
        named.append(jnp.where(here, query[q : q + 1, :], 0).astype(jnp.float32))
    lists = dot(
        jnp.concatenate(named, axis=1).astype(jnp.bfloat16), onehot[...], ((1,), (1,))
    )
    plan[0:GROUP, 0:GMAX] = lists.astype(jnp.int32)
    g_lane = iota((BLK, 256), 1)
    ends2 = jnp.concatenate([ends, ends], axis=1)
    owner_block = jnp.minimum(
        jnp.sum((ends2 <= g_lane).astype(jnp.int32), axis=0, keepdims=True), BLK - 1
    )
    total = jnp.broadcast_to(ends2[BLK - 1 : BLK, :], (1, 256))
    plan[GROUP : 2 * GROUP, :] = jnp.where(
        iota((GROUP, 256), 0) == 0,
        jnp.broadcast_to(owner_block, (GROUP, 256)),
        jnp.broadcast_to(total, (GROUP, 256)),
    )
    copy = pltpu.make_async_copy(plan, plan_s, sem)
    copy.start()
    best[...] = jnp.zeros((GMAX, GROUP * T), jnp.float32)
    copy.wait()
    len_copy.wait()
    p_copy.wait()
    same_copy.wait()
    other_copy.wait()

    token = iota((PT, GROUP * T), 0)

    def step(it, carry):
        rows = []
        for u in range(UNROLL):
            g = it * UNROLL + u
            b = plan_s[GROUP, g]
            rows_q = jnp.concatenate([q_ref[plan_s[c, g]] for c in range(GROUP)], axis=0)
            similar = dot(p_ref[b], rows_q, ((1,), (1,)))
            similar = jnp.where(token < len_ref[b], similar, -jnp.inf)
            rows.append(jnp.max(similar, axis=0, keepdims=True))
        best[pl.ds(pl.multiple_of(it * UNROLL, UNROLL), UNROLL), :] = jnp.concatenate(rows, axis=0)
        return carry

    lax.fori_loop(0, (plan_s[GROUP + 1, 0] + (UNROLL - 1)) // UNROLL, step, 0)

    w = (iota((GROUP, GROUP * T), 0) == (iota((GROUP, GROUP * T), 1) >> 5)).astype(jnp.float32)
    w = w.astype(jnp.bfloat16)
    means = sum(dot(w, part, ((1,), (1,))) for part in split3(best[...])) * (1.0 / T)
    picked = dot(jnp.concatenate(split3(means), axis=0), onehot[...], ((1,), (0,)))
    picked = picked[0:GROUP] + picked[GROUP : 2 * GROUP] + picked[2 * GROUP : 3 * GROUP]
    out = []
    for q in range(Q):
        here = (dest[q : q + 1, :] & 7) == c_iota
        out.append(
            jnp.sum(jnp.where(here, picked[:, 128 * q : 128 * (q + 1)], 0.0), axis=0, keepdims=True)
        )
    out = jnp.concatenate(out, axis=0)
    o_ref[0:8, :] = out
    o_ref[8:16, :] = pltpu.roll(out, 64, 1)


def place_kernel(cand_ref, key_ref, x_ref, o_ref):
    cand = jnp.concatenate([cand_ref[...], jnp.zeros((CL, 128 - QL), jnp.int32)], axis=1)
    lane = iota((1, 128), 1)
    turned = [cand] + [pltpu.roll(cand, 32 * i, 1) for i in range(1, 4)]
    segs = []
    for t in range(4):
        seg = turned[0][4 * t : 4 * t + 1, :]
        for i in range(1, 4):
            seg = jnp.where(lane >> 5 == i, turned[i][4 * t + i : 4 * t + i + 1, :], seg)
        segs.append(seg)
    asked = jnp.concatenate(segs, axis=1)
    place = iota((1, QL * CL), 1)
    own_key = ((place & 31) << 10) + ((place >> 5) << 6) + (asked & 63)
    owner = (asked >> 6) ^ FIRST
    lane_z = iota((Z, 128), 1)
    x = jnp.where(lane_z < 2 * YQ, x_ref[...], 0.0)
    key = jnp.where(lane_z < YQ, key_ref[...], 0)
    key_high = pltpu.roll(key >> 8, 2 * YQ, 1).astype(jnp.float32)
    key_low = pltpu.roll(key & 255, 3 * YQ, 1).astype(jnp.float32)
    high, mid, low = split3(x)
    high = jnp.where(
        lane_z < 2 * YQ,
        high.astype(jnp.float32),
        jnp.where(lane_z < 3 * YQ, key_high, key_low),
    ).astype(jnp.bfloat16)
    tables = jnp.concatenate([high, mid, low], axis=1)
    on_z = ((owner >> 5) == iota((Z, QL * CL), 0)).astype(jnp.float32).astype(jnp.bfloat16)
    found = dot(tables, on_z, ((0,), (0,)))
    on_yq = (owner & 31) == iota((YQ, QL * CL), 0)

    def pick(rows):
        return jnp.sum(jnp.where(on_yq, rows, 0.0), axis=0, keepdims=True)

    score = found[0 : 2 * YQ] + found[128 : 128 + 2 * YQ] + found[256 : 256 + 2 * YQ]
    first = pick(found[2 * YQ : 3 * YQ] * 256.0 + found[3 * YQ : 4 * YQ])
    out = jnp.where(
        first.astype(jnp.int32) == own_key, pick(score[0:YQ]), pick(score[YQ : 2 * YQ])
    )
    row = iota((CL, 128), 0)
    res = jnp.zeros((CL, 128), jnp.float32)
    for i in range(4):
        for t in range(4):
            seg = jnp.broadcast_to(out[:, 128 * t : 128 * (t + 1)], (CL, 128))
            seg = pltpu.roll(seg, 128 - 32 * i, 1) if i else seg
            res = jnp.where(row == 4 * t + i, seg, res)
    o_ref[...] = res[:, :QL]


VMEM = pl.BlockSpec(memory_space=pltpu.VMEM)


def small_call(kernel, out_shape, *args, hint=None):
    return pl.pallas_call(
        kernel,
        cost_estimate=hint,
        out_shape=out_shape,
        in_specs=[VMEM] * len(args),
        out_specs=jax.tree.map(lambda _: VMEM, out_shape),
    )(*[pltpu.with_memory_space_constraint(a, pltpu.VMEM) for a in args])


def shards(queries, passages, lengths, candidates):
    same = [queries] + [
        lax.ppermute(queries, "query", [(k, (k + 2 * d) % Q) for k in range(Q)])
        for d in range(1, Q // 2)
    ]
    cand = candidates.T
    table, keys = small_call(
        request_kernel,
        (pltpu.VMEM((YQ, 128), jnp.int32), pltpu.VMEM((Z, 128), jnp.int32)),
        cand,
    )
    got = exchange(table, YQ_GROUPS)
    hint = pl.CostEstimate(flops=10**11, transcendentals=0, bytes_accessed=2**20)
    got = small_call(by_z_kernel, pltpu.VMEM((Z, 128), jnp.int32), got, hint=hint)
    codes = exchange(got, Z_GROUPS)
    _, *same = lax.optimization_barrier((got, *same))
    same = jnp.concatenate(same, axis=0)
    other = lax.ppermute(same, "query", [(k, k ^ 1) for k in range(Q)])
    at = pltpu.with_memory_space_constraint
    hbm = pl.BlockSpec(memory_space=pltpu.HBM)
    codes = small_call(pass_kernel, pltpu.VMEM((Z, 128), jnp.int32), codes, hint=hint)
    scores = pl.pallas_call(
        score_kernel,
        out_shape=pltpu.VMEM((Z, 128), jnp.float32),
        in_specs=[hbm, VMEM, VMEM, VMEM, hbm],
        out_specs=VMEM,
        scratch_shapes=[
            pltpu.SMEM((BLK,), jnp.int32),
            pltpu.VMEM((NQ, T, D), jnp.bfloat16),
            pltpu.VMEM((BLK, PT, D), jnp.bfloat16),
            pltpu.VMEM((2 * GROUP, 256), jnp.int32),
            pltpu.SMEM((2 * GROUP, 256), jnp.int32),
            pltpu.VMEM((GMAX, Q * 128), jnp.bfloat16),
            pltpu.VMEM((GMAX, GROUP * T), jnp.float32),
            pltpu.SemaphoreType.DMA,
            pltpu.SemaphoreType.DMA,
            pltpu.SemaphoreType.DMA,
            pltpu.SemaphoreType.DMA,
            pltpu.SemaphoreType.DMA,
        ],
        compiler_params=pltpu.CompilerParams(vmem_limit_bytes=32 << 20),
    )(
        pltpu.with_memory_space_constraint(lengths, pltpu.HBM),
        pltpu.with_memory_space_constraint(codes, pltpu.VMEM),
        pltpu.with_memory_space_constraint(same, pltpu.VMEM),
        pltpu.with_memory_space_constraint(other, pltpu.VMEM),
        pltpu.with_memory_space_constraint(passages, pltpu.HBM),
    )
    back = small_call(by_plane_kernel, pltpu.VMEM((YQ, 128), jnp.float32), scores)
    back = exchange(back, YQ_GROUPS)
    back = small_call(by_z_kernel, pltpu.VMEM((Z, 128), jnp.float32), back)
    back = exchange(back, Z_GROUPS)
    out = small_call(
        place_kernel, jax.ShapeDtypeStruct((CL, QL), jnp.float32), cand, keys, back
    )
    return out.T


def solution(mesh):
    in_specs = (
        P("query", None, None),
        P(("index", "query"), None, None),
        P(("index", "query")),
        P("query", "index"),
    )
    return jax.shard_map(
        shards, mesh=mesh, in_specs=in_specs, out_specs=P("query", "index"), check_vma=False
    )
```

```python
import jax
import jax.numpy as jnp
from jax import lax
from jax.experimental import pallas as pl
from jax.experimental.pallas import tpu as pltpu
from jax.sharding import PartitionSpec as P

Z, Y, Q = 16, 4, 8
YQ = Y * Q
OWNERS = Z * YQ
BLK = 64
QL, CL = 32, 16
NQ = Q * QL
T, D, PT = 32, 128, 128
GROUP = 8
GMAX = 192
UNROLL = 32
BIG = 1 << 30

FIRST_Z, FIRST_YQ = Z // 2, (Y // 2) * Q + Q // 2
FIRST = FIRST_Z * YQ + FIRST_YQ
Z_GROUPS = [[r + YQ * (z ^ FIRST_Z) for z in range(Z)] for r in range(YQ)]
YQ_GROUPS = [[YQ * z + (r ^ FIRST_YQ) for r in range(YQ)] for z in range(Z)]


def iota(shape, axis):
    return lax.broadcasted_iota(jnp.int32, shape, axis)


def exchange(x, groups):
    return lax.all_to_all(
        x, ("index", "query"), split_axis=0, concat_axis=0, tiled=True,
        axis_index_groups=groups,
    )


def spread(rows, row, lane):
    out = jnp.zeros((Z, 128), jnp.int32)
    for k, slot in enumerate(rows):
        for j in range(4):
            shift = (32 * k - 32 * j) % 128
            for t in range(4):
                seg = jnp.broadcast_to(slot[:, 128 * t : 128 * (t + 1)], (Z, 128))
                seg = pltpu.roll(seg, shift, 1) if shift else seg
                out = jnp.where((row == 4 * t + j) & (lane >> 5 == k), seg, out)
    return out


def by_plane(x):
    xt = jnp.transpose(jnp.concatenate([x, jnp.zeros((112, 128), x.dtype)], axis=0))
    lane = iota((YQ, 128), 1)
    return jnp.where(lane < Z, xt[:YQ], pltpu.roll(xt[YQ : 2 * YQ], Z, 1))


def by_z(x):
    xt = jnp.transpose(jnp.concatenate([x, jnp.zeros((96, 128), x.dtype)], axis=0))
    lane = iota((Z, 128), 1)
    return jnp.where(lane < YQ, xt[:Z], pltpu.roll(xt[Z : 2 * Z], YQ, 1))


def by_plane_kernel(x_ref, o_ref):
    o_ref[...] = by_plane(x_ref[...])


def by_z_kernel(x_ref, o_ref):
    o_ref[...] = by_z(x_ref[...])


def request_kernel(cand_ref, code_ref, key_ref):
    cand = cand_ref[...]
    lane_owner = iota((CL, OWNERS), 1)
    sub = iota((CL, 1), 0)
    low = jnp.full((CL, OWNERS), BIG, jnp.int32)
    high = jnp.full((CL, OWNERS), -1, jnp.int32)
    for q in range(QL):
        col = cand[:, q : q + 1]
        key = (q << 10) + (sub << 6) + (col & 63)
        match = ((col >> 6) ^ FIRST) == lane_owner
        low = jnp.minimum(low, jnp.where(match, key, BIG))
        high = jnp.maximum(high, jnp.where(match, key, -1))
    last = jnp.max(high, axis=0, keepdims=True)
    first = jnp.where(last >= 0, jnp.min(low, axis=0, keepdims=True), -1)
    last = jnp.where(last != first, last, -1)
    row = iota((Z, 128), 0)
    lane = iota((Z, 128), 1)
    key = spread((first, last), row, lane)
    key_ref[...] = key
    code = jnp.where((key >= 0) & (lane < 2 * YQ), ((key >> 10) << 6) + (key & 63), -1)
    code_ref[...] = by_plane(code)


def split3(x):
    hi = x.astype(jnp.bfloat16)
    rest = x - hi.astype(jnp.float32)
    mid = rest.astype(jnp.bfloat16)
    low = (rest - mid.astype(jnp.float32)).astype(jnp.bfloat16)
    return hi, mid, low


def dot(a, b, dims):
    return lax.dot_general(a, b, (dims, ((), ())), preferred_element_type=jnp.float32)


def sort_kernel(
    code_ref, p_hbm, same_ref, len_hbm, plan_ref, dest_ref, onehot_ref, p_ref, q_ref,
    len_ref, p_sem, q_sem, len_sem,
):
    len_copy = pltpu.make_async_copy(len_hbm, len_ref, len_sem)
    len_copy.start()
    q_copy = pltpu.make_async_copy(same_ref, q_ref.at[pl.ds(0, NQ // 2)], q_sem)
    q_copy.start()
    p_copy = pltpu.make_async_copy(p_hbm, p_ref, p_sem)
    p_copy.start()
    lane8 = iota((Q, 128), 1)
    code = jnp.where(lane8 < 64, code_ref[0:8, :], pltpu.roll(code_ref[8:16, :], 64, 1))
    valid = code >= 0
    block = jnp.where(valid, code & 63, BLK)
    me = lax.axis_index("query")
    source = (lane8 ^ FIRST_YQ) & (Q - 1)
    piece = (((source ^ me) & 1) << 2) + (((me >> 1) - (source >> 1)) & 3)
    query = jnp.where(valid, (code >> 6) + QL * piece, 0)

    b_iota = iota((BLK, 128), 0)
    hits = [block[q : q + 1, :] == b_iota for q in range(Q)]
    hit = jnp.concatenate([h.astype(jnp.float32) for h in hits], axis=0).astype(jnp.bfloat16)
    r_i, c_i = iota((128, 128), 0), iota((128, 128), 1)
    earlier = jnp.concatenate(
        [(r_i < c_i).astype(jnp.float32), jnp.ones((128, 128), jnp.float32)], axis=1
    ).astype(jnp.bfloat16)
    sums = dot(hit, earlier, ((1,), (0,)))
    base = jnp.zeros((BLK, 128), jnp.float32)
    bases = []
    for q in range(Q):
        bases.append(base + sums[BLK * q : BLK * (q + 1), :128])
        base = base + sums[BLK * q : BLK * (q + 1), 128:]
    groups = ((base.astype(jnp.int32) + (GROUP - 1)) >> 3).astype(jnp.float32)
    l_i, m_i = iota((BLK, BLK), 0), iota((BLK, BLK), 1)
    before = dot(
        (m_i < l_i).astype(jnp.float32).astype(jnp.bfloat16),
        groups.astype(jnp.bfloat16),
        ((1,), (0,)),
    )
    ends = (before + groups).astype(jnp.int32)
    dest = jnp.concatenate(
        [
            jnp.sum(jnp.where(hits[q], GROUP * before + bases[q], 0.0), axis=0, keepdims=True)
            for q in range(Q)
        ],
        axis=0,
    ).astype(jnp.int32)

    dest_ref[...] = dest
    c_iota = iota((GROUP, 128), 0)
    named = []
    for q in range(Q):
        here = ((dest[q : q + 1, :] & 7) == c_iota) & valid[q : q + 1, :]
        named.append(jnp.where(here, query[q : q + 1, :], 0).astype(jnp.float32))
    onehot = in_group(dest)
    onehot_ref[...] = onehot
    lists = dot(
        jnp.concatenate(named, axis=1).astype(jnp.bfloat16), onehot, ((1,), (1,))
    )
    plan_ref[0:GROUP, 0:GMAX] = lists.astype(jnp.int32)
    plan_ref[0:GROUP, GMAX:256] = jnp.zeros((GROUP, 256 - GMAX), jnp.int32)
    g_lane = iota((BLK, 256), 1)
    ends2 = jnp.concatenate([ends, ends], axis=1)
    owner_block = jnp.minimum(
        jnp.sum((ends2 <= g_lane).astype(jnp.int32), axis=0, keepdims=True), BLK - 1
    )
    total = jnp.broadcast_to(ends2[BLK - 1 : BLK, :], (1, 256))
    len_copy.wait()
    live = jnp.concatenate([len_ref[...], jnp.zeros((1, 256 - BLK), jnp.int32)], axis=1)
    row = iota((GROUP, 256), 0)
    plan_ref[GROUP : 2 * GROUP, :] = jnp.where(
        row == 0,
        jnp.broadcast_to(owner_block, (GROUP, 256)),
        jnp.where(
            row == 1,
            jnp.broadcast_to(total, (GROUP, 256)),
            jnp.broadcast_to(live, (GROUP, 256)),
        ),
    )
    p_copy.wait()
    q_copy.wait()


def in_group(dest):
    g_iota = iota((GMAX, 128), 0)
    return jnp.concatenate(
        [((dest[q : q + 1, :] >> 3) == g_iota).astype(jnp.float32) for q in range(Q)], axis=1
    ).astype(jnp.bfloat16)


def score_kernel(
    plan, dest_ref, onehot_ref, other_ref, p_ref, _, o_ref, q_ref, plan_s, best, sem, q_sem
):
    half = NQ // 2
    q_copy = pltpu.make_async_copy(other_ref, q_ref.at[pl.ds(half, half)], q_sem)
    q_copy.start()
    copy = pltpu.make_async_copy(plan, plan_s, sem)
    copy.start()
    dest = dest_ref[...]
    c_iota = iota((GROUP, 128), 0)
    best[...] = jnp.zeros((GMAX, GROUP * T), jnp.float32)
    copy.wait()
    q_copy.wait()

    token = iota((PT, GROUP * T), 0)

    def step(it, carry):
        rows = []
        for u in range(UNROLL):
            g = it * UNROLL + u
            b = plan_s[GROUP, g]
            rows_q = jnp.concatenate([q_ref[plan_s[c, g]] for c in range(GROUP)], axis=0)
            similar = dot(p_ref[b], rows_q, ((1,), (1,)))
            similar = jnp.where(token < plan_s[GROUP + 2, b], similar, -jnp.inf)
            rows.append(jnp.max(similar, axis=0, keepdims=True))
        best[pl.ds(pl.multiple_of(it * UNROLL, UNROLL), UNROLL), :] = jnp.concatenate(rows, axis=0)
        return carry

    lax.fori_loop(0, (plan_s[GROUP + 1, 0] + (UNROLL - 1)) // UNROLL, step, 0)

    w = (iota((GROUP, GROUP * T), 0) == (iota((GROUP, GROUP * T), 1) >> 5)).astype(jnp.float32)
    w = w.astype(jnp.bfloat16)
    means = sum(dot(w, part, ((1,), (1,))) for part in split3(best[...])) * (1.0 / T)
    picked = dot(jnp.concatenate(split3(means), axis=0), onehot_ref[...], ((1,), (0,)))
    picked = picked[0:GROUP] + picked[GROUP : 2 * GROUP] + picked[2 * GROUP : 3 * GROUP]
    out = []
    for q in range(Q):
        here = (dest[q : q + 1, :] & 7) == c_iota
        out.append(
            jnp.sum(jnp.where(here, picked[:, 128 * q : 128 * (q + 1)], 0.0), axis=0, keepdims=True)
        )
    out = jnp.concatenate(out, axis=0)
    o_ref[0:8, :] = out
    o_ref[8:16, :] = pltpu.roll(out, 64, 1)


def place_kernel(cand_ref, key_ref, x_ref, o_ref):
    cand = jnp.concatenate([cand_ref[...], jnp.zeros((CL, 128 - QL), jnp.int32)], axis=1)
    lane = iota((1, 128), 1)
    turned = [cand] + [pltpu.roll(cand, 32 * i, 1) for i in range(1, 4)]
    segs = []
    for t in range(4):
        seg = turned[0][4 * t : 4 * t + 1, :]
        for i in range(1, 4):
            seg = jnp.where(lane >> 5 == i, turned[i][4 * t + i : 4 * t + i + 1, :], seg)
        segs.append(seg)
    asked = jnp.concatenate(segs, axis=1)
    place = iota((1, QL * CL), 1)
    own_key = ((place & 31) << 10) + ((place >> 5) << 6) + (asked & 63)
    owner = (asked >> 6) ^ FIRST
    lane_z = iota((Z, 128), 1)
    x = jnp.where(lane_z < 2 * YQ, x_ref[...], 0.0)
    key = jnp.where(lane_z < YQ, key_ref[...], 0)
    key_high = pltpu.roll(key >> 8, 2 * YQ, 1).astype(jnp.float32)
    key_low = pltpu.roll(key & 255, 3 * YQ, 1).astype(jnp.float32)
    high, mid, low = split3(x)
    high = jnp.where(
        lane_z < 2 * YQ,
        high.astype(jnp.float32),
        jnp.where(lane_z < 3 * YQ, key_high, key_low),
    ).astype(jnp.bfloat16)
    tables = jnp.concatenate([high, mid, low], axis=1)
    on_z = ((owner >> 5) == iota((Z, QL * CL), 0)).astype(jnp.float32).astype(jnp.bfloat16)
    found = dot(tables, on_z, ((0,), (0,)))
    on_yq = (owner & 31) == iota((YQ, QL * CL), 0)

    def pick(rows):
        return jnp.sum(jnp.where(on_yq, rows, 0.0), axis=0, keepdims=True)

    score = found[0 : 2 * YQ] + found[128 : 128 + 2 * YQ] + found[256 : 256 + 2 * YQ]
    first = pick(found[2 * YQ : 3 * YQ] * 256.0 + found[3 * YQ : 4 * YQ])
    out = jnp.where(
        first.astype(jnp.int32) == own_key, pick(score[0:YQ]), pick(score[YQ : 2 * YQ])
    )
    row = iota((CL, 128), 0)
    res = jnp.zeros((CL, 128), jnp.float32)
    for i in range(4):
        for t in range(4):
            seg = jnp.broadcast_to(out[:, 128 * t : 128 * (t + 1)], (CL, 128))
            seg = pltpu.roll(seg, 128 - 32 * i, 1) if i else seg
            res = jnp.where(row == 4 * t + i, seg, res)
    o_ref[...] = res[:, :QL]


VMEM = pl.BlockSpec(memory_space=pltpu.VMEM)


def small_call(kernel, out_shape, *args, hint=None):
    return pl.pallas_call(
        kernel,
        cost_estimate=hint,
        out_shape=out_shape,
        in_specs=[VMEM] * len(args),
        out_specs=jax.tree.map(lambda _: VMEM, out_shape),
    )(*[pltpu.with_memory_space_constraint(a, pltpu.VMEM) for a in args])


def shards(queries, passages, lengths, candidates):
    same = [queries] + [
        lax.ppermute(queries, "query", [(k, (k + 2 * d) % Q) for k in range(Q)])
        for d in range(1, Q // 2)
    ]
    cand = candidates.T
    table, keys = small_call(
        request_kernel,
        (pltpu.VMEM((YQ, 128), jnp.int32), pltpu.VMEM((Z, 128), jnp.int32)),
        cand,
    )
    got = exchange(table, YQ_GROUPS)
    hint = pl.CostEstimate(flops=10**11, transcendentals=0, bytes_accessed=2**20)
    got = small_call(by_z_kernel, pltpu.VMEM((Z, 128), jnp.int32), got, hint=hint)
    codes = exchange(got, Z_GROUPS)
    _, *same = lax.optimization_barrier((got, *same))
    same = jnp.concatenate(same, axis=0)
    other = lax.ppermute(same, "query", [(k, k ^ 1) for k in range(Q)])
    at = pltpu.with_memory_space_constraint
    hbm = pl.BlockSpec(memory_space=pltpu.HBM)
    every = pltpu.VMEM((NQ, T, D), queries.dtype)
    plan, dest, onehot, blocks, gathered = pl.pallas_call(
        sort_kernel,
        out_shape=(
            pltpu.VMEM((2 * GROUP, 256), jnp.int32),
            pltpu.VMEM((Q, 128), jnp.int32),
            pltpu.VMEM((GMAX, Q * 128), jnp.bfloat16),
            pltpu.VMEM(passages.shape, passages.dtype),
            every,
        ),
        in_specs=[VMEM, hbm, VMEM, hbm],
        out_specs=(VMEM,) * 5,
        scratch_shapes=[pltpu.VMEM((1, BLK), jnp.int32)] + [pltpu.SemaphoreType.DMA] * 3,
        cost_estimate=pl.CostEstimate(flops=10**11, transcendentals=0, bytes_accessed=2**22),
        compiler_params=pltpu.CompilerParams(vmem_limit_bytes=32 << 20),
    )(
        at(codes, pltpu.VMEM),
        at(passages, pltpu.HBM),
        at(same, pltpu.VMEM),
        at(lengths.reshape(1, BLK), pltpu.HBM),
    )
    scores, _ = pl.pallas_call(
        score_kernel,
        out_shape=(pltpu.VMEM((Z, 128), jnp.float32), every),
        in_specs=[VMEM] * 6,
        out_specs=(VMEM, VMEM),
        input_output_aliases={5: 1},
        scratch_shapes=[
            pltpu.SMEM((2 * GROUP, 256), jnp.int32),
            pltpu.VMEM((GMAX, GROUP * T), jnp.float32),
            pltpu.SemaphoreType.DMA,
            pltpu.SemaphoreType.DMA,
        ],
        compiler_params=pltpu.CompilerParams(vmem_limit_bytes=32 << 20),
    )(
        *[at(x, pltpu.VMEM) for x in (plan, dest, onehot, other, blocks, gathered)],
    )
    back = small_call(by_plane_kernel, pltpu.VMEM((YQ, 128), jnp.float32), scores)
    back = exchange(back, YQ_GROUPS)
    back = small_call(by_z_kernel, pltpu.VMEM((Z, 128), jnp.float32), back)
    back = exchange(back, Z_GROUPS)
    out = small_call(
        place_kernel, jax.ShapeDtypeStruct((CL, QL), jnp.float32), cand, keys, back
    )
    return out.T


def solution(mesh):
    in_specs = (
        P("query", None, None),
        P(("index", "query"), None, None),
        P(("index", "query")),
        P("query", "index"),
    )
    return jax.shard_map(
        shards, mesh=mesh, in_specs=in_specs, out_specs=P("query", "index"), check_vma=False
    )
```
